128 devices in a mesh: gx: 8 (over z, core), gy: 16 (over y, x).
Axes of the slice: x: 4, y: 4, z: 4, core: 2. Of those that a mesh axis runs over, the one named last changes fastest.
Arguments:
- populations: float32 [19, 512, 16, 16, 128], P(None, ('gx', 'gy')), may hold values from 0.01 to 0.1
- charge: float32 [512, 16, 16, 128], P(('gx', 'gy')), may hold values from -6 to 6
- fluid_mask: int32 [512, 18, 18, 128], P(('gx', 'gy')), may hold values from 0 to 1, as said below
- tile_ids: int32 [512], P(('gx', 'gy')), may hold values from 0 to 63, as said below
- phase_label: int32 [256, 512, 128], P('gx', 'gy'), may hold values from 0 to 3
- permittivity: float32 [4], replicated, may hold values from 0.5 to 5
Outputs:
- populations_next: float32 [19, 512, 16, 16, 128], P(None, ('gx', 'gy'))
- charge_next: float32 [512, 16, 16, 128], P(('gx', 'gy'))
- potential: float32 [256, 512, 128], P('gx', 'gy')
The draws below stay inside these ranges and needn't reach their ends.
Inputs may be any that keep to these rules, and one draw needn't show every extreme that they name: Within the slots of the devices of one gx index, tile_ids is a permutation of 0 to 63. Position p belongs to the regular block of gy index (p % 32) // 2; every device holds at most 1 positions of any one such block, and some device holds exactly 1. fluid_mask[s, i, j, z] is the fluid flag of grid cell (x0 + i - 1, y0 + j - 1, z), periodic, where (x0, y0) is the first cell of slot s's tile; the rim repeats flags of the neighbouring tiles.
All inputs are finite; a program needn't handle non-finite values.
Results may differ from the reference program's by a relative error of at most 0.0003.
Values sent between devices are 32-bit elements; how exact they have to be, the bound alone decides.
A program may use at most 192 MiB of HBM per device.

```python
import math
import jax
import jax.numpy as jnp

EDGE = 16
DEPTH = 128
TILE_ROWS = 2
TILE_COLS = 2
PHASES = 4
SWEEPS = 4
TILES_DEV = 4
CAPACITY = 1
BAND_COLS = 32
TILES = 512
GRID_X = 256
GRID_Y = 512
N_GX = 8
N_GY = 16


def band_layout(band_key):
    band_keys = jax.random.split(band_key, 6)
    favored = jax.random.randint(band_keys[0], (), 0, N_GY)
    others = (favored + 1 + jnp.arange(N_GY - 1, dtype=jnp.int32)) % N_GY
    others_pool = jax.random.permutation(band_keys[1], jnp.tile(others, CAPACITY))
    offsets = jnp.concatenate([jnp.full((CAPACITY,), favored, jnp.int32), others_pool[:TILES_DEV - CAPACITY].astype(jnp.int32)])
    offsets = jax.random.permutation(band_keys[2], offsets)
    relabel = jax.random.permutation(band_keys[3], N_GY)
    block_order = jax.vmap(lambda sub_key: jax.random.permutation(sub_key, TILES_DEV))(jax.random.split(band_keys[4], N_GY))
    owners = jnp.arange(N_GY, dtype=jnp.int32)[:, None]
    holder = relabel[(owners + offsets[None, :]) % N_GY]
    position = block_order // TILE_COLS * BAND_COLS + owners * TILE_COLS + block_order % TILE_COLS
    shuffle = jax.random.permutation(band_keys[5], N_GY * TILES_DEV)
    slot_order = jnp.argsort(holder.reshape(-1) * (N_GY * TILES_DEV) + shuffle)
    return position.reshape(-1)[slot_order].astype(jnp.int32)


def layout_all(key):
    band_keys = jax.random.split(jax.random.fold_in(key, 7001), N_GX)
    return jax.vmap(band_layout)(band_keys).reshape(-1).astype(jnp.int32)


def draw_tile_ids(key, part):
    return layout_all(key)


def draw_fluid_mask(key, part):
    tile_ids = layout_all(key)
    fluid_flags = (jax.random.randint(jax.random.fold_in(key, 7002), (GRID_X, GRID_Y, DEPTH), 0, 5) > 0).astype(jnp.int32)
    band_index = jnp.arange(TILES, dtype=jnp.int32) // (N_GY * TILES_DEV)
    first_x = (band_index * TILE_ROWS + tile_ids // BAND_COLS) * EDGE
    first_y = tile_ids % BAND_COLS * EDGE
    spread = jnp.arange(EDGE + 2, dtype=jnp.int32) - 1
    row_index = (first_x[:, None] + spread[None, :]) % GRID_X
    col_index = (first_y[:, None] + spread[None, :]) % GRID_Y
    return fluid_flags[row_index[:, :, None], col_index[:, None, :]].astype(jnp.int32)


def plant(drawn, own_key, low, largest):
    shape = drawn.shape
    index_at = [jax.random.randint(jax.random.fold_in(own_key, axis), (), 0, shape[axis]) for axis in range(len(shape))]
    drawn = drawn.at[tuple(index_at)].set(low)
    longest = shape.index(max(shape))
    index_at[longest] = (index_at[longest] + 1) % shape[longest]
    return drawn.at[tuple(index_at)].set(largest)


def levels(own_key, extent, shards, low, largest):
    loudness = 1.0
    for dim, shards_of in shards:
        draws = jax.random.uniform(jax.random.fold_in(jax.random.fold_in(own_key, 6), dim), (shards_of,), jnp.float32, low / len(shards), largest / len(shards))
        loudness = loudness * jnp.repeat(jnp.exp(draws), extent[dim] // shards_of).reshape((-1,) + (1,) * (len(extent) - 1 - dim))
    return loudness


def centred(own_key, dims, width, reach, shards=(), kind=jnp.bfloat16):
    gain = levels(own_key, dims, shards, -0.22, 0.18) if shards else 1.0
    values = jax.random.normal(own_key, dims, jnp.float32) * width * gain
    return jnp.minimum(jnp.maximum(values, -reach), reach).astype(kind)


def setup_inputs(seed: int = 0) -> dict:
    streams_of = jax.random.split(jax.random.key(seed), 7)
    return {
        "populations": jnp.clip(0.01 + 0.09 * jax.random.uniform(streams_of[0], (19, TILES, EDGE, EDGE, DEPTH), jnp.float32) ** levels(streams_of[0], (19, TILES, EDGE, EDGE, DEPTH), ((1, 128),), -0.2, 0.2), 0.01, 0.1),
        "charge": centred(streams_of[1], (TILES, EDGE, EDGE, DEPTH), 1.0, 6.0, ((0, 128),), jnp.float32),
        "fluid_mask": draw_fluid_mask(jax.random.fold_in(streams_of[6], 71), 0),
        "tile_ids": draw_tile_ids(jax.random.fold_in(streams_of[6], 71), 0),
        "phase_label": plant(jax.random.randint(streams_of[4], (GRID_X, GRID_Y, DEPTH), 0, PHASES), jax.random.fold_in(streams_of[4], 1), 0, PHASES - 1).astype(jnp.int32),
        "permittivity": jnp.clip(jnp.exp(jax.random.uniform(streams_of[5], (PHASES,), jnp.float32, math.log(0.5), math.log(5.0))), 0.5, 5.0),
    }


LATTICE = ((0, 0, 0), (1, 0, 0), (-1, 0, 0), (0, 1, 0), (0, -1, 0), (0, 0, 1), (0, 0, -1),
           (1, 1, 0), (-1, -1, 0), (1, -1, 0), (-1, 1, 0), (1, 0, 1), (-1, 0, -1),
           (1, 0, -1), (-1, 0, 1), (0, 1, 1), (0, -1, -1), (0, 1, -1), (0, -1, 1))
relax_time = 0.8
screening = 0.001
spectrum_low = 0.1
spectrum_high = 2.0


def lattice_weight(direction):
    length = sum(abs(entry) for entry in LATTICE[direction])
    if length == 0:
        return 1.0 / 3.0
    if length == 1:
        return 1.0 / 18.0
    return 1.0 / 36.0


def opposite(direction):
    return LATTICE.index(tuple(-entry for entry in LATTICE[direction]))


def population_sum(population):
    density = population[0]
    for direction in range(1, 19):
        density = density + population[direction]
    return density


def velocity_sums(population):
    sums_list = []
    for axis_index in range(3):
        total = None
        for direction in range(19):
            component = LATTICE[direction][axis_index]
            if component != 0:
                contrib = population[direction] if component > 0 else -population[direction]
                total = contrib if total is None else total + contrib
        sums_list.append(total)
    return sums_list


def collide(population, density, velocity, body_force):
    speed_sq = velocity[0] * velocity[0] + velocity[1] * velocity[1] + velocity[2] * velocity[2]
    source_scale = 1.0 - 0.5 / relax_time
    result = []
    for direction in range(19):
        lattice_step = LATTICE[direction]
        weight = lattice_weight(direction)
        projected = lattice_step[0] * velocity[0] + lattice_step[1] * velocity[1] + lattice_step[2] * velocity[2]
        force_dot = lattice_step[0] * body_force[0] + lattice_step[1] * body_force[1] + lattice_step[2] * body_force[2]
        drift_dot = ((lattice_step[0] - velocity[0]) * body_force[0] + (lattice_step[1] - velocity[1]) * body_force[1]
                     + (lattice_step[2] - velocity[2]) * body_force[2])
        equilibrium = weight * density * (1.0 + 3.0 * projected + 4.5 * projected * projected - 1.5 * speed_sq)
        source = source_scale * weight * (3.0 * drift_dot + 9.0 * projected * force_dot)
        result.append(population[direction] - (population[direction] - equilibrium) / relax_time + source)
    return result


def harmonic(left_value, right_value):
    return 2.0 * left_value * right_value / (left_value + right_value)


def placement(tile_ids):
    band_index = jnp.arange(TILES, dtype=jnp.int32) // (N_GY * TILES_DEV)
    tile_row = band_index * TILE_ROWS + tile_ids // BAND_COLS
    tile_col = tile_ids % BAND_COLS
    slot_at = jnp.zeros((GRID_X // EDGE, GRID_Y // EDGE), jnp.int32).at[tile_row, tile_col].set(
        jnp.arange(TILES, dtype=jnp.int32))
    return tile_row, tile_col, slot_at


def tiles_to_grid(tile_data, slot_at):
    leading = tile_data.shape[0]
    picked = tile_data[:, slot_at]
    picked = jnp.transpose(picked, (0, 1, 3, 2, 4, 5))
    return picked.reshape(leading, GRID_X, GRID_Y, DEPTH)


def grid_to_tiles(grid_data, tile_row, tile_col):
    leading = grid_data.shape[0]
    blocks = grid_data.reshape(leading, GRID_X // EDGE, EDGE, GRID_Y // EDGE, EDGE, DEPTH)
    blocks = jnp.transpose(blocks, (0, 1, 3, 2, 4, 5))
    return blocks[:, tile_row, tile_col]


def apply_operator(field_value, weights_plus, weights_minus, diagonal):
    result = diagonal * field_value
    for axis_index in range(3):
        result = (result - weights_plus[axis_index] * jnp.roll(field_value, -1, axis_index)
                  - weights_minus[axis_index] * jnp.roll(field_value, 1, axis_index))
    return result


def reference(populations, charge, fluid_mask, tile_ids, phase_label, permittivity):
    tile_row, tile_col, slot_at = placement(tile_ids)
    fluid_tiles = fluid_mask[:, 1:EDGE + 1, 1:EDGE + 1].astype(jnp.float32)
    fluid_grid = tiles_to_grid(fluid_tiles[None], slot_at)[0]
    charge_grid = tiles_to_grid(charge[None], slot_at)[0]
    source = charge_grid * fluid_grid
    permit = permittivity[phase_label]
    weights_plus = [harmonic(permit, jnp.roll(permit, -1, axis_index)) for axis_index in range(3)]
    weights_minus = [jnp.roll(weights_plus[axis_index], 1, axis_index) for axis_index in range(3)]
    diagonal = (weights_plus[0] + weights_minus[0] + weights_plus[1] + weights_minus[1]
                + weights_plus[2] + weights_minus[2] + screening)
    center_value = 0.5 * (spectrum_high + spectrum_low)
    half_width = 0.5 * (spectrum_high - spectrum_low)
    ratio_value = center_value / half_width
    rho_old = 1.0 / ratio_value
    residual = source / diagonal
    update = residual / center_value
    potential = update
    for sweep_index in range(SWEEPS - 1):
        residual = residual - apply_operator(update, weights_plus, weights_minus, diagonal) / diagonal
        rho_new = 1.0 / (2.0 * ratio_value - rho_old)
        update = (rho_new * rho_old) * update + (2.0 * rho_new / half_width) * residual
        potential = potential + update
        rho_old = rho_new
    field_grid = jnp.stack([0.5 * (jnp.roll(potential, 1, axis_index) - jnp.roll(potential, -1, axis_index))
                            for axis_index in range(3)])
    field_tiles = grid_to_tiles(field_grid, tile_row, tile_col)
    body_force = [charge * field_tiles[axis_index] for axis_index in range(3)]
    density = population_sum(populations)
    momentum = velocity_sums(populations)
    velocity = [(momentum[axis_index] + 0.5 * body_force[axis_index]) / density for axis_index in range(3)]
    relaxed = collide(populations, density, velocity, body_force)
    outputs = []
    for direction in range(19):
        lattice_step = LATTICE[direction]
        moved = jnp.roll(tiles_to_grid(relaxed[direction][None], slot_at)[0], lattice_step, (0, 1, 2))
        source_fluid = jnp.roll(fluid_grid, lattice_step, (0, 1, 2)) > 0.5
        bounced = tiles_to_grid(relaxed[opposite(direction)][None], slot_at)[0]
        grid_new = jnp.where(source_fluid, moved, bounced)
        tile_new = grid_to_tiles(grid_new[None], tile_row, tile_col)[0]
        outputs.append(jnp.where(fluid_tiles > 0.5, tile_new, populations[direction]))
    populations_next = jnp.stack(outputs)
    change = None
    for axis_index in range(3):
        speed_grid = tiles_to_grid(velocity[axis_index][None], slot_at)[0]
        face_vel = 0.5 * (speed_grid + jnp.roll(speed_grid, -1, axis_index))
        upwind = jnp.where(face_vel > 0, charge_grid, jnp.roll(charge_grid, -1, axis_index))
        face_flux = face_vel * upwind * fluid_grid * jnp.roll(fluid_grid, -1, axis_index)
        flux_term = face_flux - jnp.roll(face_flux, 1, axis_index)
        change = flux_term if change is None else change + flux_term
    change_tiles = grid_to_tiles(change[None], tile_row, tile_col)[0]
    charge_next = jnp.where(fluid_tiles > 0.5, charge - change_tiles, charge)
    return (populations_next, charge_next, potential)
```

```python
import functools

import jax
import jax.numpy as jnp
from jax import lax
from jax.experimental import pallas as pl
from jax.experimental.pallas import tpu as pltpu
from jax.sharding import PartitionSpec as P

EDGE = 16
DEPTH = 128
BLOCK = 32
PHASES = 4
TILES = 4
GROUPS = 16
BANDS = 8
COLS = 32
SIDE = 8
MESH = pl.DeviceIdType.MESH

LATTICE = (
    (0, 0, 0),
    (1, 0, 0),
    (-1, 0, 0),
    (0, 1, 0),
    (0, -1, 0),
    (0, 0, 1),
    (0, 0, -1),
    (1, 1, 0),
    (-1, -1, 0),
    (1, -1, 0),
    (-1, 1, 0),
    (1, 0, 1),
    (-1, 0, -1),
    (1, 0, -1),
    (-1, 0, 1),
    (0, 1, 1),
    (0, -1, -1),
    (0, 1, -1),
    (0, -1, 1),
)
WEIGHTS = (1.0 / 3.0, 1.0 / 18.0, 1.0 / 36.0)
PAIRS = ((1, 2), (3, 4), (5, 6), (7, 8), (9, 10), (11, 12), (13, 14), (15, 16), (17, 18))
relax_time = 0.8
screening = 0.001
spectrum_low = 0.1
spectrum_high = 2.0

AROUND = tuple((dx, dy) for dx in (-1, 0, 1) for dy in (-1, 0, 1) if (dx, dy) != (0, 0))

T_PEER = 0
T_BACK = 4
T_OWNER = 20
T_YLO = 24
T_YHI = 28
T_XIN = 32
T_CLO = 36
T_CHI = 40
T_ROW = 44
T_UP = 48
T_UPLO = 52
T_UPHI = 56
T_DN = 60
T_DNLO = 64
T_DNHI = 68
T_FACE = 72
T_SIZE = 80


def opposite(direction):
    return LATTICE.index(tuple(-entry for entry in LATTICE[direction]))


def crossing(axis_index, face_sign):
    return [d for d in range(19) if LATTICE[d][axis_index] == face_sign]


def shifted_id(dx, dy):
    gx = lax.rem(lax.axis_index("gx") + dx + BANDS, BANDS)
    gy = lax.rem(lax.axis_index("gy") + dy + GROUPS, GROUPS)
    return {"gx": gx, "gy": gy}


def span(step, width, pad):
    if step == 0:
        return pl.ds(0, BLOCK), pl.ds(pad, BLOCK)
    if step > 0:
        return pl.ds(BLOCK - width, width), pl.ds(pad - width, width)
    return pl.ds(0, width), pl.ds(pad + BLOCK, width)


def halo_copies(block_ref, ext_ref, width, send_sem, recv_sem):
    copies = []
    for n, (dx, dy) in enumerate(AROUND):
        src_i, dst_i = span(dx, width, width)
        src_j, dst_j = span(dy, SIDE, SIDE)
        copies.append(
            pltpu.make_async_remote_copy(
                src_ref=block_ref.at[src_i, src_j],
                dst_ref=ext_ref.at[dst_i, dst_j],
                send_sem=send_sem.at[n],
                recv_sem=recv_sem.at[n],
                device_id=shifted_id(dx, dy),
                device_id_type=MESH,
            )
        )
    return copies


def start_kernel(ids_ref, phase_ref, all_ref, ext_ref, send_sem, recv_sem, ids_send, ids_recv, own_sem):
    barrier = pltpu.get_barrier_semaphore()
    targets = [shifted_id(0, k) for k in range(1, GROUPS)]
    targets += [shifted_id(dx, dy) for dx, dy in AROUND if dx != 0]
    for target in targets:
        pl.semaphore_signal(barrier, inc=1, device_id=target, device_id_type=MESH)
    pl.semaphore_wait(barrier, len(targets))
    copies = []
    for k in range(1, GROUPS):
        copies.append((k, shifted_id(0, k)))
    copies.append((GROUPS, shifted_id(-1, 0)))
    copies.append((GROUPS + 1, shifted_id(1, 0)))
    started = []
    for k, target in copies:
        copy = pltpu.make_async_remote_copy(
            src_ref=ids_ref,
            dst_ref=all_ref.at[k],
            send_sem=ids_send.at[k],
            recv_sem=ids_recv.at[k],
            device_id=target,
            device_id_type=MESH,
        )
        copy.start()
        started.append(copy)
    for copy in halo_copies(phase_ref, ext_ref, 5, send_sem, recv_sem):
        copy.start()
        started.append(copy)
    own = [
        pltpu.make_async_copy(ids_ref, all_ref.at[0], own_sem.at[0]),
        pltpu.make_async_copy(
            phase_ref, ext_ref.at[pl.ds(5, BLOCK), pl.ds(SIDE, BLOCK)], own_sem.at[1]
        ),
    ]
    for copy in own:
        copy.start()
    for copy in own:
        copy.wait()
    for copy in started:
        copy.wait()


def exchange_start(ids, phase):
    vmem = pl.BlockSpec(memory_space=pltpu.VMEM)
    return pl.pallas_call(
        start_kernel,
        out_shape=(
            jax.ShapeDtypeStruct((GROUPS + 2, 8, DEPTH), jnp.int32),
            jax.ShapeDtypeStruct((BLOCK + 10, BLOCK + 2 * SIDE, DEPTH), jnp.int32),
        ),
        in_specs=[vmem, vmem],
        out_specs=(vmem, vmem),
        scratch_shapes=[
            pltpu.SemaphoreType.DMA((8,)),
            pltpu.SemaphoreType.DMA((8,)),
            pltpu.SemaphoreType.DMA((GROUPS + 2,)),
            pltpu.SemaphoreType.DMA((GROUPS + 2,)),
            pltpu.SemaphoreType.DMA((2,)),
        ],
        compiler_params=pltpu.CompilerParams(
            collective_id=0, has_side_effects=True, vmem_limit_bytes=8 << 20
        ),
        name="start",
    )(ids, phase)


def halo_kernel(block_ref, ext_ref, send_sem, recv_sem, own_sem):
    barrier = pltpu.get_barrier_semaphore()
    for dx, dy in AROUND:
        pl.semaphore_signal(barrier, inc=1, device_id=shifted_id(dx, dy), device_id_type=MESH)
    pl.semaphore_wait(barrier, len(AROUND))
    copies = halo_copies(block_ref, ext_ref, 4, send_sem, recv_sem)
    for copy in copies:
        copy.start()
    own = pltpu.make_async_copy(
        block_ref, ext_ref.at[pl.ds(4, BLOCK), pl.ds(SIDE, BLOCK)], own_sem
    )
    own.start()
    own.wait()
    for copy in copies:
        copy.wait()


def exchange_halo(block):
    vmem = pl.BlockSpec(memory_space=pltpu.VMEM)
    return pl.pallas_call(
        halo_kernel,
        out_shape=jax.ShapeDtypeStruct((BLOCK + 8, BLOCK + 2 * SIDE, DEPTH), jnp.float32),
        in_specs=[vmem],
        out_specs=vmem,
        scratch_shapes=[
            pltpu.SemaphoreType.DMA((8,)),
            pltpu.SemaphoreType.DMA((8,)),
            pltpu.SemaphoreType.DMA,
        ],
        compiler_params=pltpu.CompilerParams(
            collective_id=1, has_side_effects=True, vmem_limit_bytes=8 << 20
        ),
        name="halo",
    )(block)


def table_kernel(me_ref, ids_ref, out_ref, row_of):
    me = me_ref[0]

    def place(p, carry):
        k = lax.rem(me - p + GROUPS, GROUPS)
        for s in range(TILES):
            row_of[ids_ref[k, s]] = p * TILES + s
        return carry

    lax.fori_loop(0, GROUPS, place, 0)
    for p in range(GROUPS):
        out_ref[T_BACK + p] = 0
    for t in range(TILES):
        slot = row_of[(t // 2) * COLS + me * 2 + t % 2]
        peer = slot // TILES
        out_ref[T_PEER + t] = peer
        out_ref[T_BACK + peer] = t
    for s in range(TILES):
        own = ids_ref[0, s]
        row, col = own // COLS, lax.rem(own, COLS)
        left, right = lax.rem(col + COLS - 1, COLS), lax.rem(col + 1, COLS)
        other = (1 - row) * COLS
        out_ref[T_OWNER + s] = col // 2
        out_ref[T_YLO + s] = row_of[row * COLS + left]
        out_ref[T_YHI + s] = row_of[row * COLS + right]
        out_ref[T_XIN + s] = row_of[other + col]
        out_ref[T_CLO + s] = row_of[other + left]
        out_ref[T_CHI + s] = row_of[other + right]
        out_ref[T_ROW + s] = row
        out_ref[T_FACE + s] = row
        for slot, base, first in ((GROUPS, COLS, T_UP), (GROUPS + 1, 0, T_DN)):
            col = lax.rem(ids_ref[slot, s], COLS)
            left, right = lax.rem(col + COLS - 1, COLS), lax.rem(col + 1, COLS)
            out_ref[first + s] = row_of[base + col]
            out_ref[first + 4 + s] = row_of[base + left]
            out_ref[first + 8 + s] = row_of[base + right]


def make_table(me, ids):
    smem = pl.BlockSpec(memory_space=pltpu.SMEM)
    return pl.pallas_call(
        table_kernel,
        out_shape=jax.ShapeDtypeStruct((T_SIZE,), jnp.int32),
        in_specs=[smem, smem],
        out_specs=smem,
        scratch_shapes=[pltpu.SMEM((2 * COLS,), jnp.int32)],
        name="table",
    )(me, ids)


def spread_kernel(ids_ref, charge_ref, mask_ref, out_ref, masked):
    def fill(s, carry):
        def rows(i, inner):
            flags = mask_ref[s, i + 1, pl.ds(1, EDGE), :].astype(jnp.float32)
            masked[s, i] = charge_ref[s, i] * flags
            return inner

        return lax.fori_loop(0, EDGE, rows, carry)

    lax.fori_loop(0, TILES, fill, 0)

    def send(p, carry):
        slot = 0
        for s in range(1, TILES):
            owner = lax.rem(ids_ref[s], COLS) // 2
            slot = jnp.where(owner == p, s, slot)
        out_ref[p] = masked[slot]
        return carry

    lax.fori_loop(0, GROUPS, send, 0)


def spread(tile_ids, charge, fluid_mask):
    vmem = pl.BlockSpec(memory_space=pltpu.VMEM)
    return pl.pallas_call(
        spread_kernel,
        out_shape=jax.ShapeDtypeStruct((GROUPS, EDGE, EDGE, DEPTH), jnp.float32),
        in_specs=[pl.BlockSpec(memory_space=pltpu.SMEM), vmem, vmem],
        out_specs=vmem,
        scratch_shapes=[pltpu.VMEM((TILES, EDGE, EDGE, DEPTH), jnp.float32)],
        compiler_params=pltpu.CompilerParams(vmem_limit_bytes=16 << 20),
        name="spread",
    )(tile_ids, charge, fluid_mask)


def assemble_kernel(table_ref, arrived_ref, out_ref):
    out_ref[...] = arrived_ref[0]


def assemble(table, arrived):
    return pl.pallas_call(
        assemble_kernel,
        out_shape=jax.ShapeDtypeStruct((BLOCK, BLOCK, DEPTH), jnp.float32),
        grid_spec=pltpu.PrefetchScalarGridSpec(
            num_scalar_prefetch=1,
            grid=(TILES,),
            in_specs=[
                pl.BlockSpec((1, EDGE, EDGE, DEPTH), lambda t, tab: (tab[T_PEER + t], 0, 0, 0))
            ],
            out_specs=pl.BlockSpec((EDGE, EDGE, DEPTH), lambda t, tab: (t // 2, t % 2, 0)),
        ),
        compiler_params=pltpu.CompilerParams(vmem_limit_bytes=8 << 20),
        name="assemble",
    )(table, arrived)


WIDE = BLOCK + 2 * SIDE
TALL = BLOCK + 8
ROOM = WIDE + 16
INNER = pl.ds(8, WIDE)
BEFORE = pl.ds(7, WIDE)
AFTER = pl.ds(9, WIDE)
PACK = 24


def harmonic(left, right):
    return 2.0 * left * right / (left + right)


def solve_kernel(
    table_ref, permit_ref, phase_ref, source_ref, pot_ref, send_ref, permit, coef, resid, upd_a, upd_b, total, pack
):
    center = 0.5 * (spectrum_high + spectrum_low)
    half = 0.5 * (spectrum_high - spectrum_low)
    ratio = center / half

    def look_up(i, carry):
        label = phase_ref[i]
        value = jnp.where(label == 0, permit_ref[0], 0.0)
        for k in range(1, PHASES):
            value = jnp.where(label == k, permit_ref[k], value)
        permit[i] = value
        return carry

    lax.fori_loop(0, TALL + 2, look_up, 0)

    def weigh(i, below):
        here = permit[i + 1]
        above = harmonic(here, permit[i + 2])
        right = harmonic(here, pltpu.roll(here, WIDE - 1, 0))
        left = pltpu.roll(right, 1, 0)
        up = harmonic(here, pltpu.roll(here, DEPTH - 1, 1))
        down = pltpu.roll(up, 1, 1)
        scale = 1.0 / (above + below + right + left + up + down + screening)
        for k, weight in enumerate((above, below, right, left, up, down)):
            coef[k, i] = weight * scale
        first = source_ref[i] * scale
        resid[i] = first
        first = first * (1.0 / center)
        upd_a[i, INNER] = first
        total[i] = first
        return above

    lax.fori_loop(0, TALL, weigh, harmonic(permit[0], permit[1]))

    rho = 1.0 / ratio
    old, new = upd_a, upd_b
    for sweep in range(3):
        rho_new = 1.0 / (2.0 * ratio - rho)
        keep, gain = rho_new * rho, 2.0 * rho_new / half

        def relax(i, carry, old=old, new=new, keep=keep, gain=gain):
            here = old[i, INNER]
            near = coef[0, i] * old[i + 1, INNER] + coef[1, i] * old[i - 1, INNER]
            near += coef[2, i] * old[i, AFTER] + coef[3, i] * old[i, BEFORE]
            near += coef[4, i] * pltpu.roll(here, DEPTH - 1, 1)
            near += coef[5, i] * pltpu.roll(here, 1, 1)
            left = resid[i] - here + near
            resid[i] = left
            here = keep * here + gain * left
            new[i, INNER] = here
            total[i] = total[i] + here
            return carry

        lax.fori_loop(sweep + 1, TALL - 1 - sweep, relax, 0)
        old, new = new, old
        rho = rho_new

    def emit(i, carry):
        pot_ref[i] = total[i + 4, pl.ds(SIDE, BLOCK)]
        return carry

    lax.fori_loop(0, BLOCK, emit, 0)
    for t in range(TILES):
        i0, j0 = 4 + (t // 2) * EDGE, SIDE + (t % 2) * EDGE

        def rows(i, carry, t=t, i0=i0, j0=j0):
            pack[t, i] = total[i0 + i, pl.ds(j0, EDGE)]
            for place, ref in ((EDGE + 2, total), (EDGE + 6, source_ref)):
                pack[t, place, pl.ds(i, 1)] = ref[i0 + i, pl.ds(j0 - 1, 1)]
                pack[t, place + 1, pl.ds(i, 1)] = ref[i0 + i, pl.ds(j0 + EDGE, 1)]
            return carry

        lax.fori_loop(0, EDGE, rows, 0)
        for place, ref in ((EDGE, total), (EDGE + 4, source_ref)):
            pack[t, place] = ref[i0 - 1, pl.ds(j0, EDGE)]
            pack[t, place + 1] = ref[i0 + EDGE, pl.ds(j0, EDGE)]

    def send(p, carry):
        send_ref[p] = pack[table_ref[T_BACK + p]]
        return carry

    lax.fori_loop(0, GROUPS, send, 0)


def solve(table, permittivity, phase, source):
    vmem = pl.BlockSpec(memory_space=pltpu.VMEM)
    smem = pl.BlockSpec(memory_space=pltpu.SMEM)
    f32 = jnp.float32
    return pl.pallas_call(
        solve_kernel,
        out_shape=(
            jax.ShapeDtypeStruct((BLOCK, BLOCK, DEPTH), f32),
            jax.ShapeDtypeStruct((GROUPS, PACK, EDGE, DEPTH), f32),
        ),
        in_specs=[smem, smem, vmem, vmem],
        out_specs=(vmem, vmem),
        scratch_shapes=[
            pltpu.VMEM((TALL + 2, WIDE, DEPTH), f32),
            pltpu.VMEM((6, TALL, WIDE, DEPTH), f32),
            pltpu.VMEM((TALL, WIDE, DEPTH), f32),
            pltpu.VMEM((TALL, ROOM, DEPTH), f32),
            pltpu.VMEM((TALL, ROOM, DEPTH), f32),
            pltpu.VMEM((TALL, WIDE, DEPTH), f32),
            pltpu.VMEM((TILES, PACK, EDGE, DEPTH), f32),
        ],
        compiler_params=pltpu.CompilerParams(vmem_limit_bytes=32 << 20),
        name="solve",
    )(table, permittivity, phase, source)


def collide_rows(pops, charge, field):
    force = [charge * component for component in field]
    sums = {}
    diffs = {}
    for a, b in PAIRS:
        sums[a] = pops[a] + pops[b]
        diffs[a] = pops[a] - pops[b]
    density = pops[0]
    for a, _ in PAIRS:
        density = density + sums[a]
    momentum = [
        diffs[1] + diffs[7] + diffs[9] + diffs[11] + diffs[13],
        diffs[3] + diffs[7] - diffs[9] + diffs[15] + diffs[17],
        diffs[5] + diffs[11] - diffs[13] + diffs[15] - diffs[17],
    ]
    inverse = 1.0 / density
    velocity = [(momentum[d] + 0.5 * force[d]) * inverse for d in range(3)]
    scale = 1.0 - 0.5 / relax_time
    rate = 1.0 / relax_time
    speed = velocity[0] * velocity[0] + velocity[1] * velocity[1] + velocity[2] * velocity[2]
    work = velocity[0] * force[0] + velocity[1] * force[1] + velocity[2] * force[2]
    weighted = rate * density
    base = weighted - (1.5 * weighted) * speed - (3.0 * scale) * work
    odd = [3.0 * weighted * velocity[d] + (3.0 * scale) * force[d] for d in range(3)]
    inner = [4.5 * weighted * velocity[d] + (9.0 * scale) * force[d] for d in range(3)]
    keep = 1.0 - rate
    result = [None] * 19
    result[0] = keep * pops[0] + WEIGHTS[0] * base
    for a, b in PAIRS:
        step = LATTICE[a]
        axes = [d for d in range(3) if step[d] != 0]
        if len(axes) == 1:
            (d,) = axes
            cu, co, ci = velocity[d], odd[d], inner[d]
            weight = WEIGHTS[1]
        else:
            d, e = axes
            weight = WEIGHTS[2]
            if step[d] * step[e] > 0:
                cu, co, ci = velocity[d] + velocity[e], odd[d] + odd[e], inner[d] + inner[e]
            else:
                cu, co, ci = velocity[d] - velocity[e], odd[d] - odd[e], inner[d] - inner[e]
        even = weight * (base + cu * ci)
        lean = weight * co
        result[a] = keep * pops[a] + (even + lean)
        result[b] = keep * pops[b] + (even - lean)
    return result, velocity


def collide_kernel(table_ref, pops_ref, charge_ref, mask_ref, pot_ref, out_ref, vel_ref, face_ref, grown):
    def place(i, carry):
        grown[i + 1, pl.ds(8, EDGE)] = pot_ref[0, i]
        grown[i + 1, pl.ds(7, 1)] = pot_ref[0, EDGE + 2, pl.ds(i, 1)]
        grown[i + 1, pl.ds(8 + EDGE, 1)] = pot_ref[0, EDGE + 3, pl.ds(i, 1)]
        return carry

    lax.fori_loop(0, EDGE, place, 0)
    grown[0, pl.ds(8, EDGE)] = pot_ref[0, EDGE]
    grown[EDGE + 1, pl.ds(8, EDGE)] = pot_ref[0, EDGE + 1]
    y_low, y_high = crossing(1, -1), crossing(1, 1)

    def rows(i, carry):
        here = grown[i + 1, pl.ds(8, EDGE)]
        field = [
            0.5 * (grown[i, pl.ds(8, EDGE)] - grown[i + 2, pl.ds(8, EDGE)]),
            0.5 * (grown[i + 1, pl.ds(7, EDGE)] - grown[i + 1, pl.ds(9, EDGE)]),
            0.5 * (pltpu.roll(here, 1, 1) - pltpu.roll(here, DEPTH - 1, 1)),
        ]
        pops = [pops_ref[q, 0, i] for q in range(19)]
        relaxed, velocity = collide_rows(pops, charge_ref[0, i], field)
        fluid = mask_ref[0, i + 1, pl.ds(1, EDGE), :] == 1
        for q in range(19):
            value = jnp.where(fluid, relaxed[q], pops[q])
            out_ref[q, 0, i] = value
            if q in y_low:
                face_ref[0, 2, y_low.index(q), pl.ds(i, 1)] = value[0:1]
            if q in y_high:
                face_ref[0, 3, y_high.index(q), pl.ds(i, 1)] = value[EDGE - 1 :]
        for d in range(3):
            vel_ref[d, 0, i] = velocity[d]
        face_ref[0, 2, 5, pl.ds(i, 1)] = velocity[1][0:1]
        face_ref[0, 3, 5, pl.ds(i, 1)] = velocity[1][EDGE - 1 :]
        return carry

    lax.fori_loop(0, EDGE, rows, 0)
    for face, sign, layer in ((0, -1, 0), (1, 1, EDGE - 1)):
        for k, q in enumerate(crossing(0, sign)):
            face_ref[0, face, k] = out_ref[q, 0, layer]
        face_ref[0, face, 5] = vel_ref[0, 0, layer]


def collide(table, populations, charge, fluid_mask, returned):
    f32 = jnp.float32
    return pl.pallas_call(
        collide_kernel,
        out_shape=(
            jax.ShapeDtypeStruct((19, TILES, EDGE, EDGE, DEPTH), f32),
            jax.ShapeDtypeStruct((3, TILES, EDGE, EDGE, DEPTH), f32),
            jax.ShapeDtypeStruct((TILES, 4, 6, EDGE, DEPTH), f32),
        ),
        grid_spec=pltpu.PrefetchScalarGridSpec(
            num_scalar_prefetch=1,
            grid=(TILES,),
            in_specs=[
                pl.BlockSpec((19, 1, EDGE, EDGE, DEPTH), lambda s, tab: (0, s, 0, 0, 0)),
                pl.BlockSpec((1, EDGE, EDGE, DEPTH), lambda s, tab: (s, 0, 0, 0)),
                pl.BlockSpec((1, EDGE + 2, EDGE + 2, DEPTH), lambda s, tab: (s, 0, 0, 0)),
                pl.BlockSpec((1, PACK, EDGE, DEPTH), lambda s, tab: (tab[T_OWNER + s], 0, 0, 0)),
            ],
            out_specs=[
                pl.BlockSpec((19, 1, EDGE, EDGE, DEPTH), lambda s, tab: (0, s, 0, 0, 0)),
                pl.BlockSpec((3, 1, EDGE, EDGE, DEPTH), lambda s, tab: (0, s, 0, 0, 0)),
                pl.BlockSpec((1, 4, 6, EDGE, DEPTH), lambda s, tab: (s, 0, 0, 0, 0)),
            ],
            scratch_shapes=[pltpu.VMEM((EDGE + 2, 32, DEPTH), f32)],
        ),
        compiler_params=pltpu.CompilerParams(vmem_limit_bytes=32 << 20),
        name="collide",
    )(table, populations, charge, fluid_mask, returned)


def outer_kernel(table_ref, up_ref, uplo_ref, uphi_ref, dn_ref, dnlo_ref, dnhi_ref, to_up, to_dn):
    plus, minus = crossing(0, 1), crossing(0, -1)
    for out, face, low, high, low_q, high_q in (
        (to_up, up_ref, uplo_ref, uphi_ref, plus.index(7), plus.index(9)),
        (to_dn, dn_ref, dnlo_ref, dnhi_ref, minus.index(10), minus.index(8)),
    ):
        for k in range(6):
            out[0, k] = face[0, 0, k]
        out[0, 6, pl.ds(0, 1)] = low[0, 0, low_q, pl.ds(EDGE - 1, 1)]
        out[0, 6, pl.ds(1, 1)] = high[0, 0, high_q, pl.ds(0, 1)]


def outer(table, gathered):
    def face(place, side):
        return pl.BlockSpec(
            (1, 1, 6, EDGE, DEPTH), lambda s, tab: (tab[place + s], side, 0, 0, 0)
        )

    shape = jax.ShapeDtypeStruct((TILES, 7, EDGE, DEPTH), jnp.float32)
    spec = pl.BlockSpec((1, 7, EDGE, DEPTH), lambda s, tab: (s, 0, 0, 0))
    return pl.pallas_call(
        outer_kernel,
        out_shape=(shape, shape),
        grid_spec=pltpu.PrefetchScalarGridSpec(
            num_scalar_prefetch=1,
            grid=(TILES,),
            in_specs=[
                face(T_UP, 1),
                face(T_UPLO, 1),
                face(T_UPHI, 1),
                face(T_DN, 0),
                face(T_DNLO, 0),
                face(T_DNHI, 0),
            ],
            out_specs=[spec, spec],
        ),
        compiler_params=pltpu.CompilerParams(vmem_limit_bytes=8 << 20),
        name="outer",
    )(table, *([gathered] * 6))


def stream_kernel(
    table_ref,
    relaxed_ref,
    vel_ref,
    charge_ref,
    mask_ref,
    rim_ref,
    ylo_ref,
    yhi_ref,
    xin_ref,
    clo_ref,
    chi_ref,
    below_ref,
    above_ref,
    pops_out,
    charge_out,
    xrim,
    corner,
):
    row = table_ref[T_ROW + pl.program_id(0)]
    plus = [crossing(0, 1), crossing(1, 1)]
    minus = [crossing(0, -1), crossing(1, -1)]

    def inside(side, low_q, high_q):
        for k in range(6):
            xrim[side, k] = xin_ref[0, 0, k]
        corner[side, pl.ds(0, 1)] = clo_ref[0, 0, low_q, pl.ds(EDGE - 1, 1)]
        corner[side, pl.ds(1, 1)] = chi_ref[0, 0, high_q, pl.ds(0, 1)]

    def outside(side, ref):
        for k in range(6):
            xrim[side, k] = ref[0, k]
        corner[side, pl.ds(0, 2)] = ref[0, 6, pl.ds(0, 2)]

    @pl.when(row == 0)
    def _():
        outside(0, below_ref)
        inside(1, minus[0].index(10), minus[0].index(8))

    @pl.when(row == 1)
    def _():
        inside(0, plus[0].index(7), plus[0].index(9))
        outside(1, above_ref)

    place = lax.broadcasted_iota(jnp.int32, (EDGE, DEPTH), 0)
    first, last = place == 0, place == EDGE - 1

    def rows(i, low_edge, high_edge):
        own = mask_ref[0, i + 1, pl.ds(1, EDGE), :]
        own_fluid = own == 1
        for q in range(19):
            step_x, step_y, step_z = LATTICE[q]
            value_here = relaxed_ref[q, 0, i]
            if q == 0:
                pops_out[q, 0, i] = value_here
                continue
            side = None
            if step_x == 1 and low_edge:
                side, channel = 0, plus[0].index(q)
            if step_x == -1 and high_edge:
                side, channel = 1, minus[0].index(q)
            if side is None:
                moved = value_here if step_x == 0 else relaxed_ref[q, 0, i - step_x]
            else:
                moved = xrim[side, channel]
            if step_y == 1:
                if side is None:
                    edge = ylo_ref[0, 0, plus[1].index(q), pl.ds(i - step_x, 1)]
                else:
                    edge = corner[side, pl.ds(0, 1)]
                moved = jnp.where(first, edge, pltpu.roll(moved, 1, 0))
            elif step_y == -1:
                if side is None:
                    edge = yhi_ref[0, 0, minus[1].index(q), pl.ds(i - step_x, 1)]
                else:
                    edge = corner[side, pl.ds(1, 1)]
                moved = jnp.where(last, edge, pltpu.roll(moved, EDGE - 1, 0))
            from_fluid = mask_ref[0, i + 1 - step_x, pl.ds(1 - step_y, EDGE), :]
            if step_z != 0:
                moved = pltpu.roll(moved, step_z % DEPTH, 1)
                from_fluid = pltpu.roll(from_fluid, step_z % DEPTH, 1)
            bounced = relaxed_ref[opposite(q), 0, i]
            read = jnp.where(from_fluid == 1, moved, bounced)
            pops_out[q, 0, i] = jnp.where(own_fluid, read, value_here)

        charge = charge_ref[0, i]
        flag = own.astype(jnp.float32)

        def flux(speed_a, speed_b, value_a, value_b, flags):
            speed = 0.5 * (speed_a + speed_b)
            return speed * jnp.where(speed > 0, value_a, value_b) * flags

        speed = vel_ref[0, 0, i]
        if low_edge:
            other, other_speed = rim_ref[0, 0], xrim[0, 5]
        else:
            other, other_speed = charge_ref[0, i - 1], vel_ref[0, 0, i - 1]
        other_flag = mask_ref[0, i, pl.ds(1, EDGE), :].astype(jnp.float32)
        change = -flux(other_speed, speed, other, charge, other_flag * flag)
        if high_edge:
            other, other_speed = rim_ref[0, 1], xrim[1, 5]
        else:
            other, other_speed = charge_ref[0, i + 1], vel_ref[0, 0, i + 1]
        other_flag = mask_ref[0, i + 2, pl.ds(1, EDGE), :].astype(jnp.float32)
        change += flux(speed, other_speed, charge, other, flag * other_flag)

        speed = vel_ref[1, 0, i]
        other = jnp.where(first, rim_ref[0, 2, pl.ds(i, 1)], pltpu.roll(charge, 1, 0))
        other_speed = jnp.where(first, ylo_ref[0, 0, 5, pl.ds(i, 1)], pltpu.roll(speed, 1, 0))
        other_flag = mask_ref[0, i + 1, pl.ds(0, EDGE), :].astype(jnp.float32)
        change -= flux(other_speed, speed, other, charge, other_flag * flag)
        other = jnp.where(last, rim_ref[0, 3, pl.ds(i, 1)], pltpu.roll(charge, EDGE - 1, 0))
        other_speed = jnp.where(
            last, yhi_ref[0, 0, 5, pl.ds(i, 1)], pltpu.roll(speed, EDGE - 1, 0)
        )
        other_flag = mask_ref[0, i + 1, pl.ds(2, EDGE), :].astype(jnp.float32)
        change += flux(speed, other_speed, charge, other, flag * other_flag)

        speed = vel_ref[2, 0, i]
        over = flux(
            speed,
            pltpu.roll(speed, DEPTH - 1, 1),
            charge,
            pltpu.roll(charge, DEPTH - 1, 1),
            flag * pltpu.roll(flag, DEPTH - 1, 1),
        )
        change += over - pltpu.roll(over, 1, 1)
        charge_out[0, i] = jnp.where(own_fluid, charge - change, charge)

    rows(0, True, False)

    def middle(i, carry):
        rows(i, False, False)
        return carry

    lax.fori_loop(1, EDGE - 1, middle, 0)
    rows(EDGE - 1, False, True)


def stream(table, relaxed, velocity, charge, fluid_mask, returned, gathered, below, above):
    f32 = jnp.float32

    def face(place, side):
        return pl.BlockSpec(
            (1, 1, 6, EDGE, DEPTH), lambda s, tab: (tab[place + s], side, 0, 0, 0)
        )

    def inner_face(place):
        return pl.BlockSpec(
            (1, 1, 6, EDGE, DEPTH),
            lambda s, tab: (tab[place + s], tab[T_FACE + s], 0, 0, 0),
        )

    outer_spec = pl.BlockSpec((1, 7, EDGE, DEPTH), lambda s, tab: (s, 0, 0, 0))
    return pl.pallas_call(
        stream_kernel,
        out_shape=(
            jax.ShapeDtypeStruct((19, TILES, EDGE, EDGE, DEPTH), f32),
            jax.ShapeDtypeStruct((TILES, EDGE, EDGE, DEPTH), f32),
        ),
        grid_spec=pltpu.PrefetchScalarGridSpec(
            num_scalar_prefetch=1,
            grid=(TILES,),
            in_specs=[
                pl.BlockSpec((19, 1, EDGE, EDGE, DEPTH), lambda s, tab: (0, s, 0, 0, 0)),
                pl.BlockSpec((3, 1, EDGE, EDGE, DEPTH), lambda s, tab: (0, s, 0, 0, 0)),
                pl.BlockSpec((1, EDGE, EDGE, DEPTH), lambda s, tab: (s, 0, 0, 0)),
                pl.BlockSpec((1, EDGE + 2, EDGE + 2, DEPTH), lambda s, tab: (s, 0, 0, 0)),
                pl.BlockSpec((1, 4, EDGE, DEPTH), lambda s, tab: (tab[T_OWNER + s], 5, 0, 0)),
                face(T_YLO, 3),
                face(T_YHI, 2),
                inner_face(T_XIN),
                inner_face(T_CLO),
                inner_face(T_CHI),
                outer_spec,
                outer_spec,
            ],
            out_specs=[
                pl.BlockSpec((19, 1, EDGE, EDGE, DEPTH), lambda s, tab: (0, s, 0, 0, 0)),
                pl.BlockSpec((1, EDGE, EDGE, DEPTH), lambda s, tab: (s, 0, 0, 0)),
            ],
            scratch_shapes=[
                pltpu.VMEM((2, 6, EDGE, DEPTH), f32),
                pltpu.VMEM((2, 8, DEPTH), f32),
            ],
        ),
        compiler_params=pltpu.CompilerParams(vmem_limit_bytes=32 << 20),
        name="stream",
    )(
        table,
        relaxed,
        velocity,
        charge,
        fluid_mask,
        returned,
        gathered,
        gathered,
        gathered,
        gathered,
        gathered,
        below,
        above,
    )


def per_device(populations, charge, fluid_mask, tile_ids, phase_label, permittivity):
    outgoing = spread(tile_ids, charge, fluid_mask)
    arrived = lax.all_to_all(outgoing, "gy", split_axis=0, concat_axis=0, tiled=True)
    ids_row = jnp.pad(tile_ids[None], ((0, 7), (0, DEPTH - TILES)))
    ids_all, phase_ext = exchange_start(ids_row, phase_label)
    me = lax.axis_index("gy").astype(jnp.int32).reshape(1)
    table = make_table(me, ids_all[:, 0, :TILES])
    source_ext = exchange_halo(assemble(table, arrived))
    potential, packed = solve(table, permittivity, phase_ext, source_ext)
    returned = lax.all_to_all(packed, "gy", split_axis=0, concat_axis=0, tiled=True)
    relaxed, velocity, faces = collide(table, populations, charge, fluid_mask, returned)
    gathered = lax.all_gather(faces, "gy", axis=0, tiled=True)
    to_up, to_dn = outer(table, gathered)
    up = [(k, (k + 1) % BANDS) for k in range(BANDS)]
    below = lax.ppermute(to_up, "gx", up)
    above = lax.ppermute(to_dn, "gx", [(b, a) for a, b in up])
    populations_next, charge_next = stream(
        table, relaxed, velocity, charge, fluid_mask, returned, gathered, below, above
    )
    return (populations_next, charge_next, potential)


def solution(mesh):
    placed = (
        P(None, ("gx", "gy"), None, None, None),
        P(("gx", "gy"), None, None, None),
        P(("gx", "gy"), None, None, None),
        P(("gx", "gy")),
        P("gx", "gy", None),
        P(),
    )
    return jax.shard_map(
        per_device,
        mesh=mesh,
        in_specs=placed,
        out_specs=(
            P(None, ("gx", "gy"), None, None, None),
            P(("gx", "gy"), None, None, None),
            P("gx", "gy", None),
        ),
        check_vma=False,
    )
```

```python
import functools

import jax
import jax.numpy as jnp
from jax import lax
from jax.experimental import pallas as pl
from jax.experimental.pallas import tpu as pltpu
from jax.sharding import PartitionSpec as P

EDGE = 16
DEPTH = 128
BLOCK = 32
PHASES = 4
TILES = 4
GROUPS = 16
BANDS = 8
COLS = 32
SIDE = 8
MESH = pl.DeviceIdType.MESH

LATTICE = (
    (0, 0, 0),
    (1, 0, 0),
    (-1, 0, 0),
    (0, 1, 0),
    (0, -1, 0),
    (0, 0, 1),
    (0, 0, -1),
    (1, 1, 0),
    (-1, -1, 0),
    (1, -1, 0),
    (-1, 1, 0),
    (1, 0, 1),
    (-1, 0, -1),
    (1, 0, -1),
    (-1, 0, 1),
    (0, 1, 1),
    (0, -1, -1),
    (0, 1, -1),
    (0, -1, 1),
)
WEIGHTS = (1.0 / 3.0, 1.0 / 18.0, 1.0 / 36.0)
PAIRS = ((1, 2), (3, 4), (5, 6), (7, 8), (9, 10), (11, 12), (13, 14), (15, 16), (17, 18))
relax_time = 0.8
screening = 0.001
spectrum_low = 0.1
spectrum_high = 2.0

AROUND = tuple((dx, dy) for dx in (-1, 0, 1) for dy in (-1, 0, 1) if (dx, dy) != (0, 0))

T_PEER = 0
T_ROW = 4
T_CORNER = 8
T_SIZE = 24


def opposite(direction):
    return LATTICE.index(tuple(-entry for entry in LATTICE[direction]))


def crossing(axis_index, face_sign):
    return [d for d in range(19) if LATTICE[d][axis_index] == face_sign]


def shifted_id(dx, dy):
    gx = lax.rem(lax.axis_index("gx") + dx + BANDS, BANDS)
    gy = lax.rem(lax.axis_index("gy") + dy + GROUPS, GROUPS)
    return {"gx": gx, "gy": gy}


def span(step, width, pad):
    if step == 0:
        return pl.ds(0, BLOCK), pl.ds(pad, BLOCK)
    if step > 0:
        return pl.ds(BLOCK - width, width), pl.ds(pad - width, width)
    return pl.ds(0, width), pl.ds(pad + BLOCK, width)


def halo_copies(block_ref, ext_ref, width, send_sem, recv_sem):
    copies = []
    for n, (dx, dy) in enumerate(AROUND):
        src_i, dst_i = span(dx, width, width)
        src_j, dst_j = span(dy, SIDE, SIDE)
        copies.append(
            pltpu.make_async_remote_copy(
                src_ref=block_ref.at[src_i, src_j],
                dst_ref=ext_ref.at[dst_i, dst_j],
                send_sem=send_sem.at[n],
                recv_sem=recv_sem.at[n],
                device_id=shifted_id(dx, dy),
                device_id_type=MESH,
            )
        )
    return copies


def start_kernel(
    ids_ref,
    phase_ref,
    tiles_ref,
    all_ref,
    ext_ref,
    arrived_ref,
    send_sem,
    recv_sem,
    ids_send,
    ids_recv,
    tile_send,
    tile_recv,
    own_sem,
):
    me = lax.axis_index("gy")
    barrier = pltpu.get_barrier_semaphore()
    peers = [shifted_id(0, k) for k in range(1, GROUPS)]
    targets = peers + [shifted_id(dx, dy) for dx, dy in AROUND if dx != 0]
    for target in targets:
        pl.semaphore_signal(barrier, inc=1, device_id=target, device_id_type=MESH)
    pl.semaphore_wait(barrier, len(targets))
    early, late = [], []
    for k, target in enumerate(peers):
        copy = pltpu.make_async_remote_copy(
            src_ref=ids_ref,
            dst_ref=all_ref.at[0, me],
            send_sem=ids_send.at[k],
            recv_sem=ids_recv.at[k],
            device_id=target,
            device_id_type=MESH,
        )
        copy.start()
        early.append(copy)
    for k, target in enumerate(peers):
        copy = pltpu.make_async_remote_copy(
            src_ref=tiles_ref.at[target["gy"]],
            dst_ref=arrived_ref.at[me],
            send_sem=tile_send.at[k],
            recv_sem=tile_recv.at[k],
            device_id=target,
            device_id_type=MESH,
        )
        copy.start()
        late.append(copy)
    for copy in halo_copies(phase_ref, ext_ref, 5, send_sem, recv_sem):
        copy.start()
        late.append(copy)
    own = [
        pltpu.make_async_copy(ids_ref, all_ref.at[0, me], own_sem.at[0]),
        pltpu.make_async_copy(
            phase_ref, ext_ref.at[pl.ds(5, BLOCK), pl.ds(SIDE, BLOCK)], own_sem.at[1]
        ),
        pltpu.make_async_copy(tiles_ref.at[me], arrived_ref.at[me], own_sem.at[2]),
    ]
    for copy in own:
        copy.start()
    own[0].wait()
    for copy in early:
        copy.wait()
    for n, step in enumerate((1, -1)):
        copy = pltpu.make_async_remote_copy(
            src_ref=all_ref.at[0],
            dst_ref=all_ref.at[1 + n],
            send_sem=ids_send.at[GROUPS - 1 + n],
            recv_sem=ids_recv.at[GROUPS - 1 + n],
            device_id=shifted_id(step, 0),
            device_id_type=MESH,
        )
        copy.start()
        late.append(copy)
    own[1].wait()
    own[2].wait()
    for copy in late:
        copy.wait()


def exchange_start(ids, phase, tiles):
    vmem = pl.BlockSpec(memory_space=pltpu.VMEM)
    dma = pltpu.SemaphoreType.DMA
    return pl.pallas_call(
        start_kernel,
        out_shape=(
            jax.ShapeDtypeStruct((3, GROUPS, 8, DEPTH), jnp.int32),
            jax.ShapeDtypeStruct((BLOCK + 10, BLOCK + 2 * SIDE, DEPTH), jnp.int32),
            jax.ShapeDtypeStruct((GROUPS, EDGE, EDGE, DEPTH), jnp.float32),
        ),
        in_specs=[vmem, vmem, vmem],
        out_specs=(vmem, vmem, vmem),
        scratch_shapes=[
            dma((8,)),
            dma((8,)),
            dma((GROUPS + 1,)),
            dma((GROUPS + 1,)),
            dma((GROUPS - 1,)),
            dma((GROUPS - 1,)),
            dma((3,)),
        ],
        compiler_params=pltpu.CompilerParams(
            collective_id=0, has_side_effects=True, vmem_limit_bytes=16 << 20
        ),
        name="start",
    )(ids, phase, tiles)


def halo_kernel(block_ref, ext_ref, send_sem, recv_sem, own_sem):
    barrier = pltpu.get_barrier_semaphore()
    for dx, dy in AROUND:
        pl.semaphore_signal(barrier, inc=1, device_id=shifted_id(dx, dy), device_id_type=MESH)
    pl.semaphore_wait(barrier, len(AROUND))
    copies = halo_copies(block_ref, ext_ref, 4, send_sem, recv_sem)
    for copy in copies:
        copy.start()
    own = pltpu.make_async_copy(
        block_ref, ext_ref.at[pl.ds(4, BLOCK), pl.ds(SIDE, BLOCK)], own_sem
    )
    own.start()
    own.wait()
    for copy in copies:
        copy.wait()


def exchange_halo(block):
    vmem = pl.BlockSpec(memory_space=pltpu.VMEM)
    return pl.pallas_call(
        halo_kernel,
        out_shape=jax.ShapeDtypeStruct((BLOCK + 8, BLOCK + 2 * SIDE, DEPTH), jnp.float32),
        in_specs=[vmem],
        out_specs=vmem,
        scratch_shapes=[
            pltpu.SemaphoreType.DMA((8,)),
            pltpu.SemaphoreType.DMA((8,)),
            pltpu.SemaphoreType.DMA,
        ],
        compiler_params=pltpu.CompilerParams(
            collective_id=1, has_side_effects=True, vmem_limit_bytes=8 << 20
        ),
        name="halo",
    )(block)


def table_kernel(me_ref, ids_ref, out_ref, row_of):
    me = me_ref[0]

    def place(e, carry):
        for band in range(3):
            row_of[band * 2 * COLS + ids_ref[band, e]] = band * 2 * COLS + e
        return carry

    lax.fori_loop(0, 2 * COLS, place, 0)
    for t in range(TILES):
        out_ref[T_PEER + t] = row_of[(t // 2) * COLS + me * 2 + t % 2] // TILES
    for s in range(TILES):
        own = ids_ref[0, me * TILES + s]
        row, col = own // COLS, lax.rem(own, COLS)
        left, right = lax.rem(col + COLS - 1, COLS), lax.rem(col + 1, COLS)
        low = jnp.where(row == 1, 0, 2 * COLS) + (1 - row) * COLS
        high = jnp.where(row == 0, 0, 4 * COLS) + (1 - row) * COLS
        out_ref[T_ROW + s] = row
        for n, place_of in enumerate((low + left, low + right, high + left, high + right)):
            out_ref[T_CORNER + n * TILES + s] = row_of[place_of]


def make_table(me, ids):
    smem = pl.BlockSpec(memory_space=pltpu.SMEM)
    return pl.pallas_call(
        table_kernel,
        out_shape=jax.ShapeDtypeStruct((T_SIZE,), jnp.int32),
        in_specs=[smem, smem],
        out_specs=smem,
        scratch_shapes=[pltpu.SMEM((6 * COLS,), jnp.int32)],
        name="table",
    )(me, ids)


K_FIRST, K_X2, K_X3, K_X4, K_Y2, K_Y3, K_Y4, K_LAST = range(8)
PERMS = 6
PORTS = 64


def to_column(row, eye):
    return jnp.sum(jnp.where(eye, row, 0), axis=1, keepdims=True)


def split_edges(left, right, sub, lane):
    def partners(ends):
        same = ends[0] == ends[1]
        before = jnp.where(same & (lane < sub), 1, 0)
        after = jnp.where(same & (sub < lane), 1, 0)
        rank_c = jnp.sum(before, axis=1, keepdims=True)
        rank_r = jnp.sum(after, axis=0, keepdims=True)
        pair = same & ((rank_c >> 1) == (rank_r >> 1)) & (sub != lane)
        return jnp.where(pair, 1.0, 0.0).astype(jnp.bfloat16)

    def times(a, b):
        return jnp.dot(a, b, preferred_element_type=jnp.float32)

    by_left, by_right = partners(left), partners(right)
    reach = jnp.where(sub == lane, 1.0, times(by_left, by_right)).astype(jnp.bfloat16)
    for _ in range(5):
        reach = jnp.where(times(reach, reach) > 0.0, 1.0, 0.0).astype(jnp.bfloat16)
    mate = times(by_left, reach)
    own = reach.astype(jnp.float32) > 0.0
    mate = mate > 0.0
    size = sub.shape[0]
    col = jnp.where(
        jnp.min(jnp.where(own, lane, size), axis=1, keepdims=True)
        > jnp.min(jnp.where(mate, lane, size), axis=1, keepdims=True),
        1,
        0,
    )
    row = jnp.where(
        jnp.min(jnp.where(own, sub, size), axis=0, keepdims=True)
        > jnp.min(jnp.where(mate, sub, size), axis=0, keepdims=True),
        1,
        0,
    )
    return col, row


def join(first, second, base):
    return tuple(a * base + b for a, b in zip(first, second))


def colour(left, right, sub, lane):
    high = split_edges(left, right, sub, lane)
    low = split_edges(join(left, high, 2), join(right, high, 2), sub, lane)
    return join(high, low, 2)


def routing_tables(me, ids, store):
    size = 2 * PORTS
    sub = lax.broadcasted_iota(jnp.int32, (size, size), 0)
    lane = lax.broadcasted_iota(jnp.int32, (size, size), 1)
    eye = sub == lane
    edge = (
        lax.broadcasted_iota(jnp.int32, (size, 1), 0),
        lax.broadcasted_iota(jnp.int32, (1, size), 1),
    )
    port = tuple(e & (PORTS - 1) for e in edge)
    half = tuple(e >> 6 for e in edge)
    device = tuple(e >> 2 for e in port)
    owner = (port[1] & 3) // 2 * COLS + device[1] * 2 + (port[1] & 1)
    own, below, above = (ids[n : n + 1] for n in range(3))

    def turn(pos, step):
        return (pos & COLS) + ((pos + step) & (COLS - 1))

    def both(first, second):
        return jnp.where(half[1] == 0, first, pltpu.roll(second, PORTS, 1))

    twice = both(own, own)
    at = to_column(twice, eye) + half[0] * PORTS
    my_row, my_col = me >> 2, me & 3
    entry = lax.broadcasted_iota(jnp.int32, (size, size), 1)
    for pair, target in enumerate(
        (
            both(owner, turn(own, 1)),
            both(turn(own, COLS - 1), own ^ COLS),
            both(below ^ COLS, above ^ COLS),
        )
    ):
        target = target + half[1] * PORTS
        drop = jnp.sum(jnp.where(at == target, sub & (PORTS - 1), 0), axis=0, keepdims=True)
        drop = (to_column(drop, eye), drop)
        goal = tuple(d >> 2 for d in drop)
        begin = tuple(h * GROUPS + d for h, d in zip(half, device))
        end = tuple(h * GROUPS + d for h, d in zip(half, goal))
        j = colour(begin, end, sub, lane)
        group = tuple(h * 4 + c for h, c in zip(half, j))
        src_row, src_col = (tuple(d >> 2 for d in device), tuple(d & 3 for d in device))
        dst_row, dst_col = (tuple(d >> 2 for d in goal), tuple(d & 3 for d in goal))
        b = colour(join(group, src_row, 4), join(group, dst_row, 4), sub, lane)
        g = colour(join(group, src_col, 4), join(group, dst_col, 4), sub, lane)
        for h in range(2):
            mine = half[0] == h
            for kind, given, key, value in (
                (K_FIRST, device[0] == me, j, port[0] & 3),
                (K_X2, (src_row[0] == my_row) & (j[0] == my_col), b, src_col[0]),
                (K_X3, (j[0] == my_col) & (b[0] == my_row), dst_row, src_row[0]),
                (K_X4, (j[0] == my_col) & (dst_row[0] == my_row), dst_col, b[0]),
                (K_Y2, (src_col[0] == my_col) & (j[0] == my_row), g, src_row[0]),
                (K_Y3, (j[0] == my_row) & (g[0] == my_col), dst_col, src_col[0]),
                (K_Y4, (j[0] == my_row) & (dst_col[0] == my_col), dst_row, g[0]),
                (K_LAST, goal[0] == me, (drop[0] & 3,), j[0]),
            ):
                kept = jnp.where(mine & given, value, 0)
                found = jnp.where(key[0] == entry, kept, 0)
                store((2 * pair + h) * 8 + kind, jnp.sum(found, axis=0, keepdims=True))


def routing_kernel(me_ref, ids_ref, out_ref):
    def store(place, row):
        out_ref[pl.ds(place, 1)] = row

    routing_tables(me_ref[0], ids_ref[...], store)


def make_routes(me, ids):
    vmem = pl.BlockSpec(memory_space=pltpu.VMEM)
    return pl.pallas_call(
        routing_kernel,
        out_shape=jax.ShapeDtypeStruct((8 * PERMS, DEPTH), jnp.int32),
        in_specs=[pl.BlockSpec(memory_space=pltpu.SMEM), vmem],
        out_specs=vmem,
        compiler_params=pltpu.CompilerParams(vmem_limit_bytes=8 << 20),
        name="routes",
    )(me, ids)


def ring(axis, step):
    gy = lax.axis_index("gy")
    row, col = gy // 4, lax.rem(gy, 4)
    if axis == 0:
        place = lax.rem(col + step, 4)
        return col, place, {"gx": lax.axis_index("gx"), "gy": row * 4 + place}
    place = lax.rem(row + step, 4)
    return row, place, {"gx": lax.axis_index("gx"), "gy": place * 4 + col}


RING_AXES = ((0, 1, 1, 0), (1, 0, 0, 1))
RING_KINDS = ((K_FIRST, K_X2, K_X3, K_X4), (K_FIRST, K_Y2, K_Y3, K_Y4))


def exchange(order, stage, perms, first, table_ref, before, bufs, sems, sent):
    send, recv = bufs
    send_sem, recv_sem = sems
    started = []
    for step in (2, 1, 3, 0):
        here, place, target = ring(RING_AXES[order][stage], step)
        for n, perm in enumerate(perms):
            slot = table_ref[perm * 8 + RING_KINDS[order][stage], place]
            value = before(order, first + n, slot)
            if step:
                send[step - 1, first + n] = value
            else:
                recv[here, first + n] = value
        if step:
            items = pl.ds(first, len(perms))
            copy = pltpu.make_async_remote_copy(
                src_ref=send.at[step - 1, items],
                dst_ref=recv.at[here, items],
                send_sem=send_sem.at[order, step - 1],
                recv_sem=recv_sem.at[order, step - 1],
                device_id=target,
                device_id_type=MESH,
            )
            copy.start()
            started.append(copy)
            sent.append(copy)
    return started


def greet(targets):
    barrier = pltpu.get_barrier_semaphore()
    for target in targets:
        pl.semaphore_signal(barrier, inc=1, device_id=target, device_id_type=MESH)
    pl.semaphore_wait(barrier, len(targets))


def back_kernel(table_ref, items_ref, outx_ref, outy_ref, *scratch):
    greet([ring(axis, step)[2] for axis in range(2) for step in (1, 2, 3)])
    buffers, semaphores = scratch[:16], scratch[16:]
    half = PACK // 2
    sent = []

    def first(order, n, slot):
        return items_ref[slot, order * half : (order + 1) * half]

    waiting = [None, None]
    for stage in range(4):
        sems = semaphores[2 * stage : 2 * stage + 2]
        for order in range(2):
            bufs = ring_buffers(buffers, stage, order)
            if stage:
                for copy in waiting[order]:
                    copy.wait_recv()
                before = reader(buffers, stage - 1)
            else:
                before = first
            waiting[order] = exchange(order, stage, (0,), 0, table_ref, before, bufs, sems, sent)
    for order, out in ((0, outx_ref), (1, outy_ref)):
        for copy in waiting[order]:
            copy.wait_recv()
        final = ring_buffers(buffers, 3, order)[1]
        for slot in range(4):
            out[slot] = final[slot, 0]
    for copy in sent:
        copy.wait_send()


def ring_scratch(items, shape):
    scratch = []
    for _ in range(8):
        scratch.append(pltpu.VMEM((3, items) + shape, jnp.float32))
        scratch.append(pltpu.VMEM((4, items) + shape, jnp.float32))
    return scratch


def ring_buffers(buffers, stage, order):
    place = 4 * stage + 2 * order
    return buffers[place : place + 2]


def reader(buffers, stage):
    def before(order, n, slot):
        return ring_buffers(buffers, stage, order)[1][slot, n]

    return before


def send_back(routes, packed):
    vmem = pl.BlockSpec(memory_space=pltpu.VMEM)
    half = (PACK // 2, EDGE, DEPTH)
    shape = jax.ShapeDtypeStruct((TILES,) + half, jnp.float32)
    return pl.pallas_call(
        back_kernel,
        out_shape=(shape, shape),
        in_specs=[pl.BlockSpec(memory_space=pltpu.SMEM), vmem],
        out_specs=(vmem, vmem),
        scratch_shapes=ring_scratch(1, half) + [pltpu.SemaphoreType.DMA((2, 3))] * 8,
        compiler_params=pltpu.CompilerParams(
            collective_id=2, has_side_effects=True, vmem_limit_bytes=32 << 20
        ),
        name="back",
    )(routes, packed)


FACES = 5


def faces_kernel(
    table_ref,
    faces_ref,
    corners_ref,
    outx_ref,
    outy_ref,
    all_ref,
    shifted,
    corner_send,
    corner_recv,
    shift_send,
    shift_recv,
    late_send,
    late_recv,
    own_sem,
    *scratch,
):
    me = lax.axis_index("gy")
    peers = [shifted_id(0, k) for k in range(1, GROUPS)]
    bands = [shifted_id(1, 0), shifted_id(-1, 0)]
    greet(peers + bands)
    buffers, semaphores = scratch[:16], scratch[16:]
    sent = []
    shifts = []
    for n, target in enumerate(bands):
        copy = pltpu.make_async_remote_copy(
            src_ref=faces_ref.at[:, 3 + n],
            dst_ref=shifted.at[n],
            send_sem=shift_send.at[n],
            recv_sem=shift_recv.at[n],
            device_id=target,
            device_id_type=MESH,
        )
        copy.start()
        shifts.append(copy)

    def first(order, n, slot):
        if n < 3:
            return faces_ref[slot, n, order * 3 : order * 3 + 3]
        return shifted[n - 3, slot, order * 3 : order * 3 + 3]

    waiting = [[], []]
    for order in range(2):
        waiting[order] += exchange(
            order, 0, (1, 2, 3), 0, table_ref, first, ring_buffers(buffers, 0, order), semaphores[:2], sent
        )
    spread_out = []
    for k, target in enumerate(peers):
        copy = pltpu.make_async_remote_copy(
            src_ref=corners_ref,
            dst_ref=all_ref.at[0, me],
            send_sem=corner_send.at[k],
            recv_sem=corner_recv.at[k],
            device_id=target,
            device_id_type=MESH,
        )
        copy.start()
        spread_out.append(copy)
    own = pltpu.make_async_copy(corners_ref, all_ref.at[0, me], own_sem)
    own.start()
    for copy in shifts:
        copy.wait_recv()
    late = (late_send, late_recv)
    for order in range(2):
        waiting[order] += exchange(
            order, 0, (4, 5), 3, table_ref, first, ring_buffers(buffers, 0, order), late, sent
        )
    forward = []
    for stage in range(1, 4):
        sems = semaphores[2 * stage : 2 * stage + 2]
        before = reader(buffers, stage - 1)
        for order in range(2):
            bufs = ring_buffers(buffers, stage, order)
            for copy in waiting[order]:
                copy.wait_recv()
            waiting[order] = exchange(
                order, stage, (1, 2, 3, 4, 5), 0, table_ref, before, bufs, sems, sent
            )
        if stage == 1:
            own.wait()
            for copy in spread_out:
                copy.wait_recv()
            for n, target in enumerate(bands):
                copy = pltpu.make_async_remote_copy(
                    src_ref=all_ref.at[0],
                    dst_ref=all_ref.at[1 + n],
                    send_sem=corner_send.at[GROUPS - 1 + n],
                    recv_sem=corner_recv.at[GROUPS - 1 + n],
                    device_id=target,
                    device_id_type=MESH,
                )
                copy.start()
                forward.append(copy)
    for order, out in ((0, outx_ref), (1, outy_ref)):
        for copy in waiting[order]:
            copy.wait_recv()
        final = ring_buffers(buffers, 3, order)[1]
        for slot in range(4):
            out[slot] = final[slot]
    for copy in forward:
        copy.wait_recv()
    for copy in shifts + spread_out + forward + sent:
        copy.wait_send()


def send_faces(routes, faces, corners):
    vmem = pl.BlockSpec(memory_space=pltpu.VMEM)
    f32 = jnp.float32
    dma = pltpu.SemaphoreType.DMA
    shape = jax.ShapeDtypeStruct((TILES, FACES, 3, EDGE, DEPTH), f32)
    return pl.pallas_call(
        faces_kernel,
        out_shape=(shape, shape, jax.ShapeDtypeStruct((3, GROUPS, 2, 8, DEPTH), f32)),
        in_specs=[pl.BlockSpec(memory_space=pltpu.SMEM), vmem, vmem],
        out_specs=(vmem, vmem, vmem),
        scratch_shapes=[
            pltpu.VMEM((2, TILES, 6, EDGE, DEPTH), f32),
            dma((GROUPS + 1,)),
            dma((GROUPS + 1,)),
            dma((2,)),
            dma((2,)),
            dma((2, 3)),
            dma((2, 3)),
            dma,
        ]
        + ring_scratch(FACES, (3, EDGE, DEPTH))
        + [dma((2, 3))] * 8,
        compiler_params=pltpu.CompilerParams(
            collective_id=3, has_side_effects=True, vmem_limit_bytes=24 << 20
        ),
        name="faces",
    )(routes, faces, corners)


def spread_kernel(ids_ref, charge_ref, mask_ref, out_ref, masked):
    def fill(s, carry):
        def rows(i, inner):
            flags = mask_ref[s, i + 1, pl.ds(1, EDGE), :].astype(jnp.float32)
            masked[s, i] = charge_ref[s, i] * flags
            return inner

        return lax.fori_loop(0, EDGE, rows, carry)

    lax.fori_loop(0, TILES, fill, 0)

    def send(p, carry):
        slot = 0
        for s in range(1, TILES):
            owner = lax.rem(ids_ref[s], COLS) // 2
            slot = jnp.where(owner == p, s, slot)
        out_ref[p] = masked[slot]
        return carry

    lax.fori_loop(0, GROUPS, send, 0)


def spread(tile_ids, charge, fluid_mask):
    vmem = pl.BlockSpec(memory_space=pltpu.VMEM)
    return pl.pallas_call(
        spread_kernel,
        out_shape=jax.ShapeDtypeStruct((GROUPS, EDGE, EDGE, DEPTH), jnp.float32),
        in_specs=[pl.BlockSpec(memory_space=pltpu.SMEM), vmem, vmem],
        out_specs=vmem,
        scratch_shapes=[pltpu.VMEM((TILES, EDGE, EDGE, DEPTH), jnp.float32)],
        compiler_params=pltpu.CompilerParams(vmem_limit_bytes=16 << 20),
        name="spread",
    )(tile_ids, charge, fluid_mask)


def assemble_kernel(table_ref, arrived_ref, out_ref):
    out_ref[...] = arrived_ref[0]


def assemble(table, arrived):
    return pl.pallas_call(
        assemble_kernel,
        out_shape=jax.ShapeDtypeStruct((BLOCK, BLOCK, DEPTH), jnp.float32),
        grid_spec=pltpu.PrefetchScalarGridSpec(
            num_scalar_prefetch=1,
            grid=(TILES,),
            in_specs=[
                pl.BlockSpec((1, EDGE, EDGE, DEPTH), lambda t, tab: (tab[T_PEER + t], 0, 0, 0))
            ],
            out_specs=pl.BlockSpec((EDGE, EDGE, DEPTH), lambda t, tab: (t // 2, t % 2, 0)),
        ),
        compiler_params=pltpu.CompilerParams(vmem_limit_bytes=8 << 20),
        name="assemble",
    )(table, arrived)


WIDE = BLOCK + 2 * SIDE
TALL = BLOCK + 8
ROOM = WIDE + 16
INNER = pl.ds(8, WIDE)
BEFORE = pl.ds(7, WIDE)
AFTER = pl.ds(9, WIDE)
PACK = 24


def harmonic(left, right):
    return 2.0 * left * right / (left + right)


def solve_kernel(
    permit_ref, phase_ref, source_ref, pot_ref, pack, permit, coef, resid, upd_a, upd_b, total
):
    center = 0.5 * (spectrum_high + spectrum_low)
    half = 0.5 * (spectrum_high - spectrum_low)
    ratio = center / half

    def look_up(i, carry):
        label = phase_ref[i]
        value = jnp.where(label == 0, permit_ref[0], 0.0)
        for k in range(1, PHASES):
            value = jnp.where(label == k, permit_ref[k], value)
        permit[i] = value
        return carry

    lax.fori_loop(0, TALL + 2, look_up, 0)

    def weigh(i, below):
        here = permit[i + 1]
        above = harmonic(here, permit[i + 2])
        right = harmonic(here, pltpu.roll(here, WIDE - 1, 0))
        left = pltpu.roll(right, 1, 0)
        up = harmonic(here, pltpu.roll(here, DEPTH - 1, 1))
        down = pltpu.roll(up, 1, 1)
        scale = 1.0 / (above + below + right + left + up + down + screening)
        for k, weight in enumerate((above, below, right, left, up, down)):
            coef[k, i] = weight * scale
        first = source_ref[i] * scale
        resid[i] = first
        first = first * (1.0 / center)
        upd_a[i, INNER] = first
        total[i] = first
        return above

    lax.fori_loop(0, TALL, weigh, harmonic(permit[0], permit[1]))

    rho = 1.0 / ratio
    old, new = upd_a, upd_b
    for sweep in range(3):
        rho_new = 1.0 / (2.0 * ratio - rho)
        keep, gain = rho_new * rho, 2.0 * rho_new / half

        def relax(i, carry, old=old, new=new, keep=keep, gain=gain):
            here = old[i, INNER]
            near = coef[0, i] * old[i + 1, INNER] + coef[1, i] * old[i - 1, INNER]
            near += coef[2, i] * old[i, AFTER] + coef[3, i] * old[i, BEFORE]
            near += coef[4, i] * pltpu.roll(here, DEPTH - 1, 1)
            near += coef[5, i] * pltpu.roll(here, 1, 1)
            left = resid[i] - here + near
            resid[i] = left
            here = keep * here + gain * left
            new[i, INNER] = here
            total[i] = total[i] + here
            return carry

        lax.fori_loop(sweep + 1, TALL - 1 - sweep, relax, 0)
        old, new = new, old
        rho = rho_new

    def emit(i, carry):
        pot_ref[i] = total[i + 4, pl.ds(SIDE, BLOCK)]
        return carry

    lax.fori_loop(0, BLOCK, emit, 0)
    for t in range(TILES):
        i0, j0 = 4 + (t // 2) * EDGE, SIDE + (t % 2) * EDGE

        def rows(i, carry, t=t, i0=i0, j0=j0):
            pack[t, i] = total[i0 + i, pl.ds(j0, EDGE)]
            for place, ref in ((EDGE + 2, total), (EDGE + 6, source_ref)):
                pack[t, place, pl.ds(i, 1)] = ref[i0 + i, pl.ds(j0 - 1, 1)]
                pack[t, place + 1, pl.ds(i, 1)] = ref[i0 + i, pl.ds(j0 + EDGE, 1)]
            return carry

        lax.fori_loop(0, EDGE, rows, 0)
        for place, ref in ((EDGE, total), (EDGE + 4, source_ref)):
            pack[t, place] = ref[i0 - 1, pl.ds(j0, EDGE)]
            pack[t, place + 1] = ref[i0 + EDGE, pl.ds(j0, EDGE)]


def solve(permittivity, phase, source):
    vmem = pl.BlockSpec(memory_space=pltpu.VMEM)
    smem = pl.BlockSpec(memory_space=pltpu.SMEM)
    f32 = jnp.float32
    return pl.pallas_call(
        solve_kernel,
        out_shape=(
            jax.ShapeDtypeStruct((BLOCK, BLOCK, DEPTH), f32),
            jax.ShapeDtypeStruct((TILES, PACK, EDGE, DEPTH), f32),
        ),
        in_specs=[smem, vmem, vmem],
        out_specs=(vmem, vmem),
        scratch_shapes=[
            pltpu.VMEM((TALL + 2, WIDE, DEPTH), f32),
            pltpu.VMEM((6, TALL, WIDE, DEPTH), f32),
            pltpu.VMEM((TALL, WIDE, DEPTH), f32),
            pltpu.VMEM((TALL, ROOM, DEPTH), f32),
            pltpu.VMEM((TALL, ROOM, DEPTH), f32),
            pltpu.VMEM((TALL, WIDE, DEPTH), f32),
        ],
        compiler_params=pltpu.CompilerParams(vmem_limit_bytes=32 << 20),
        name="solve",
    )(permittivity, phase, source)


def collide_rows(pops, charge, field):
    force = [charge * component for component in field]
    sums = {}
    diffs = {}
    for a, b in PAIRS:
        sums[a] = pops[a] + pops[b]
        diffs[a] = pops[a] - pops[b]
    density = pops[0]
    for a, _ in PAIRS:
        density = density + sums[a]
    momentum = [
        diffs[1] + diffs[7] + diffs[9] + diffs[11] + diffs[13],
        diffs[3] + diffs[7] - diffs[9] + diffs[15] + diffs[17],
        diffs[5] + diffs[11] - diffs[13] + diffs[15] - diffs[17],
    ]
    inverse = 1.0 / density
    velocity = [(momentum[d] + 0.5 * force[d]) * inverse for d in range(3)]
    scale = 1.0 - 0.5 / relax_time
    rate = 1.0 / relax_time
    speed = velocity[0] * velocity[0] + velocity[1] * velocity[1] + velocity[2] * velocity[2]
    work = velocity[0] * force[0] + velocity[1] * force[1] + velocity[2] * force[2]
    weighted = rate * density
    base = weighted - (1.5 * weighted) * speed - (3.0 * scale) * work
    odd = [3.0 * weighted * velocity[d] + (3.0 * scale) * force[d] for d in range(3)]
    inner = [4.5 * weighted * velocity[d] + (9.0 * scale) * force[d] for d in range(3)]
    keep = 1.0 - rate
    result = [None] * 19
    result[0] = keep * pops[0] + WEIGHTS[0] * base
    for a, b in PAIRS:
        step = LATTICE[a]
        axes = [d for d in range(3) if step[d] != 0]
        if len(axes) == 1:
            (d,) = axes
            cu, co, ci = velocity[d], odd[d], inner[d]
            weight = WEIGHTS[1]
        else:
            d, e = axes
            weight = WEIGHTS[2]
            if step[d] * step[e] > 0:
                cu, co, ci = velocity[d] + velocity[e], odd[d] + odd[e], inner[d] + inner[e]
            else:
                cu, co, ci = velocity[d] - velocity[e], odd[d] - odd[e], inner[d] - inner[e]
        even = weight * (base + cu * ci)
        lean = weight * co
        result[a] = keep * pops[a] + (even + lean)
        result[b] = keep * pops[b] + (even - lean)
    return result, velocity


def collide_kernel(
    table_ref, routes_ref, pops_ref, charge_ref, mask_ref, potx_ref, poty_ref, out_ref, vel_ref, face_ref, corner_ref, grown
):
    half = PACK // 2
    tile = pl.program_id(0)

    for ref, first, count in ((potx_ref, 0, half), (poty_ref, half, EDGE - half)):

        def place(i, carry, ref=ref, first=first):
            grown[first + i + 1, pl.ds(8, EDGE)] = ref[0, i]
            return carry

        lax.fori_loop(0, count, place, 0)

    def sides(i, carry):
        grown[i + 1, pl.ds(7, 1)] = poty_ref[0, EDGE + 2 - half, pl.ds(i, 1)]
        grown[i + 1, pl.ds(8 + EDGE, 1)] = poty_ref[0, EDGE + 3 - half, pl.ds(i, 1)]
        return carry

    lax.fori_loop(0, EDGE, sides, 0)
    grown[0, pl.ds(8, EDGE)] = poty_ref[0, EDGE - half]
    grown[EDGE + 1, pl.ds(8, EDGE)] = poty_ref[0, EDGE + 1 - half]
    y_low, y_high = crossing(1, -1), crossing(1, 1)

    def rows(i, carry):
        here = grown[i + 1, pl.ds(8, EDGE)]
        field = [
            0.5 * (grown[i, pl.ds(8, EDGE)] - grown[i + 2, pl.ds(8, EDGE)]),
            0.5 * (grown[i + 1, pl.ds(7, EDGE)] - grown[i + 1, pl.ds(9, EDGE)]),
            0.5 * (pltpu.roll(here, 1, 1) - pltpu.roll(here, DEPTH - 1, 1)),
        ]
        pops = [pops_ref[q, 0, i] for q in range(19)]
        relaxed, velocity = collide_rows(pops, charge_ref[0, i], field)
        fluid = mask_ref[0, i + 1, pl.ds(1, EDGE), :] == 1
        for q in range(19):
            value = jnp.where(fluid, relaxed[q], pops[q])
            out_ref[q, 0, i] = value
            if q in y_low:
                face_ref[0, 1, y_low.index(q), pl.ds(i, 1)] = value[0:1]
            if q in y_high:
                face_ref[0, 0, y_high.index(q), pl.ds(i, 1)] = value[EDGE - 1 :]
        for d in range(3):
            vel_ref[d, 0, i] = velocity[d]
        face_ref[0, 1, 5, pl.ds(i, 1)] = velocity[1][0:1]
        face_ref[0, 0, 5, pl.ds(i, 1)] = velocity[1][EDGE - 1 :]
        return carry

    lax.fori_loop(0, EDGE, rows, 0)

    def x_face(face, sign, layer):
        for k, q in enumerate(crossing(0, sign)):
            face_ref[0, face, k] = out_ref[q, 0, layer]
        face_ref[0, face, 5] = vel_ref[0, 0, layer]

    x_face(3, 1, EDGE - 1)
    x_face(4, -1, 0)

    @pl.when(table_ref[T_ROW + tile] == 0)
    def _():
        x_face(2, 1, EDGE - 1)

    @pl.when(table_ref[T_ROW + tile] == 1)
    def _():
        x_face(2, -1, 0)

    for n, (q, i, j) in enumerate(
        ((7, EDGE - 1, EDGE - 1), (9, EDGE - 1, 0), (10, 0, EDGE - 1), (8, 0, 0))
    ):
        corner_ref[tile // 2, pl.ds(lax.rem(tile, 2) * 4 + n, 1)] = out_ref[q, 0, i, pl.ds(j, 1)]


def collide(table, routes, populations, charge, fluid_mask, potx, poty):
    f32 = jnp.float32
    pot_spec = pl.BlockSpec(
        (1, PACK // 2, EDGE, DEPTH), lambda s, tab, rts: (rts[K_LAST, s], 0, 0, 0)
    )
    return pl.pallas_call(
        collide_kernel,
        out_shape=(
            jax.ShapeDtypeStruct((19, TILES, EDGE, EDGE, DEPTH), f32),
            jax.ShapeDtypeStruct((3, TILES, EDGE, EDGE, DEPTH), f32),
            jax.ShapeDtypeStruct((TILES, FACES, 6, EDGE, DEPTH), f32),
            jax.ShapeDtypeStruct((2, 8, DEPTH), f32),
        ),
        grid_spec=pltpu.PrefetchScalarGridSpec(
            num_scalar_prefetch=2,
            grid=(TILES,),
            in_specs=[
                pl.BlockSpec((19, 1, EDGE, EDGE, DEPTH), lambda s, tab, rts: (0, s, 0, 0, 0)),
                pl.BlockSpec((1, EDGE, EDGE, DEPTH), lambda s, tab, rts: (s, 0, 0, 0)),
                pl.BlockSpec((1, EDGE + 2, EDGE + 2, DEPTH), lambda s, tab, rts: (s, 0, 0, 0)),
                pot_spec,
                pot_spec,
            ],
            out_specs=[
                pl.BlockSpec((19, 1, EDGE, EDGE, DEPTH), lambda s, tab, rts: (0, s, 0, 0, 0)),
                pl.BlockSpec((3, 1, EDGE, EDGE, DEPTH), lambda s, tab, rts: (0, s, 0, 0, 0)),
                pl.BlockSpec((1, FACES, 6, EDGE, DEPTH), lambda s, tab, rts: (s, 0, 0, 0, 0)),
                pl.BlockSpec((2, 8, DEPTH), lambda s, tab, rts: (0, 0, 0)),
            ],
            scratch_shapes=[pltpu.VMEM((EDGE + 2, 32, DEPTH), f32)],
        ),
        compiler_params=pltpu.CompilerParams(vmem_limit_bytes=32 << 20),
        name="collide",
    )(table, routes, populations, charge, fluid_mask, potx, poty)


def stream_kernel(
    table_ref,
    routes_ref,
    relaxed_ref,
    vel_ref,
    charge_ref,
    mask_ref,
    rim_ref,
    *rest,
):
    halves, (corner_ref, pops_out, charge_out, xrim, yrim, corner) = rest[:10], rest[10:]
    tile = pl.program_id(0)
    row = table_ref[T_ROW + tile]
    plus = [crossing(0, 1), crossing(1, 1)]
    minus = [crossing(0, -1), crossing(1, -1)]

    def fill(out, face):
        for k in range(6):
            out[k] = halves[2 * face + k // 3][0, 0, k % 3]

    fill(yrim.at[0], 0)
    fill(yrim.at[1], 1)
    for n, (side, end, which) in enumerate(((0, 0, 0), (0, 1, 1), (1, 0, 2), (1, 1, 3))):
        found = table_ref[T_CORNER + n * TILES + tile]
        tile_in = lax.rem(found, TILES)
        corner[side, pl.ds(end, 1)] = corner_ref[
            found // TILES, tile_in // 2, pl.ds(lax.rem(tile_in, 2) * 4 + which, 1)
        ]

    @pl.when(row == 0)
    def _():
        fill(xrim.at[0], 3)
        fill(xrim.at[1], 2)

    @pl.when(row == 1)
    def _():
        fill(xrim.at[0], 2)
        fill(xrim.at[1], 4)

    place = lax.broadcasted_iota(jnp.int32, (EDGE, DEPTH), 0)
    first, last = place == 0, place == EDGE - 1

    def rows(i, low_edge, high_edge):
        own = mask_ref[0, i + 1, pl.ds(1, EDGE), :]
        own_fluid = own == 1
        for q in range(19):
            step_x, step_y, step_z = LATTICE[q]
            value_here = relaxed_ref[q, 0, i]
            if q == 0:
                pops_out[q, 0, i] = value_here
                continue
            side = None
            if step_x == 1 and low_edge:
                side, channel = 0, plus[0].index(q)
            if step_x == -1 and high_edge:
                side, channel = 1, minus[0].index(q)
            if side is None:
                moved = value_here if step_x == 0 else relaxed_ref[q, 0, i - step_x]
            else:
                moved = xrim[side, channel]
            if step_y == 1:
                if side is None:
                    edge = yrim[0, plus[1].index(q), pl.ds(i - step_x, 1)]
                else:
                    edge = corner[side, pl.ds(0, 1)]
                moved = jnp.where(first, edge, pltpu.roll(moved, 1, 0))
            elif step_y == -1:
                if side is None:
                    edge = yrim[1, minus[1].index(q), pl.ds(i - step_x, 1)]
                else:
                    edge = corner[side, pl.ds(1, 1)]
                moved = jnp.where(last, edge, pltpu.roll(moved, EDGE - 1, 0))
            from_fluid = mask_ref[0, i + 1 - step_x, pl.ds(1 - step_y, EDGE), :]
            if step_z != 0:
                moved = pltpu.roll(moved, step_z % DEPTH, 1)
                from_fluid = pltpu.roll(from_fluid, step_z % DEPTH, 1)
            bounced = relaxed_ref[opposite(q), 0, i]
            read = jnp.where(from_fluid == 1, moved, bounced)
            pops_out[q, 0, i] = jnp.where(own_fluid, read, value_here)

        charge = charge_ref[0, i]
        flag = own.astype(jnp.float32)

        def flux(speed_a, speed_b, value_a, value_b, flags):
            speed = 0.5 * (speed_a + speed_b)
            return speed * jnp.where(speed > 0, value_a, value_b) * flags

        speed = vel_ref[0, 0, i]
        if low_edge:
            other, other_speed = rim_ref[0, 0], xrim[0, 5]
        else:
            other, other_speed = charge_ref[0, i - 1], vel_ref[0, 0, i - 1]
        other_flag = mask_ref[0, i, pl.ds(1, EDGE), :].astype(jnp.float32)
        change = -flux(other_speed, speed, other, charge, other_flag * flag)
        if high_edge:
            other, other_speed = rim_ref[0, 1], xrim[1, 5]
        else:
            other, other_speed = charge_ref[0, i + 1], vel_ref[0, 0, i + 1]
        other_flag = mask_ref[0, i + 2, pl.ds(1, EDGE), :].astype(jnp.float32)
        change += flux(speed, other_speed, charge, other, flag * other_flag)

        speed = vel_ref[1, 0, i]
        other = jnp.where(first, rim_ref[0, 2, pl.ds(i, 1)], pltpu.roll(charge, 1, 0))
        other_speed = jnp.where(first, yrim[0, 5, pl.ds(i, 1)], pltpu.roll(speed, 1, 0))
        other_flag = mask_ref[0, i + 1, pl.ds(0, EDGE), :].astype(jnp.float32)
        change -= flux(other_speed, speed, other, charge, other_flag * flag)
        other = jnp.where(last, rim_ref[0, 3, pl.ds(i, 1)], pltpu.roll(charge, EDGE - 1, 0))
        other_speed = jnp.where(
            last, yrim[1, 5, pl.ds(i, 1)], pltpu.roll(speed, EDGE - 1, 0)
        )
        other_flag = mask_ref[0, i + 1, pl.ds(2, EDGE), :].astype(jnp.float32)
        change += flux(speed, other_speed, charge, other, flag * other_flag)

        speed = vel_ref[2, 0, i]
        over = flux(
            speed,
            pltpu.roll(speed, DEPTH - 1, 1),
            charge,
            pltpu.roll(charge, DEPTH - 1, 1),
            flag * pltpu.roll(flag, DEPTH - 1, 1),
        )
        change += over - pltpu.roll(over, 1, 1)
        charge_out[0, i] = jnp.where(own_fluid, charge - change, charge)

    rows(0, True, False)

    def middle(i, carry):
        rows(i, False, False)
        return carry

    lax.fori_loop(1, EDGE - 1, middle, 0)
    rows(EDGE - 1, False, True)


def stream(table, routes, relaxed, velocity, charge, fluid_mask, poty, facex, facey, corners):
    f32 = jnp.float32
    face_specs = [
        pl.BlockSpec(
            (1, 1, 3, EDGE, DEPTH),
            lambda s, tab, rts, face=face: (rts[(1 + face) * 8 + K_LAST, s], face, 0, 0, 0),
        )
        for face in range(FACES)
        for _ in range(2)
    ]
    return pl.pallas_call(
        stream_kernel,
        out_shape=(
            jax.ShapeDtypeStruct((19, TILES, EDGE, EDGE, DEPTH), f32),
            jax.ShapeDtypeStruct((TILES, EDGE, EDGE, DEPTH), f32),
        ),
        grid_spec=pltpu.PrefetchScalarGridSpec(
            num_scalar_prefetch=2,
            grid=(TILES,),
            in_specs=[
                pl.BlockSpec((19, 1, EDGE, EDGE, DEPTH), lambda s, tab, rts: (0, s, 0, 0, 0)),
                pl.BlockSpec((3, 1, EDGE, EDGE, DEPTH), lambda s, tab, rts: (0, s, 0, 0, 0)),
                pl.BlockSpec((1, EDGE, EDGE, DEPTH), lambda s, tab, rts: (s, 0, 0, 0)),
                pl.BlockSpec((1, EDGE + 2, EDGE + 2, DEPTH), lambda s, tab, rts: (s, 0, 0, 0)),
                pl.BlockSpec((1, 4, EDGE, DEPTH), lambda s, tab, rts: (rts[K_LAST, s], 2, 0, 0)),
            ]
            + face_specs
            + [pl.BlockSpec((3 * GROUPS, 2, 8, DEPTH), lambda s, tab, rts: (0, 0, 0, 0))],
            out_specs=[
                pl.BlockSpec((19, 1, EDGE, EDGE, DEPTH), lambda s, tab, rts: (0, s, 0, 0, 0)),
                pl.BlockSpec((1, EDGE, EDGE, DEPTH), lambda s, tab, rts: (s, 0, 0, 0)),
            ],
            scratch_shapes=[
                pltpu.VMEM((2, 6, EDGE, DEPTH), f32),
                pltpu.VMEM((2, 6, EDGE, DEPTH), f32),
                pltpu.VMEM((2, 8, DEPTH), f32),
            ],
        ),
        compiler_params=pltpu.CompilerParams(vmem_limit_bytes=32 << 20),
        name="stream",
    )(
        table,
        routes,
        relaxed,
        velocity,
        charge,
        fluid_mask,
        poty,
        *([facex, facey] * FACES),
        corners.reshape(3 * GROUPS, 2, 8, DEPTH),
    )


def per_device(populations, charge, fluid_mask, tile_ids, phase_label, permittivity):
    outgoing = spread(tile_ids, charge, fluid_mask)
    me = lax.axis_index("gy").astype(jnp.int32).reshape(1)
    place = jnp.arange(8 * DEPTH, dtype=jnp.int32).reshape(8, DEPTH)
    ids_row = jnp.where(place // TILES == me, jnp.tile(tile_ids, 2 * DEPTH).reshape(8, DEPTH), 0)
    ids_all, phase_ext, arrived = exchange_start(ids_row, phase_label, outgoing)
    ids = jnp.sum(ids_all[:, :, 0, :], axis=1)
    table = make_table(me, ids)
    routes = make_routes(me, ids)
    source_ext = exchange_halo(assemble(table, arrived))
    potential, packed = solve(permittivity, phase_ext, source_ext)
    potx, poty = send_back(routes, packed)
    relaxed, velocity, faces, corners = collide(
        table, routes, populations, charge, fluid_mask, potx, poty
    )
    facex, facey, all_corners = send_faces(routes, faces, corners)
    populations_next, charge_next = stream(
        table, routes, relaxed, velocity, charge, fluid_mask, poty, facex, facey, all_corners
    )
    return (populations_next, charge_next, potential)


def solution(mesh):
    placed = (
        P(None, ("gx", "gy"), None, None, None),
        P(("gx", "gy"), None, None, None),
        P(("gx", "gy"), None, None, None),
        P(("gx", "gy")),
        P("gx", "gy", None),
        P(),
    )
    return jax.shard_map(
        per_device,
        mesh=mesh,
        in_specs=placed,
        out_specs=(
            P(None, ("gx", "gy"), None, None, None),
            P(("gx", "gy"), None, None, None),
            P("gx", "gy", None),
        ),
        check_vma=False,
    )
```

```python
import functools

import jax
import jax.numpy as jnp
from jax import lax
from jax.experimental import pallas as pl
from jax.experimental.pallas import tpu as pltpu
from jax.sharding import PartitionSpec as P

EDGE = 16
DEPTH = 128
BLOCK = 32
PHASES = 4
TILES = 4
GROUPS = 16
BANDS = 8
COLS = 32
SIDE = 8
MESH = pl.DeviceIdType.MESH

LATTICE = (
    (0, 0, 0),
    (1, 0, 0),
    (-1, 0, 0),
    (0, 1, 0),
    (0, -1, 0),
    (0, 0, 1),
    (0, 0, -1),
    (1, 1, 0),
    (-1, -1, 0),
    (1, -1, 0),
    (-1, 1, 0),
    (1, 0, 1),
    (-1, 0, -1),
    (1, 0, -1),
    (-1, 0, 1),
    (0, 1, 1),
    (0, -1, -1),
    (0, 1, -1),
    (0, -1, 1),
)
WEIGHTS = (1.0 / 3.0, 1.0 / 18.0, 1.0 / 36.0)
PAIRS = ((1, 2), (3, 4), (5, 6), (7, 8), (9, 10), (11, 12), (13, 14), (15, 16), (17, 18))
relax_time = 0.8
screening = 0.001
spectrum_low = 0.1
spectrum_high = 2.0

AROUND = tuple((dx, dy) for dx in (-1, 0, 1) for dy in (-1, 0, 1) if (dx, dy) != (0, 0))

TO_OWNER, TO_HOLDER = 0, 1
UP_Y, DOWN_Y, SAME_X, BELOW_X, ABOVE_X = range(5)
R_ROW, R_CORNER = 40, 41


def opposite(direction):
    return LATTICE.index(tuple(-entry for entry in LATTICE[direction]))


def crossing(axis_index, face_sign):
    return [d for d in range(19) if LATTICE[d][axis_index] == face_sign]


def shifted_id(dx, dy):
    gx = lax.rem(lax.axis_index("gx") + dx + BANDS, BANDS)
    gy = lax.rem(lax.axis_index("gy") + dy + GROUPS, GROUPS)
    return {"gx": gx, "gy": gy}


def span(step, width, pad):
    if step == 0:
        return pl.ds(0, BLOCK), pl.ds(pad, BLOCK)
    if step > 0:
        return pl.ds(BLOCK - width, width), pl.ds(pad - width, width)
    return pl.ds(0, width), pl.ds(pad + BLOCK, width)


def halo_copies(block_ref, ext_ref, width, send_sem, recv_sem):
    copies = []
    for n, (dx, dy) in enumerate(AROUND):
        src_i, dst_i = span(dx, width, width)
        src_j, dst_j = span(dy, SIDE, SIDE)
        copies.append(
            pltpu.make_async_remote_copy(
                src_ref=block_ref.at[src_i, src_j],
                dst_ref=ext_ref.at[dst_i, dst_j],
                send_sem=send_sem.at[n],
                recv_sem=recv_sem.at[n],
                device_id=shifted_id(dx, dy),
                device_id_type=MESH,
            )
        )
    return copies


def greet(targets):
    barrier = pltpu.get_barrier_semaphore()
    for target in targets:
        pl.semaphore_signal(barrier, inc=1, device_id=target, device_id_type=MESH)
    pl.semaphore_wait(barrier, len(targets))


def start_kernel(
    ids_ref, phase_ref, all_ref, ext_ref, send_sem, recv_sem, ids_send, ids_recv, own_sem
):
    me = lax.axis_index("gy")
    peers = [shifted_id(0, k) for k in range(1, GROUPS)]
    greet(peers + [shifted_id(dx, dy) for dx, dy in AROUND if dx != 0])
    started = []
    for k, target in enumerate(peers):
        copy = pltpu.make_async_remote_copy(
            src_ref=ids_ref,
            dst_ref=all_ref.at[me],
            send_sem=ids_send.at[k],
            recv_sem=ids_recv.at[k],
            device_id=target,
            device_id_type=MESH,
        )
        copy.start()
        started.append(copy)
    for copy in halo_copies(phase_ref, ext_ref, 5, send_sem, recv_sem):
        copy.start()
        started.append(copy)
    own = [
        pltpu.make_async_copy(ids_ref, all_ref.at[me], own_sem.at[0]),
        pltpu.make_async_copy(
            phase_ref, ext_ref.at[pl.ds(5, BLOCK), pl.ds(SIDE, BLOCK)], own_sem.at[1]
        ),
    ]
    for copy in own:
        copy.start()
    for copy in own + started:
        copy.wait()


def exchange_start(ids, phase):
    vmem = pl.BlockSpec(memory_space=pltpu.VMEM)
    dma = pltpu.SemaphoreType.DMA
    return pl.pallas_call(
        start_kernel,
        out_shape=(
            jax.ShapeDtypeStruct((GROUPS, 8, DEPTH), jnp.int32),
            jax.ShapeDtypeStruct((BLOCK + 10, BLOCK + 2 * SIDE, DEPTH), jnp.int32),
        ),
        in_specs=[vmem, vmem],
        out_specs=(vmem, vmem),
        scratch_shapes=[
            dma((8,)),
            dma((8,)),
            dma((GROUPS - 1,)),
            dma((GROUPS - 1,)),
            dma((2,)),
        ],
        compiler_params=pltpu.CompilerParams(
            collective_id=0, has_side_effects=True, vmem_limit_bytes=8 << 20
        ),
        name="start",
    )(ids, phase)


WIDE = BLOCK + 2 * SIDE
TALL = BLOCK + 8
ROOM = WIDE + 16
INNER = pl.ds(8, WIDE)
BEFORE = pl.ds(7, WIDE)
AFTER = pl.ds(9, WIDE)
PACK = 24


def harmonic(left, right):
    return 2.0 * left * right / (left + right)


def look_up_rows(permit_ref, phase_ref, permit):
    def look_up(i, carry):
        label = phase_ref[i]
        value = jnp.where(label == 0, permit_ref[0], 0.0)
        for k in range(1, PHASES):
            value = jnp.where(label == k, permit_ref[k], value)
        permit[i] = value
        return carry

    lax.fori_loop(0, TALL + 2, look_up, 0)


def weigh_rows(begin, end, permit, coef, scale_ref):
    def weigh(i, below):
        here = permit[i + 1]
        above = harmonic(here, permit[i + 2])
        right = harmonic(here, pltpu.roll(here, WIDE - 1, 0))
        left = pltpu.roll(right, 1, 0)
        up = harmonic(here, pltpu.roll(here, DEPTH - 1, 1))
        down = pltpu.roll(up, 1, 1)
        scale = 1.0 / (above + below + right + left + up + down + screening)
        for k, weight in enumerate((above, below, right, left, up, down)):
            coef[k, i] = weight * scale
        scale_ref[i] = scale
        return above

    lax.fori_loop(begin, end, weigh, harmonic(permit[begin], permit[begin + 1]))


K_FIRST, K_X2, K_X3, K_X4, K_Y2, K_Y3, K_Y4, K_LAST = range(8)
PORTS = 64


def to_column(row, eye):
    return jnp.sum(jnp.where(eye, row, 0), axis=1, keepdims=True)


def split_edges(left, right, sub, lane, doublings):
    def partners(ends):
        same = ends[0] == ends[1]
        before = jnp.where(same & (lane < sub), 1, 0)
        after = jnp.where(same & (sub < lane), 1, 0)
        rank_c = jnp.sum(before, axis=1, keepdims=True)
        rank_r = jnp.sum(after, axis=0, keepdims=True)
        pair = same & ((rank_c >> 1) == (rank_r >> 1)) & (sub != lane)
        return jnp.where(pair, 1.0, 0.0).astype(jnp.bfloat16)

    def times(a, b):
        return jnp.dot(a, b, preferred_element_type=jnp.float32)

    by_left, by_right = partners(left), partners(right)
    reach = times(by_left, by_right) + times(by_right, by_left)
    reach = jnp.where((sub == lane) | (reach > 0.0), 1.0, 0.0).astype(jnp.bfloat16)
    for _ in range(doublings):
        reach = jnp.where(times(reach, reach) > 0.0, 1.0, 0.0).astype(jnp.bfloat16)
    mate = times(by_left, reach) > 0.0
    own = reach.astype(jnp.float32) > 0.0
    size = sub.shape[0]
    col = jnp.where(
        jnp.min(jnp.where(own, lane, size), axis=1, keepdims=True)
        > jnp.min(jnp.where(mate, lane, size), axis=1, keepdims=True),
        1,
        0,
    )
    row = jnp.where(
        jnp.min(jnp.where(own, sub, size), axis=0, keepdims=True)
        > jnp.min(jnp.where(mate, sub, size), axis=0, keepdims=True),
        1,
        0,
    )
    return col, row


def join(first, second, base):
    return tuple(a * base + b for a, b in zip(first, second))


def colour(left, right, sub, lane, doublings):
    high = split_edges(left, right, sub, lane, doublings)
    low = split_edges(join(left, high, 2), join(right, high, 2), sub, lane, doublings - 1)
    return join(high, low, 2)


class Ports:
    def __init__(self, size):
        self.size = size
        self.sub = lax.broadcasted_iota(jnp.int32, (size, size), 0)
        self.lane = lax.broadcasted_iota(jnp.int32, (size, size), 1)
        self.eye = self.sub == self.lane
        edge = (
            lax.broadcasted_iota(jnp.int32, (size, 1), 0),
            lax.broadcasted_iota(jnp.int32, (1, size), 1),
        )
        self.port = tuple(e & (PORTS - 1) for e in edge)
        self.half = tuple(e >> 6 for e in edge)
        self.device = tuple(e >> 2 for e in self.port)
        self.entry = lax.broadcasted_iota(jnp.int32, (size, DEPTH), 1)


def store_routes(me, ports, places, goal_ids, target, store):
    half, port, device = ports.half, ports.port, ports.device
    sub, lane = ports.sub, ports.lane
    my_row, my_col = me >> 2, me & 3
    at = to_column(goal_ids, ports.eye) + half[0] * PORTS
    target = target + half[1] * PORTS
    drop = jnp.sum(jnp.where(at == target, sub & (PORTS - 1), 0), axis=0, keepdims=True)
    drop = (to_column(drop, ports.eye), drop)
    goal = tuple(d >> 2 for d in drop)
    begin = tuple(h * GROUPS + d for h, d in zip(half, device))
    end = tuple(h * GROUPS + d for h, d in zip(half, goal))
    j = colour(begin, end, sub, lane, 4)
    group = tuple(h * 4 + c for h, c in zip(half, j))
    rows = (tuple(d >> 2 for d in device), tuple(d >> 2 for d in goal))
    cols = (tuple(d & 3 for d in device), tuple(d & 3 for d in goal))
    b = colour(join(group, rows[0], 4), join(group, rows[1], 4), sub, lane, 2)[0]
    g = colour(join(group, cols[0], 4), join(group, cols[1], 4), sub, lane, 2)[0]
    j = j[0]
    slots = (port[0] & 3, drop[0] & 3)
    ends = (device[0], goal[0])
    rows, cols = tuple(r[0] for r in rows), tuple(c[0] for c in cols)
    for perm, h, back in places:
        mine = half[0] == h
        src, dst = (1, 0) if back else (0, 1)
        for kind, given, key, value in (
            (K_FIRST, ends[src] == me, j, slots[src]),
            (K_X2, (rows[src] == my_row) & (j == my_col), b, cols[src]),
            (K_X3, (j == my_col) & (b == my_row), rows[dst], rows[src]),
            (K_X4, (j == my_col) & (rows[dst] == my_row), cols[dst], b),
            (K_Y2, (cols[src] == my_col) & (j == my_row), g, rows[src]),
            (K_Y3, (j == my_row) & (g == my_col), cols[dst], cols[src]),
            (K_Y4, (j == my_row) & (cols[dst] == my_col), rows[dst], g),
            (K_LAST, ends[dst] == me, slots[dst], j),
        ):
            kept = jnp.where(mine & given, value, 0)
            found = jnp.where(key == ports.entry, kept, 0)
            store(perm * 8 + kind, jnp.sum(found, axis=0, keepdims=True))


def owner_tables(me, own, store):
    ports = Ports(PORTS)
    owner = (ports.port[1] & 3) // 2 * COLS + ports.device[1] * 2 + (ports.port[1] & 1)
    places = ((TO_OWNER, 0, True), (TO_HOLDER, 0, False))
    store_routes(me, ports, places, own[:, :PORTS], owner, store)


def face_tables(me, own, below, above, store):
    ports = Ports(2 * PORTS)
    half = ports.half

    def turn(pos, step):
        return (pos & COLS) + ((pos + step) & (COLS - 1))

    def both(first, second):
        return jnp.where(half[1] == 0, first, pltpu.roll(second, PORTS, 1))

    twice = both(own, own)
    places = ((UP_Y, 0, False), (DOWN_Y, 0, True), (SAME_X, 1, False))
    store_routes(me, ports, places, twice, both(turn(own, 1), own ^ COLS), store)
    yield
    places = ((BELOW_X, 0, False), (ABOVE_X, 1, False))
    store_routes(me, ports, places, twice, both(below ^ COLS, above ^ COLS), store)
    yield
    mine = jnp.sum(
        jnp.where((ports.sub == me * TILES + ports.lane) & (ports.lane < TILES), to_column(own, ports.eye), 0),
        axis=0,
        keepdims=True,
    )
    store(R_ROW, mine >> 5)
    found = []
    for band in (own, below, above):
        at = to_column(band, ports.eye)
        for step in (-1, 1):
            there = (at == turn(mine ^ COLS, step)) & (ports.sub < PORTS)
            found.append(jnp.sum(jnp.where(there, ports.sub, 0), axis=0, keepdims=True))
    upper = (mine >> 5) == 1
    for n in range(2):
        store(R_CORNER + n, jnp.where(upper, found[n], found[2 + n] + PORTS))
        store(R_CORNER + 2 + n, jnp.where(upper, found[4 + n] + 2 * PORTS, found[n]))


def gathered_ids(ids):
    return jnp.sum(ids, axis=0)[0:1]


def owner_routes_kernel(me_ref, ids_ref, out_ref):
    def store(place, row):
        out_ref[pl.ds(place, 1)] = row

    owner_tables(me_ref[0], gathered_ids(ids_ref[...]), store)


def make_routes(kernel, rows, me, *ids):
    vmem = pl.BlockSpec(memory_space=pltpu.VMEM)
    return pl.pallas_call(
        kernel,
        out_shape=jax.ShapeDtypeStruct((rows, DEPTH), jnp.int32),
        in_specs=[pl.BlockSpec(memory_space=pltpu.SMEM)] + [vmem] * len(ids),
        out_specs=vmem,
        compiler_params=pltpu.CompilerParams(vmem_limit_bytes=8 << 20),
        name=kernel.__name__,
    )(me, *ids)


def ring(axis, step):
    gy = lax.axis_index("gy")
    row, col = gy // 4, lax.rem(gy, 4)
    if axis == 0:
        place = lax.rem(col + step, 4)
        return col, place, {"gx": lax.axis_index("gx"), "gy": row * 4 + place}
    place = lax.rem(row + step, 4)
    return row, place, {"gx": lax.axis_index("gx"), "gy": place * 4 + col}


RING_AXES = ((0, 1, 1, 0), (1, 0, 0, 1))
RING_KINDS = ((K_FIRST, K_X2, K_X3, K_X4), (K_FIRST, K_Y2, K_Y3, K_Y4))


class Lane:
    def __init__(self, order, perms, table_ref, first, scratch, final=None):
        self.order, self.perms, self.table_ref = order, perms, table_ref
        self.first, self.final = first, final
        self.stages = [scratch[4 * n : 4 * n + 4] for n in range(4)]
        self.waiting, self.sent = [], []

    def arrived(self):
        for copy in self.waiting:
            copy.wait_recv()
        self.waiting = []

    def target(self, stage, here):
        if stage == 3 and self.final is not None:
            return self.final(here)
        return self.stages[stage][1].at[here]

    def advance(self, stage):
        self.arrived()
        send, _, send_sem, recv_sem = self.stages[stage]
        for step in (2, 1, 3, 0):
            here, place, target = ring(RING_AXES[self.order][stage], step)
            landing = self.target(stage, here)
            for n, perm in enumerate(self.perms):
                slot = self.table_ref[perm * 8 + RING_KINDS[self.order][stage], place]
                if stage:
                    value = self.stages[stage - 1][1][slot, n]
                else:
                    value = self.first(n, slot)
                if step:
                    send[step - 1, n] = value
                else:
                    landing[n] = value
            if step:
                copy = pltpu.make_async_remote_copy(
                    src_ref=send.at[step - 1],
                    dst_ref=landing,
                    send_sem=send_sem.at[step - 1],
                    recv_sem=recv_sem.at[step - 1],
                    device_id=target,
                    device_id_type=MESH,
                )
                copy.start()
                self.waiting.append(copy)
                self.sent.append(copy)

    def close(self):
        for copy in self.sent:
            copy.wait_send()


def lane_scratch(items, shape):
    scratch = []
    for stage in range(4):
        scratch += [
            pltpu.VMEM((3, items) + shape, jnp.float32),
            pltpu.VMEM((4, items) + shape, jnp.float32),
            pltpu.SemaphoreType.DMA((3,)),
            pltpu.SemaphoreType.DMA((3,)),
        ]
    return scratch


RING_PEERS = tuple((axis, step) for axis in range(2) for step in (1, 2, 3))
LANES = 4


def source_kernel(
    permit_ref,
    me_ref,
    table_ref,
    charge_ref,
    mask_ref,
    ids_ref,
    phase_ref,
    ext_ref,
    face_ref,
    coef_ref,
    scale_ref,
    others,
    permit,
    send_sem,
    recv_sem,
    ids_send,
    ids_recv,
    *scratch,
):
    bands = [shifted_id(1, 0), shifted_id(-1, 0)]
    greet([ring(*peer)[2] for peer in RING_PEERS] + [shifted_id(dx, dy) for dx, dy in AROUND])
    passed = []
    for n, target in enumerate(bands):
        copy = pltpu.make_async_remote_copy(
            src_ref=ids_ref,
            dst_ref=others.at[n],
            send_sem=ids_send.at[n],
            recv_sem=ids_recv.at[n],
            device_id=target,
            device_id_type=MESH,
        )
        copy.start()
        passed.append(copy)
    part = EDGE // LANES
    lanes = []
    for n in range(LANES):

        def first(_, slot, n=n):
            flags = mask_ref[slot, 1 + n * part : 1 + (n + 1) * part, 1 : EDGE + 1]
            return charge_ref[slot, n * part : (n + 1) * part] * flags.astype(jnp.float32)

        lanes.append(
            Lane(n % 2, (TO_OWNER,), table_ref, first, scratch[16 * n : 16 * n + 16])
        )

    def store(place, row):
        face_ref[pl.ds(place, 1)] = row

    def weights(begin, end):
        weigh_rows(begin, end, permit, coef_ref, scale_ref)

    for stage in range(4):
        for lane in lanes:
            lane.advance(stage)
        if stage == 0:
            look_up_rows(permit_ref, phase_ref, permit)
            weights(0, 8)
            for copy in passed:
                copy.wait_recv()
            tables = face_tables(
                me_ref[0],
                gathered_ids(ids_ref[...]),
                gathered_ids(others[0]),
                gathered_ids(others[1]),
                store,
            )
            next(tables)
        elif stage < 3:
            next(tables, None)
        else:
            weights(8, 24)
    for n, lane in enumerate(lanes):
        lane.arrived()
        final = lane.stages[3][1]
        for t in range(TILES):
            i0, j0 = 4 + (t // 2) * EDGE + n * part, SIDE + (t % 2) * EDGE
            ext_ref[i0 : i0 + part, j0 : j0 + EDGE] = final[
                table_ref[TO_OWNER * 8 + K_LAST, t], 0
            ]
    block = ext_ref.at[pl.ds(4, BLOCK), pl.ds(SIDE, BLOCK)]
    copies = halo_copies(block, ext_ref, 4, send_sem, recv_sem)
    for copy in copies:
        copy.start()
    weights(24, TALL)
    for copy in copies:
        copy.wait()
    for copy in passed:
        copy.wait_send()
    for lane in lanes:
        lane.close()


def gather_source(permittivity, me, routes, charge, fluid_mask, ids, phase):
    vmem = pl.BlockSpec(memory_space=pltpu.VMEM)
    smem = pl.BlockSpec(memory_space=pltpu.SMEM)
    dma = pltpu.SemaphoreType.DMA
    f32 = jnp.float32
    return pl.pallas_call(
        source_kernel,
        out_shape=(
            jax.ShapeDtypeStruct((TALL, WIDE, DEPTH), f32),
            jax.ShapeDtypeStruct((48, DEPTH), jnp.int32),
            jax.ShapeDtypeStruct((6, TALL, WIDE, DEPTH), f32),
            jax.ShapeDtypeStruct((TALL, WIDE, DEPTH), f32),
        ),
        in_specs=[smem] * 3 + [vmem] * 4,
        out_specs=(vmem,) * 4,
        scratch_shapes=[
            pltpu.VMEM((2, GROUPS, 8, DEPTH), jnp.int32),
            pltpu.VMEM((TALL + 2, WIDE, DEPTH), f32),
            dma((8,)),
            dma((8,)),
            dma((2,)),
            dma((2,)),
        ]
        + lane_scratch(1, (EDGE // LANES, EDGE, DEPTH)) * LANES,
        compiler_params=pltpu.CompilerParams(
            collective_id=1, has_side_effects=True, vmem_limit_bytes=24 << 20
        ),
        name="source",
    )(permittivity, me, routes, charge, fluid_mask, ids, phase)


def back_kernel(table_ref, items_ref, out_ref, *scratch):
    greet([ring(*peer)[2] for peer in RING_PEERS])
    part = PACK // LANES
    lanes = []
    for n in range(LANES):
        rows = slice(n * part, (n + 1) * part)

        def first(_, slot, rows=rows):
            return items_ref[slot, rows]

        def final(here, n=n):
            return out_ref.at[here, :, pl.ds(n * part, part)]

        lanes.append(
            Lane(n % 2, (TO_HOLDER,), table_ref, first, scratch[16 * n : 16 * n + 16], final)
        )
    for stage in range(4):
        for lane in lanes:
            lane.advance(stage)
    for lane in lanes:
        lane.arrived()
    for lane in lanes:
        lane.close()


def send_back(routes, packed):
    vmem = pl.BlockSpec(memory_space=pltpu.VMEM)
    return pl.pallas_call(
        back_kernel,
        out_shape=jax.ShapeDtypeStruct((TILES, 1, PACK, EDGE, DEPTH), jnp.float32),
        in_specs=[pl.BlockSpec(memory_space=pltpu.SMEM), vmem],
        out_specs=vmem,
        scratch_shapes=lane_scratch(1, (PACK // LANES, EDGE, DEPTH)) * LANES,
        compiler_params=pltpu.CompilerParams(
            collective_id=2, has_side_effects=True, vmem_limit_bytes=24 << 20
        ),
        name="back",
    )(routes, packed)


FACES = 5


FACE_LANES = (
    (0, (UP_Y, DOWN_Y, SAME_X)),
    (1, (UP_Y, DOWN_Y, SAME_X)),
    (0, (BELOW_X, ABOVE_X)),
    (1, (BELOW_X, ABOVE_X)),
)


def faces_kernel(
    table_ref,
    faces_ref,
    corners_ref,
    out_ref,
    all_ref,
    shifted,
    corner_send,
    corner_recv,
    shift_send,
    shift_recv,
    own_sem,
    *scratch,
):
    me = lax.axis_index("gy")
    peers = [shifted_id(0, k) for k in range(1, GROUPS)]
    bands = [shifted_id(1, 0), shifted_id(-1, 0)]
    greet(peers + bands)
    shifts = []
    for n, target in enumerate(bands):
        copy = pltpu.make_async_remote_copy(
            src_ref=faces_ref.at[:, 3 + n],
            dst_ref=shifted.at[n],
            send_sem=shift_send.at[n],
            recv_sem=shift_recv.at[n],
            device_id=target,
            device_id_type=MESH,
        )
        copy.start()
        shifts.append(copy)
    lanes = []
    for n, (order, perms) in enumerate(FACE_LANES):
        rows = slice(order * 3, order * 3 + 3)

        def first(k, slot, perms=perms, rows=rows):
            if perms[k] < BELOW_X:
                return faces_ref[slot, perms[k], rows]
            return shifted[perms[k] - BELOW_X, slot, rows]

        def final(here, perms=perms, order=order):
            return out_ref.at[here, pl.ds(perms[0], len(perms)), pl.ds(order * 3, 3)]

        lanes.append(Lane(order, perms, table_ref, first, scratch[16 * n : 16 * n + 16], final))
    spread_out, forward = [], []
    own = pltpu.make_async_copy(corners_ref, all_ref.at[0, me], own_sem)
    for stage in range(4):
        for n, lane in enumerate(lanes):
            if stage == 0 and n == 2:
                for k, target in enumerate(peers):
                    copy = pltpu.make_async_remote_copy(
                        src_ref=corners_ref,
                        dst_ref=all_ref.at[0, me],
                        send_sem=corner_send.at[k],
                        recv_sem=corner_recv.at[k],
                        device_id=target,
                        device_id_type=MESH,
                    )
                    copy.start()
                    spread_out.append(copy)
                own.start()
                for copy in shifts:
                    copy.wait_recv()
            lane.advance(stage)
        if stage == 1:
            own.wait()
            for copy in spread_out:
                copy.wait_recv()
            for n, target in enumerate(bands):
                copy = pltpu.make_async_remote_copy(
                    src_ref=all_ref.at[0],
                    dst_ref=all_ref.at[1 + n],
                    send_sem=corner_send.at[GROUPS - 1 + n],
                    recv_sem=corner_recv.at[GROUPS - 1 + n],
                    device_id=target,
                    device_id_type=MESH,
                )
                copy.start()
                forward.append(copy)
    for lane in lanes:
        lane.arrived()
    for copy in forward:
        copy.wait_recv()
    for copy in shifts + spread_out + forward:
        copy.wait_send()
    for lane in lanes:
        lane.close()


def send_faces(routes, faces, corners):
    vmem = pl.BlockSpec(memory_space=pltpu.VMEM)
    f32 = jnp.float32
    dma = pltpu.SemaphoreType.DMA
    scratch = []
    for _, perms in FACE_LANES:
        scratch += lane_scratch(len(perms), (3, EDGE, DEPTH))
    return pl.pallas_call(
        faces_kernel,
        out_shape=(
            jax.ShapeDtypeStruct((TILES, FACES, 6, EDGE, DEPTH), f32),
            jax.ShapeDtypeStruct((3, GROUPS, 2, 8, DEPTH), f32),
        ),
        in_specs=[pl.BlockSpec(memory_space=pltpu.SMEM), vmem, vmem],
        out_specs=(vmem, vmem),
        scratch_shapes=[
            pltpu.VMEM((2, TILES, 6, EDGE, DEPTH), f32),
            dma((GROUPS + 1,)),
            dma((GROUPS + 1,)),
            dma((2,)),
            dma((2,)),
            dma,
        ]
        + scratch,
        compiler_params=pltpu.CompilerParams(
            collective_id=3, has_side_effects=True, vmem_limit_bytes=24 << 20
        ),
        name="faces",
    )(routes, faces, corners)


def solve_kernel(
    coef, scale_ref, source_ref, pot_ref, pack, resid, upd_a, upd_b, total
):
    center = 0.5 * (spectrum_high + spectrum_low)
    half = 0.5 * (spectrum_high - spectrum_low)
    ratio = center / half

    def begin(i, carry):
        value = source_ref[i] * scale_ref[i]
        resid[i] = value
        value = value * (1.0 / center)
        upd_a[i, INNER] = value
        total[i] = value
        return carry

    lax.fori_loop(0, TALL, begin, 0)

    rho = 1.0 / ratio
    old, new = upd_a, upd_b
    for sweep in range(3):
        rho_new = 1.0 / (2.0 * ratio - rho)
        keep, gain = rho_new * rho, 2.0 * rho_new / half

        def relax(i, carry, old=old, new=new, keep=keep, gain=gain):
            here = old[i, INNER]
            near = coef[0, i] * old[i + 1, INNER] + coef[1, i] * old[i - 1, INNER]
            near += coef[2, i] * old[i, AFTER] + coef[3, i] * old[i, BEFORE]
            near += coef[4, i] * pltpu.roll(here, DEPTH - 1, 1)
            near += coef[5, i] * pltpu.roll(here, 1, 1)
            left = resid[i] - here + near
            resid[i] = left
            here = keep * here + gain * left
            new[i, INNER] = here
            total[i] = total[i] + here
            return carry

        lax.fori_loop(sweep + 1, TALL - 1 - sweep, relax, 0)
        old, new = new, old
        rho = rho_new

    def emit(i, carry):
        pot_ref[i] = total[i + 4, pl.ds(SIDE, BLOCK)]
        return carry

    lax.fori_loop(0, BLOCK, emit, 0)
    for t in range(TILES):
        i0, j0 = 4 + (t // 2) * EDGE, SIDE + (t % 2) * EDGE

        def rows(i, carry, t=t, i0=i0, j0=j0):
            pack[t, i] = total[i0 + i, pl.ds(j0, EDGE)]
            for place, ref in ((EDGE + 2, total), (EDGE + 6, source_ref)):
                pack[t, place, pl.ds(i, 1)] = ref[i0 + i, pl.ds(j0 - 1, 1)]
                pack[t, place + 1, pl.ds(i, 1)] = ref[i0 + i, pl.ds(j0 + EDGE, 1)]
            return carry

        lax.fori_loop(0, EDGE, rows, 0)
        for place, ref in ((EDGE, total), (EDGE + 4, source_ref)):
            pack[t, place] = ref[i0 - 1, pl.ds(j0, EDGE)]
            pack[t, place + 1] = ref[i0 + EDGE, pl.ds(j0, EDGE)]


def solve(coef, scale, source):
    vmem = pl.BlockSpec(memory_space=pltpu.VMEM)
    f32 = jnp.float32
    return pl.pallas_call(
        solve_kernel,
        out_shape=(
            jax.ShapeDtypeStruct((BLOCK, BLOCK, DEPTH), f32),
            jax.ShapeDtypeStruct((TILES, PACK, EDGE, DEPTH), f32),
        ),
        in_specs=[vmem, vmem, vmem],
        out_specs=(vmem, vmem),
        scratch_shapes=[
            pltpu.VMEM((TALL, WIDE, DEPTH), f32),
            pltpu.VMEM((TALL, ROOM, DEPTH), f32),
            pltpu.VMEM((TALL, ROOM, DEPTH), f32),
            pltpu.VMEM((TALL, WIDE, DEPTH), f32),
        ],
        compiler_params=pltpu.CompilerParams(vmem_limit_bytes=32 << 20),
        name="solve",
    )(coef, scale, source)


def collide_rows(pops, charge, field):
    force = [charge * component for component in field]
    sums = {}
    diffs = {}
    for a, b in PAIRS:
        sums[a] = pops[a] + pops[b]
        diffs[a] = pops[a] - pops[b]
    density = pops[0]
    for a, _ in PAIRS:
        density = density + sums[a]
    momentum = [
        diffs[1] + diffs[7] + diffs[9] + diffs[11] + diffs[13],
        diffs[3] + diffs[7] - diffs[9] + diffs[15] + diffs[17],
        diffs[5] + diffs[11] - diffs[13] + diffs[15] - diffs[17],
    ]
    inverse = 1.0 / density
    velocity = [(momentum[d] + 0.5 * force[d]) * inverse for d in range(3)]
    scale = 1.0 - 0.5 / relax_time
    rate = 1.0 / relax_time
    speed = velocity[0] * velocity[0] + velocity[1] * velocity[1] + velocity[2] * velocity[2]
    work = velocity[0] * force[0] + velocity[1] * force[1] + velocity[2] * force[2]
    weighted = rate * density
    base = weighted - (1.5 * weighted) * speed - (3.0 * scale) * work
    odd = [3.0 * weighted * velocity[d] + (3.0 * scale) * force[d] for d in range(3)]
    inner = [4.5 * weighted * velocity[d] + (9.0 * scale) * force[d] for d in range(3)]
    keep = 1.0 - rate
    result = [None] * 19
    result[0] = keep * pops[0] + WEIGHTS[0] * base
    for a, b in PAIRS:
        step = LATTICE[a]
        axes = [d for d in range(3) if step[d] != 0]
        if len(axes) == 1:
            (d,) = axes
            cu, co, ci = velocity[d], odd[d], inner[d]
            weight = WEIGHTS[1]
        else:
            d, e = axes
            weight = WEIGHTS[2]
            if step[d] * step[e] > 0:
                cu, co, ci = velocity[d] + velocity[e], odd[d] + odd[e], inner[d] + inner[e]
            else:
                cu, co, ci = velocity[d] - velocity[e], odd[d] - odd[e], inner[d] - inner[e]
        even = weight * (base + cu * ci)
        lean = weight * co
        result[a] = keep * pops[a] + (even + lean)
        result[b] = keep * pops[b] + (even - lean)
    return result, velocity


def collide_kernel(
    table_ref, routes_ref, pops_ref, charge_ref, mask_ref, pot_ref, out_ref, vel_ref, face_ref, corner_ref, grown
):
    tile = pl.program_id(0)

    def place(i, carry):
        grown[i + 1, pl.ds(8, EDGE)] = pot_ref[0, 0, i]
        grown[i + 1, pl.ds(7, 1)] = pot_ref[0, 0, EDGE + 2, pl.ds(i, 1)]
        grown[i + 1, pl.ds(8 + EDGE, 1)] = pot_ref[0, 0, EDGE + 3, pl.ds(i, 1)]
        return carry

    lax.fori_loop(0, EDGE, place, 0)
    grown[0, pl.ds(8, EDGE)] = pot_ref[0, 0, EDGE]
    grown[EDGE + 1, pl.ds(8, EDGE)] = pot_ref[0, 0, EDGE + 1]
    y_low, y_high = crossing(1, -1), crossing(1, 1)

    def rows(i, carry):
        here = grown[i + 1, pl.ds(8, EDGE)]
        field = [
            0.5 * (grown[i, pl.ds(8, EDGE)] - grown[i + 2, pl.ds(8, EDGE)]),
            0.5 * (grown[i + 1, pl.ds(7, EDGE)] - grown[i + 1, pl.ds(9, EDGE)]),
            0.5 * (pltpu.roll(here, 1, 1) - pltpu.roll(here, DEPTH - 1, 1)),
        ]
        pops = [pops_ref[q, 0, i] for q in range(19)]
        relaxed, velocity = collide_rows(pops, charge_ref[0, i], field)
        fluid = mask_ref[0, i + 1, pl.ds(1, EDGE), :] == 1
        for q in range(19):
            value = jnp.where(fluid, relaxed[q], pops[q])
            out_ref[q, 0, i] = value
            if q in y_low:
                face_ref[0, 1, y_low.index(q), pl.ds(i, 1)] = value[0:1]
            if q in y_high:
                face_ref[0, 0, y_high.index(q), pl.ds(i, 1)] = value[EDGE - 1 :]
        for d in range(3):
            vel_ref[d, 0, i] = velocity[d]
        face_ref[0, 1, 5, pl.ds(i, 1)] = velocity[1][0:1]
        face_ref[0, 0, 5, pl.ds(i, 1)] = velocity[1][EDGE - 1 :]
        return carry

    lax.fori_loop(0, EDGE, rows, 0)

    def x_face(face, sign, layer):
        for k, q in enumerate(crossing(0, sign)):
            face_ref[0, face, k] = out_ref[q, 0, layer]
        face_ref[0, face, 5] = vel_ref[0, 0, layer]

    x_face(3, 1, EDGE - 1)
    x_face(4, -1, 0)

    @pl.when(table_ref[R_ROW, tile] == 0)
    def _():
        x_face(2, 1, EDGE - 1)

    @pl.when(table_ref[R_ROW, tile] == 1)
    def _():
        x_face(2, -1, 0)

    for n, (q, i, j) in enumerate(
        ((7, EDGE - 1, EDGE - 1), (9, EDGE - 1, 0), (10, 0, EDGE - 1), (8, 0, 0))
    ):
        corner_ref[tile // 2, pl.ds(lax.rem(tile, 2) * 4 + n, 1)] = out_ref[q, 0, i, pl.ds(j, 1)]


def collide(table, routes, populations, charge, fluid_mask, returned):
    f32 = jnp.float32
    pot_spec = pl.BlockSpec(
        (1, 1, PACK, EDGE, DEPTH), lambda s, tab, rts: (rts[TO_HOLDER * 8 + K_LAST, s], 0, 0, 0, 0)
    )
    return pl.pallas_call(
        collide_kernel,
        out_shape=(
            jax.ShapeDtypeStruct((19, TILES, EDGE, EDGE, DEPTH), f32),
            jax.ShapeDtypeStruct((3, TILES, EDGE, EDGE, DEPTH), f32),
            jax.ShapeDtypeStruct((TILES, FACES, 6, EDGE, DEPTH), f32),
            jax.ShapeDtypeStruct((2, 8, DEPTH), f32),
        ),
        grid_spec=pltpu.PrefetchScalarGridSpec(
            num_scalar_prefetch=2,
            grid=(TILES,),
            in_specs=[
                pl.BlockSpec((19, 1, EDGE, EDGE, DEPTH), lambda s, tab, rts: (0, s, 0, 0, 0)),
                pl.BlockSpec((1, EDGE, EDGE, DEPTH), lambda s, tab, rts: (s, 0, 0, 0)),
                pl.BlockSpec((1, EDGE + 2, EDGE + 2, DEPTH), lambda s, tab, rts: (s, 0, 0, 0)),
                pot_spec,
            ],
            out_specs=[
                pl.BlockSpec((19, 1, EDGE, EDGE, DEPTH), lambda s, tab, rts: (0, s, 0, 0, 0)),
                pl.BlockSpec((3, 1, EDGE, EDGE, DEPTH), lambda s, tab, rts: (0, s, 0, 0, 0)),
                pl.BlockSpec((1, FACES, 6, EDGE, DEPTH), lambda s, tab, rts: (s, 0, 0, 0, 0)),
                pl.BlockSpec((2, 8, DEPTH), lambda s, tab, rts: (0, 0, 0)),
            ],
            scratch_shapes=[pltpu.VMEM((EDGE + 2, 32, DEPTH), f32)],
        ),
        compiler_params=pltpu.CompilerParams(vmem_limit_bytes=32 << 20),
        name="collide",
    )(table, routes, populations, charge, fluid_mask, returned)


def stream_kernel(
    table_ref,
    routes_ref,
    relaxed_ref,
    vel_ref,
    charge_ref,
    mask_ref,
    rim_ref,
    *rest,
):
    faces, (corner_ref, pops_out, charge_out, xrim, yrim, corner) = rest[:FACES], rest[FACES:]
    tile = pl.program_id(0)
    row = table_ref[R_ROW, tile]
    plus = [crossing(0, 1), crossing(1, 1)]
    minus = [crossing(0, -1), crossing(1, -1)]

    def fill(out, face):
        for k in range(6):
            out[k] = faces[face][0, 0, k]

    fill(yrim.at[0], 0)
    fill(yrim.at[1], 1)
    for n, (side, end, which) in enumerate(((0, 0, 0), (0, 1, 1), (1, 0, 2), (1, 1, 3))):
        found = table_ref[R_CORNER + n, tile]
        tile_in = lax.rem(found, TILES)
        corner[side, pl.ds(end, 1)] = corner_ref[
            found // TILES, tile_in // 2, pl.ds(lax.rem(tile_in, 2) * 4 + which, 1)
        ]

    @pl.when(row == 0)
    def _():
        fill(xrim.at[0], 3)
        fill(xrim.at[1], 2)

    @pl.when(row == 1)
    def _():
        fill(xrim.at[0], 2)
        fill(xrim.at[1], 4)

    place = lax.broadcasted_iota(jnp.int32, (EDGE, DEPTH), 0)
    first, last = place == 0, place == EDGE - 1

    def rows(i, low_edge, high_edge):
        own = mask_ref[0, i + 1, pl.ds(1, EDGE), :]
        own_fluid = own == 1
        for q in range(19):
            step_x, step_y, step_z = LATTICE[q]
            value_here = relaxed_ref[q, 0, i]
            if q == 0:
                pops_out[q, 0, i] = value_here
                continue
            side = None
            if step_x == 1 and low_edge:
                side, channel = 0, plus[0].index(q)
            if step_x == -1 and high_edge:
                side, channel = 1, minus[0].index(q)
            if side is None:
                moved = value_here if step_x == 0 else relaxed_ref[q, 0, i - step_x]
            else:
                moved = xrim[side, channel]
            if step_y == 1:
                if side is None:
                    edge = yrim[0, plus[1].index(q), pl.ds(i - step_x, 1)]
                else:
                    edge = corner[side, pl.ds(0, 1)]
                moved = jnp.where(first, edge, pltpu.roll(moved, 1, 0))
            elif step_y == -1:
                if side is None:
                    edge = yrim[1, minus[1].index(q), pl.ds(i - step_x, 1)]
                else:
                    edge = corner[side, pl.ds(1, 1)]
                moved = jnp.where(last, edge, pltpu.roll(moved, EDGE - 1, 0))
            from_fluid = mask_ref[0, i + 1 - step_x, pl.ds(1 - step_y, EDGE), :]
            if step_z != 0:
                moved = pltpu.roll(moved, step_z % DEPTH, 1)
                from_fluid = pltpu.roll(from_fluid, step_z % DEPTH, 1)
            bounced = relaxed_ref[opposite(q), 0, i]
            read = jnp.where(from_fluid == 1, moved, bounced)
            pops_out[q, 0, i] = jnp.where(own_fluid, read, value_here)

        charge = charge_ref[0, i]
        flag = own.astype(jnp.float32)

        def flux(speed_a, speed_b, value_a, value_b, flags):
            speed = 0.5 * (speed_a + speed_b)
            return speed * jnp.where(speed > 0, value_a, value_b) * flags

        speed = vel_ref[0, 0, i]
        if low_edge:
            other, other_speed = rim_ref[0, 0, 0], xrim[0, 5]
        else:
            other, other_speed = charge_ref[0, i - 1], vel_ref[0, 0, i - 1]
        other_flag = mask_ref[0, i, pl.ds(1, EDGE), :].astype(jnp.float32)
        change = -flux(other_speed, speed, other, charge, other_flag * flag)
        if high_edge:
            other, other_speed = rim_ref[0, 0, 1], xrim[1, 5]
        else:
            other, other_speed = charge_ref[0, i + 1], vel_ref[0, 0, i + 1]
        other_flag = mask_ref[0, i + 2, pl.ds(1, EDGE), :].astype(jnp.float32)
        change += flux(speed, other_speed, charge, other, flag * other_flag)

        speed = vel_ref[1, 0, i]
        other = jnp.where(first, rim_ref[0, 0, 2, pl.ds(i, 1)], pltpu.roll(charge, 1, 0))
        other_speed = jnp.where(first, yrim[0, 5, pl.ds(i, 1)], pltpu.roll(speed, 1, 0))
        other_flag = mask_ref[0, i + 1, pl.ds(0, EDGE), :].astype(jnp.float32)
        change -= flux(other_speed, speed, other, charge, other_flag * flag)
        other = jnp.where(last, rim_ref[0, 0, 3, pl.ds(i, 1)], pltpu.roll(charge, EDGE - 1, 0))
        other_speed = jnp.where(
            last, yrim[1, 5, pl.ds(i, 1)], pltpu.roll(speed, EDGE - 1, 0)
        )
        other_flag = mask_ref[0, i + 1, pl.ds(2, EDGE), :].astype(jnp.float32)
        change += flux(speed, other_speed, charge, other, flag * other_flag)

        speed = vel_ref[2, 0, i]
        over = flux(
            speed,
            pltpu.roll(speed, DEPTH - 1, 1),
            charge,
            pltpu.roll(charge, DEPTH - 1, 1),
            flag * pltpu.roll(flag, DEPTH - 1, 1),
        )
        change += over - pltpu.roll(over, 1, 1)
        charge_out[0, i] = jnp.where(own_fluid, charge - change, charge)

    rows(0, True, False)

    def middle(i, carry):
        rows(i, False, False)
        return carry

    lax.fori_loop(1, EDGE - 1, middle, 0)
    rows(EDGE - 1, False, True)


def stream(table, routes, relaxed, velocity, charge, fluid_mask, returned, faces, corners):
    f32 = jnp.float32
    face_specs = [
        pl.BlockSpec(
            (1, 1, 6, EDGE, DEPTH),
            lambda s, tab, rts, face=face: (tab[face * 8 + K_LAST, s], face, 0, 0, 0),
        )
        for face in range(FACES)
    ]
    return pl.pallas_call(
        stream_kernel,
        out_shape=(
            jax.ShapeDtypeStruct((19, TILES, EDGE, EDGE, DEPTH), f32),
            jax.ShapeDtypeStruct((TILES, EDGE, EDGE, DEPTH), f32),
        ),
        grid_spec=pltpu.PrefetchScalarGridSpec(
            num_scalar_prefetch=2,
            grid=(TILES,),
            in_specs=[
                pl.BlockSpec((19, 1, EDGE, EDGE, DEPTH), lambda s, tab, rts: (0, s, 0, 0, 0)),
                pl.BlockSpec((3, 1, EDGE, EDGE, DEPTH), lambda s, tab, rts: (0, s, 0, 0, 0)),
                pl.BlockSpec((1, EDGE, EDGE, DEPTH), lambda s, tab, rts: (s, 0, 0, 0)),
                pl.BlockSpec((1, EDGE + 2, EDGE + 2, DEPTH), lambda s, tab, rts: (s, 0, 0, 0)),
                pl.BlockSpec(
                    (1, 1, 4, EDGE, DEPTH), lambda s, tab, rts: (rts[TO_HOLDER * 8 + K_LAST, s], 0, 5, 0, 0)
                ),
            ]
            + face_specs
            + [pl.BlockSpec((3 * GROUPS, 2, 8, DEPTH), lambda s, tab, rts: (0, 0, 0, 0))],
            out_specs=[
                pl.BlockSpec((19, 1, EDGE, EDGE, DEPTH), lambda s, tab, rts: (0, s, 0, 0, 0)),
                pl.BlockSpec((1, EDGE, EDGE, DEPTH), lambda s, tab, rts: (s, 0, 0, 0)),
            ],
            scratch_shapes=[
                pltpu.VMEM((2, 6, EDGE, DEPTH), f32),
                pltpu.VMEM((2, 6, EDGE, DEPTH), f32),
                pltpu.VMEM((2, 8, DEPTH), f32),
            ],
        ),
        compiler_params=pltpu.CompilerParams(vmem_limit_bytes=32 << 20),
        name="stream",
    )(
        table,
        routes,
        relaxed,
        velocity,
        charge,
        fluid_mask,
        returned,
        *([faces] * FACES),
        corners.reshape(3 * GROUPS, 2, 8, DEPTH),
    )


def per_device(populations, charge, fluid_mask, tile_ids, phase_label, permittivity):
    me = lax.axis_index("gy").astype(jnp.int32).reshape(1)
    place = jnp.arange(8 * DEPTH, dtype=jnp.int32).reshape(8, DEPTH)
    ids_row = jnp.where(place // TILES == me, jnp.tile(tile_ids, 2 * DEPTH).reshape(8, DEPTH), 0)
    ids, phase_ext = exchange_start(ids_row, phase_label)
    routes = make_routes(owner_routes_kernel, 16, me, ids)
    source_ext, table, coef, scale = gather_source(
        permittivity, me, routes, charge, fluid_mask, ids, phase_ext
    )
    potential, packed = solve(coef, scale, source_ext)
    returned = send_back(routes, packed)
    relaxed, velocity, faces, corners = collide(
        table, routes, populations, charge, fluid_mask, returned
    )
    rims, all_corners = send_faces(table, faces, corners)
    populations_next, charge_next = stream(
        table, routes, relaxed, velocity, charge, fluid_mask, returned, rims, all_corners
    )
    return (populations_next, charge_next, potential)


def solution(mesh):
    placed = (
        P(None, ("gx", "gy"), None, None, None),
        P(("gx", "gy"), None, None, None),
        P(("gx", "gy"), None, None, None),
        P(("gx", "gy")),
        P("gx", "gy", None),
        P(),
    )
    return jax.shard_map(
        per_device,
        mesh=mesh,
        in_specs=placed,
        out_specs=(
            P(None, ("gx", "gy"), None, None, None),
            P(("gx", "gy"), None, None, None),
            P("gx", "gy", None),
        ),
        check_vma=False,
    )
```

```python
import functools

import jax
import jax.numpy as jnp
from jax import lax
from jax.experimental import pallas as pl
from jax.experimental.pallas import tpu as pltpu
from jax.sharding import PartitionSpec as P

EDGE = 16
DEPTH = 128
BLOCK = 32
PHASES = 4
SWEEPS = 4
UNROLL = 2
TILES = 4
GROUPS = 16
BANDS = 8
COLS = 32
SIDE = 8
MESH = pl.DeviceIdType.MESH

LATTICE = (
    (0, 0, 0),
    (1, 0, 0),
    (-1, 0, 0),
    (0, 1, 0),
    (0, -1, 0),
    (0, 0, 1),
    (0, 0, -1),
    (1, 1, 0),
    (-1, -1, 0),
    (1, -1, 0),
    (-1, 1, 0),
    (1, 0, 1),
    (-1, 0, -1),
    (1, 0, -1),
    (-1, 0, 1),
    (0, 1, 1),
    (0, -1, -1),
    (0, 1, -1),
    (0, -1, 1),
)
WEIGHTS = (1.0 / 3.0, 1.0 / 18.0, 1.0 / 36.0)
PAIRS = ((1, 2), (3, 4), (5, 6), (7, 8), (9, 10), (11, 12), (13, 14), (15, 16), (17, 18))
relax_time = 0.8
screening = 0.001
spectrum_low = 0.1
spectrum_high = 2.0

AROUND = tuple((dx, dy) for dx in (-1, 0, 1) for dy in (-1, 0, 1) if (dx, dy) != (0, 0))

TO_OWNER, TO_HOLDER = 0, 1
UP_Y, DOWN_Y, SAME_X, BELOW_X, ABOVE_X = range(5)
R_ROW, R_CORNER = 40, 41


def opposite(direction):
    return LATTICE.index(tuple(-entry for entry in LATTICE[direction]))


def crossing(axis_index, face_sign):
    return [d for d in range(19) if LATTICE[d][axis_index] == face_sign]


def shifted_id(dx, dy):
    gx = lax.rem(lax.axis_index("gx") + dx + BANDS, BANDS)
    gy = lax.rem(lax.axis_index("gy") + dy + GROUPS, GROUPS)
    return {"gx": gx, "gy": gy}


def span(step, width, pad):
    if step == 0:
        return pl.ds(0, BLOCK), pl.ds(pad, BLOCK)
    if step > 0:
        return pl.ds(BLOCK - width, width), pl.ds(pad - width, width)
    return pl.ds(0, width), pl.ds(pad + BLOCK, width)


def halo_copies(block_ref, ext_ref, width, send_sem, recv_sem):
    copies = []
    for n, (dx, dy) in enumerate(AROUND):
        src_i, dst_i = span(dx, width, width)
        src_j, dst_j = span(dy, SIDE, SIDE)
        copies.append(
            pltpu.make_async_remote_copy(
                src_ref=block_ref.at[src_i, src_j],
                dst_ref=ext_ref.at[dst_i, dst_j],
                send_sem=send_sem.at[n],
                recv_sem=recv_sem.at[n],
                device_id=shifted_id(dx, dy),
                device_id_type=MESH,
            )
        )
    return copies


def greet(targets):
    barrier = pltpu.get_barrier_semaphore()
    for target in targets:
        pl.semaphore_signal(barrier, inc=1, device_id=target, device_id_type=MESH)
    pl.semaphore_wait(barrier, len(targets))


def start_kernel(ids_ref, all_ref, ids_send, ids_recv, own_sem):
    me = lax.axis_index("gy")
    peers = [shifted_id(0, k) for k in range(1, GROUPS)]
    greet(peers)
    started = []
    for k, target in enumerate(peers):
        copy = pltpu.make_async_remote_copy(
            src_ref=ids_ref,
            dst_ref=all_ref.at[me],
            send_sem=ids_send.at[k],
            recv_sem=ids_recv.at[k],
            device_id=target,
            device_id_type=MESH,
        )
        copy.start()
        started.append(copy)
    own = pltpu.make_async_copy(ids_ref, all_ref.at[me], own_sem)
    own.start()
    own.wait()
    for copy in started:
        copy.wait()


def exchange_start(ids):
    vmem = pl.BlockSpec(memory_space=pltpu.VMEM)
    dma = pltpu.SemaphoreType.DMA
    return pl.pallas_call(
        start_kernel,
        out_shape=jax.ShapeDtypeStruct((GROUPS, 8, DEPTH), jnp.int32),
        in_specs=[vmem],
        out_specs=vmem,
        scratch_shapes=[dma((GROUPS - 1,)), dma((GROUPS - 1,)), dma],
        compiler_params=pltpu.CompilerParams(
            collective_id=0, has_side_effects=True, vmem_limit_bytes=8 << 20
        ),
        name="start",
    )(ids)


WIDE = BLOCK + 2 * SIDE
TALL = BLOCK + 8
ROOM = WIDE + 16
INNER = pl.ds(8, WIDE)
BEFORE = pl.ds(7, WIDE)
AFTER = pl.ds(9, WIDE)
PACK = 20


def harmonic(left, right):
    return 2.0 * left * right / (left + right)


def look_up_rows(permit_ref, phase_ref, permit):
    def look_up(i, carry):
        label = phase_ref[i]
        value = jnp.where(label == 0, permit_ref[0], 0.0)
        for k in range(1, PHASES):
            value = jnp.where(label == k, permit_ref[k], value)
        permit[i] = value
        return carry

    lax.fori_loop(0, TALL + 2, look_up, 0)


def weigh_rows(begin, end, permit, coef, scale_ref):
    def weigh(i, below):
        here = permit[i + 1]
        above = harmonic(here, permit[i + 2])
        right = harmonic(here, pltpu.roll(here, WIDE - 1, 0))
        left = pltpu.roll(right, 1, 0)
        up = harmonic(here, pltpu.roll(here, DEPTH - 1, 1))
        down = pltpu.roll(up, 1, 1)
        scale = 1.0 / (above + below + right + left + up + down + screening)
        for k, weight in enumerate((above, below, right, left, up, down)):
            coef[k, i] = weight * scale
        scale_ref[i] = scale
        return above

    lax.fori_loop(begin, end, weigh, harmonic(permit[begin], permit[begin + 1]), unroll=2)


def tile_corner(t):
    return 4 + (t // 2) * EDGE, SIDE + (t % 2) * EDGE


def pack_rims(out, place, ref):
    for t in range(TILES):
        i0, j0 = tile_corner(t)

        def rows(i, carry, t=t, i0=i0, j0=j0):
            out[t, place + 2, pl.ds(i, 1)] = ref[i0 + i, pl.ds(j0 - 1, 1)]
            out[t, place + 3, pl.ds(i, 1)] = ref[i0 + i, pl.ds(j0 + EDGE, 1)]
            return carry

        lax.fori_loop(0, EDGE, rows, 0, unroll=4)
        out[t, place] = ref[i0 - 1, pl.ds(j0, EDGE)]
        out[t, place + 1] = ref[i0 + EDGE, pl.ds(j0, EDGE)]


def sweep_rows(coef, scale_ref, source_ref, pot_ref, pack, resid, upd_a, upd_b, total, between):
    center = 0.5 * (spectrum_high + spectrum_low)
    half = 0.5 * (spectrum_high - spectrum_low)
    ratio = center / half

    def begin(i, carry):
        value = source_ref[i] * scale_ref[i]
        resid[i] = value
        value = value * (1.0 / center)
        upd_a[i, INNER] = value
        total[i] = value
        return carry

    lax.fori_loop(0, TALL, begin, 0, unroll=2)
    rho = 1.0 / ratio
    old, new = upd_a, upd_b
    for sweep in range(SWEEPS - 1):
        between(sweep + 1)
        rho_new = 1.0 / (2.0 * ratio - rho)
        keep, gain = rho_new * rho, 2.0 * rho_new / half

        def relax(i, carry, old=old, new=new, keep=keep, gain=gain):
            here = old[i, INNER]
            near = coef[0, i] * old[i + 1, INNER] + coef[1, i] * old[i - 1, INNER]
            near += coef[2, i] * old[i, AFTER] + coef[3, i] * old[i, BEFORE]
            near += coef[4, i] * pltpu.roll(here, DEPTH - 1, 1)
            near += coef[5, i] * pltpu.roll(here, 1, 1)
            left = resid[i] - here + near
            resid[i] = left
            here = keep * here + gain * left
            new[i, INNER] = here
            total[i] = total[i] + here
            return carry

        lax.fori_loop(sweep + 1, TALL - 1 - sweep, relax, 0, unroll=UNROLL)
        old, new = new, old
        rho = rho_new

    def emit(i, carry):
        pot_ref[i] = total[i + 4, pl.ds(SIDE, BLOCK)]
        return carry

    lax.fori_loop(0, BLOCK, emit, 0, unroll=4)
    for t in range(TILES):
        i0, j0 = tile_corner(t)

        def rows(i, carry, t=t, i0=i0, j0=j0):
            pack[t, i] = total[i0 + i, pl.ds(j0, EDGE)]
            return carry

        lax.fori_loop(0, EDGE, rows, 0, unroll=4)
    pack_rims(pack, EDGE, total)


K_FIRST, K_X2, K_X3, K_X4, K_Y2, K_Y3, K_Y4, K_LAST = range(8)
PORTS = 64


def to_column(row, eye):
    return jnp.sum(jnp.where(eye, row, 0), axis=1, keepdims=True)


def split_edges(left, right, sub, lane, doublings):
    def partners(ends):
        same = ends[0] == ends[1]
        before = jnp.where(same & (lane < sub), 1, 0)
        after = jnp.where(same & (sub < lane), 1, 0)
        rank_c = jnp.sum(before, axis=1, keepdims=True)
        rank_r = jnp.sum(after, axis=0, keepdims=True)
        pair = same & ((rank_c >> 1) == (rank_r >> 1)) & (sub != lane)
        return jnp.where(pair, 1.0, 0.0).astype(jnp.bfloat16)

    def times(a, b):
        return jnp.dot(a, b, preferred_element_type=jnp.float32)

    by_left, by_right = partners(left), partners(right)
    reach = times(by_left, by_right) + times(by_right, by_left)
    reach = jnp.where((sub == lane) | (reach > 0.0), 1.0, 0.0).astype(jnp.bfloat16)
    for _ in range(doublings):
        reach = jnp.where(times(reach, reach) > 0.0, 1.0, 0.0).astype(jnp.bfloat16)
    mate = times(by_left, reach) > 0.0
    own = reach.astype(jnp.float32) > 0.0
    size = sub.shape[0]
    col = jnp.where(
        jnp.min(jnp.where(own, lane, size), axis=1, keepdims=True)
        > jnp.min(jnp.where(mate, lane, size), axis=1, keepdims=True),
        1,
        0,
    )
    row = jnp.where(
        jnp.min(jnp.where(own, sub, size), axis=0, keepdims=True)
        > jnp.min(jnp.where(mate, sub, size), axis=0, keepdims=True),
        1,
        0,
    )
    return col, row


def join(first, second, base):
    return tuple(a * base + b for a, b in zip(first, second))


def colour(left, right, sub, lane, doublings):
    high = split_edges(left, right, sub, lane, doublings)
    low = split_edges(join(left, high, 2), join(right, high, 2), sub, lane, doublings - 1)
    return join(high, low, 2)


class Ports:
    def __init__(self, size):
        self.size = size
        self.sub = lax.broadcasted_iota(jnp.int32, (size, size), 0)
        self.lane = lax.broadcasted_iota(jnp.int32, (size, size), 1)
        self.eye = self.sub == self.lane
        edge = (
            lax.broadcasted_iota(jnp.int32, (size, 1), 0),
            lax.broadcasted_iota(jnp.int32, (1, size), 1),
        )
        self.port = tuple(e & (PORTS - 1) for e in edge)
        self.half = tuple(e >> 6 for e in edge)
        self.device = tuple(e >> 2 for e in self.port)
        self.entry = lax.broadcasted_iota(jnp.int32, (size, DEPTH), 1)


def store_routes(me, ports, places, goal_ids, target, store):
    half, port, device = ports.half, ports.port, ports.device
    sub, lane = ports.sub, ports.lane
    my_row, my_col = me >> 2, me & 3
    at = to_column(goal_ids, ports.eye) + half[0] * PORTS
    target = target + half[1] * PORTS
    drop = jnp.sum(jnp.where(at == target, sub & (PORTS - 1), 0), axis=0, keepdims=True)
    drop = (to_column(drop, ports.eye), drop)
    goal = tuple(d >> 2 for d in drop)
    begin = tuple(h * GROUPS + d for h, d in zip(half, device))
    end = tuple(h * GROUPS + d for h, d in zip(half, goal))
    j = colour(begin, end, sub, lane, 4)
    group = tuple(h * 4 + c for h, c in zip(half, j))
    rows = (tuple(d >> 2 for d in device), tuple(d >> 2 for d in goal))
    cols = (tuple(d & 3 for d in device), tuple(d & 3 for d in goal))
    b = colour(join(group, rows[0], 4), join(group, rows[1], 4), sub, lane, 2)[0]
    g = colour(join(group, cols[0], 4), join(group, cols[1], 4), sub, lane, 2)[0]
    j = j[0]
    slots = (port[0] & 3, drop[0] & 3)
    ends = (device[0], goal[0])
    rows, cols = tuple(r[0] for r in rows), tuple(c[0] for c in cols)
    for perm, h, back in places:
        mine = half[0] == h
        src, dst = (1, 0) if back else (0, 1)
        for kind, given, key, value in (
            (K_FIRST, ends[src] == me, j, slots[src]),
            (K_X2, (rows[src] == my_row) & (j == my_col), b, cols[src]),
            (K_X3, (j == my_col) & (b == my_row), rows[dst], rows[src]),
            (K_X4, (j == my_col) & (rows[dst] == my_row), cols[dst], b),
            (K_Y2, (cols[src] == my_col) & (j == my_row), g, rows[src]),
            (K_Y3, (j == my_row) & (g == my_col), cols[dst], cols[src]),
            (K_Y4, (j == my_row) & (cols[dst] == my_col), rows[dst], g),
            (K_LAST, ends[dst] == me, slots[dst], j),
        ):
            kept = jnp.where(mine & given, value, 0)
            found = jnp.where(key == ports.entry, kept, 0)
            store(perm * 8 + kind, jnp.sum(found, axis=0, keepdims=True))


def owner_tables(me, own, store):
    ports = Ports(PORTS)
    owner = (ports.port[1] & 3) // 2 * COLS + ports.device[1] * 2 + (ports.port[1] & 1)
    places = ((TO_OWNER, 0, True), (TO_HOLDER, 0, False))
    store_routes(me, ports, places, own[:, :PORTS], owner, store)


def face_tables(me, own, below, above, store):
    ports = Ports(2 * PORTS)
    half = ports.half

    def turn(pos, step):
        return (pos & COLS) + ((pos + step) & (COLS - 1))

    def both(first, second):
        return jnp.where(half[1] == 0, first, pltpu.roll(second, PORTS, 1))

    twice = both(own, own)
    places = ((UP_Y, 0, False), (DOWN_Y, 0, True), (SAME_X, 1, False))
    store_routes(me, ports, places, twice, both(turn(own, 1), own ^ COLS), store)
    yield
    places = ((BELOW_X, 0, False), (ABOVE_X, 1, False))
    store_routes(me, ports, places, twice, both(below ^ COLS, above ^ COLS), store)
    yield
    mine = jnp.sum(
        jnp.where((ports.sub == me * TILES + ports.lane) & (ports.lane < TILES), to_column(own, ports.eye), 0),
        axis=0,
        keepdims=True,
    )
    store(R_ROW, mine >> 5)
    found = []
    for band in (own, below, above):
        at = to_column(band, ports.eye)
        for step in (-1, 1):
            there = (at == turn(mine ^ COLS, step)) & (ports.sub < PORTS)
            found.append(jnp.sum(jnp.where(there, ports.sub, 0), axis=0, keepdims=True))
    upper = (mine >> 5) == 1
    for n in range(2):
        store(R_CORNER + n, jnp.where(upper, found[n], found[2 + n] + PORTS))
        store(R_CORNER + 2 + n, jnp.where(upper, found[4 + n] + 2 * PORTS, found[n]))


def gathered_ids(ids):
    return jnp.sum(ids, axis=0)[0:1]


def owner_routes_kernel(me_ref, ids_ref, out_ref):
    def store(place, row):
        out_ref[pl.ds(place, 1)] = row

    owner_tables(me_ref[0], gathered_ids(ids_ref[...]), store)


def make_routes(kernel, rows, me, *ids):
    vmem = pl.BlockSpec(memory_space=pltpu.VMEM)
    return pl.pallas_call(
        kernel,
        out_shape=jax.ShapeDtypeStruct((rows, DEPTH), jnp.int32),
        in_specs=[pl.BlockSpec(memory_space=pltpu.SMEM)] + [vmem] * len(ids),
        out_specs=vmem,
        compiler_params=pltpu.CompilerParams(vmem_limit_bytes=8 << 20),
        name=kernel.__name__,
    )(me, *ids)


def ring(axis, step):
    gy = lax.axis_index("gy")
    row, col = gy // 4, lax.rem(gy, 4)
    if axis == 0:
        place = lax.rem(col + step, 4)
        return col, place, {"gx": lax.axis_index("gx"), "gy": row * 4 + place}
    place = lax.rem(row + step, 4)
    return row, place, {"gx": lax.axis_index("gx"), "gy": place * 4 + col}


RING_AXES = ((0, 1, 1, 0), (1, 0, 0, 1))
RING_KINDS = ((K_FIRST, K_X2, K_X3, K_X4), (K_FIRST, K_Y2, K_Y3, K_Y4))


class Lane:
    def __init__(self, order, perms, table_ref, first, scratch, final=None):
        self.order, self.perms, self.table_ref = order, perms, table_ref
        self.first, self.final = first, final
        self.stages = [scratch[4 * n : 4 * n + 4] for n in range(4)]
        self.waiting, self.sent = [], []

    def arrived(self):
        for copy in self.waiting:
            copy.wait_recv()
        self.waiting = []

    def target(self, stage, here):
        if stage == 3 and self.final is not None:
            return self.final(here)
        return self.stages[stage][1].at[here]

    def advance(self, stage):
        self.arrived()
        send, _, send_sem, recv_sem = self.stages[stage]
        for step in (2, 1, 3, 0):
            here, place, target = ring(RING_AXES[self.order][stage], step)
            landing = self.target(stage, here)
            for n, perm in enumerate(self.perms):
                slot = self.table_ref[perm * 8 + RING_KINDS[self.order][stage], place]
                if stage:
                    value = self.stages[stage - 1][1][slot, n]
                else:
                    value = self.first(n, slot)
                if step:
                    send[step - 1, n] = value
                else:
                    landing[n] = value
            if step:
                copy = pltpu.make_async_remote_copy(
                    src_ref=send.at[step - 1],
                    dst_ref=landing,
                    send_sem=send_sem.at[step - 1],
                    recv_sem=recv_sem.at[step - 1],
                    device_id=target,
                    device_id_type=MESH,
                )
                copy.start()
                self.waiting.append(copy)
                self.sent.append(copy)

    def close(self):
        for copy in self.sent:
            copy.wait_send()


def lane_scratch(items, shape):
    scratch = []
    for stage in range(4):
        scratch += [
            pltpu.VMEM((3, items) + shape, jnp.float32),
            pltpu.VMEM((4, items) + shape, jnp.float32),
            pltpu.SemaphoreType.DMA((3,)),
            pltpu.SemaphoreType.DMA((3,)),
        ]
    return scratch


RING_PEERS = tuple((axis, step) for axis in range(2) for step in (1, 2, 3))
LANES = 4


def source_kernel(
    permit_ref,
    table_ref,
    charge_ref,
    mask_ref,
    ids_ref,
    phase_ref,
    pot_ref,
    pack_ref,
    others,
    rims_ref,
    rims,
    ext_ref,
    coef_ref,
    scale_ref,
    resid,
    upd_a,
    upd_b,
    total,
    phase_ext,
    permit,
    send_sem,
    recv_sem,
    phase_send,
    phase_recv,
    ids_send,
    ids_recv,
    own_sem,
    *scratch,
):
    bands = [shifted_id(1, 0), shifted_id(-1, 0)]
    greet([ring(*peer)[2] for peer in RING_PEERS] + [shifted_id(dx, dy) for dx, dy in AROUND])
    part = EDGE // LANES
    lanes = []
    for n in range(LANES):

        def first(_, slot, n=n):
            flags = mask_ref[slot, 1 + n * part : 1 + (n + 1) * part, 1 : EDGE + 1]
            return charge_ref[slot, n * part : (n + 1) * part] * flags.astype(jnp.float32)

        lanes.append(
            Lane(n % 2, (TO_OWNER,), table_ref, first, scratch[16 * n : 16 * n + 16])
        )
    passed = []
    own = pltpu.make_async_copy(
        phase_ref, phase_ext.at[pl.ds(5, BLOCK), pl.ds(SIDE, BLOCK)], own_sem
    )
    phases = halo_copies(phase_ref, phase_ext, 5, phase_send, phase_recv)

    def weights(begin, end):
        weigh_rows(begin, end, permit, coef_ref, scale_ref)

    for stage in range(4):
        for lane in lanes:
            lane.advance(stage)
        if stage == 0:
            for copy in phases:
                copy.start()
            own.start()
            for n, target in enumerate(bands):
                copy = pltpu.make_async_remote_copy(
                    src_ref=ids_ref,
                    dst_ref=others.at[n],
                    send_sem=ids_send.at[n],
                    recv_sem=ids_recv.at[n],
                    device_id=target,
                    device_id_type=MESH,
                )
                copy.start()
                passed.append(copy)
        elif stage == 1:
            own.wait()
            for copy in phases:
                copy.wait_recv()
            look_up_rows(permit_ref, phase_ext, permit)
            weights(0, 8)
        elif stage == 2:
            weights(8, 18)
        else:
            weights(18, 30)
    for n, lane in enumerate(lanes):
        lane.arrived()
        final = lane.stages[3][1]
        for t in range(TILES):
            i0, j0 = 4 + (t // 2) * EDGE + n * part, SIDE + (t % 2) * EDGE
            ext_ref[i0 : i0 + part, j0 : j0 + EDGE] = final[
                table_ref[TO_OWNER * 8 + K_LAST, t], 0
            ]
    block = ext_ref.at[pl.ds(4, BLOCK), pl.ds(SIDE, BLOCK)]
    copies = halo_copies(block, ext_ref, 4, send_sem, recv_sem)
    for copy in copies:
        copy.start()
    weights(30, TALL)
    for copy in copies + passed:
        copy.wait()
    for copy in phases:
        copy.wait_send()
    pack_rims(rims, 0, ext_ref)
    returning = []
    for n in range(2):

        def first(_, slot, n=n):
            return rims[slot, 2 * n : 2 * n + 2]

        def final(here, n=n):
            return rims_ref.at[here, :, pl.ds(2 * n, 2)]

        refs = scratch[16 * (LANES + n) : 16 * (LANES + n) + 16]
        returning.append(Lane(n, (TO_HOLDER,), table_ref, first, refs, final))

    def between(stage):
        for lane in returning:
            lane.advance(stage)

    between(0)
    sweep_rows(
        coef_ref, scale_ref, ext_ref, pot_ref, pack_ref, resid, upd_a, upd_b, total, between
    )
    for lane in returning:
        lane.arrived()
    for lane in lanes + returning:
        lane.close()


def find_potential(permittivity, routes, charge, fluid_mask, ids, phase):
    vmem = pl.BlockSpec(memory_space=pltpu.VMEM)
    smem = pl.BlockSpec(memory_space=pltpu.SMEM)
    dma = pltpu.SemaphoreType.DMA
    f32 = jnp.float32
    return pl.pallas_call(
        source_kernel,
        out_shape=(
            jax.ShapeDtypeStruct((BLOCK, BLOCK, DEPTH), f32),
            jax.ShapeDtypeStruct((TILES, PACK, EDGE, DEPTH), f32),
            jax.ShapeDtypeStruct((2, GROUPS, 8, DEPTH), jnp.int32),
            jax.ShapeDtypeStruct((TILES, 1, 4, EDGE, DEPTH), f32),
        ),
        in_specs=[smem] * 2 + [vmem] * 4,
        out_specs=(vmem,) * 4,
        scratch_shapes=[
            pltpu.VMEM((TILES, 4, EDGE, DEPTH), f32),
            pltpu.VMEM((TALL, WIDE, DEPTH), f32),
            pltpu.VMEM((6, TALL, WIDE, DEPTH), f32),
            pltpu.VMEM((TALL, WIDE, DEPTH), f32),
            pltpu.VMEM((TALL, WIDE, DEPTH), f32),
            pltpu.VMEM((TALL, ROOM, DEPTH), f32),
            pltpu.VMEM((TALL, ROOM, DEPTH), f32),
            pltpu.VMEM((TALL, WIDE, DEPTH), f32),
            pltpu.VMEM((TALL + 2, WIDE, DEPTH), jnp.int32),
            pltpu.VMEM((TALL + 2, WIDE, DEPTH), f32),
            dma((8,)),
            dma((8,)),
            dma((8,)),
            dma((8,)),
            dma((2,)),
            dma((2,)),
            dma,
        ]
        + lane_scratch(1, (EDGE // LANES, EDGE, DEPTH)) * LANES
        + lane_scratch(1, (2, EDGE, DEPTH)) * 2,
        compiler_params=pltpu.CompilerParams(
            collective_id=1, has_side_effects=True, vmem_limit_bytes=28 << 20
        ),
        name="source",
    )(permittivity, routes, charge, fluid_mask, ids, phase)


def back_kernel(me_ref, table_ref, items_ref, ids_ref, others_ref, out_ref, face_ref, *scratch):
    def store(place, row):
        face_ref[pl.ds(place, 1)] = row

    greet([ring(*peer)[2] for peer in RING_PEERS])
    part = PACK // LANES
    lanes = []
    for n in range(LANES):
        rows = slice(n * part, (n + 1) * part)

        def first(_, slot, rows=rows):
            return items_ref[slot, rows]

        def final(here, n=n):
            return out_ref.at[here, :, pl.ds(n * part, part)]

        lanes.append(
            Lane(n % 2, (TO_HOLDER,), table_ref, first, scratch[16 * n : 16 * n + 16], final)
        )
    tables = None
    for stage in range(4):
        for lane in lanes:
            lane.advance(stage)
        if stage == 0:
            tables = face_tables(
                me_ref[0],
                gathered_ids(ids_ref[...]),
                gathered_ids(others_ref[0]),
                gathered_ids(others_ref[1]),
                store,
            )
        next(tables, None)
    for lane in lanes:
        lane.arrived()
    for lane in lanes:
        lane.close()


def send_back(me, routes, packed, ids, others):
    vmem = pl.BlockSpec(memory_space=pltpu.VMEM)
    smem = pl.BlockSpec(memory_space=pltpu.SMEM)
    return pl.pallas_call(
        back_kernel,
        out_shape=(
            jax.ShapeDtypeStruct((TILES, 1, PACK, EDGE, DEPTH), jnp.float32),
            jax.ShapeDtypeStruct((48, DEPTH), jnp.int32),
        ),
        in_specs=[smem, smem, vmem, vmem, vmem],
        out_specs=(vmem, vmem),
        scratch_shapes=lane_scratch(1, (PACK // LANES, EDGE, DEPTH)) * LANES,
        compiler_params=pltpu.CompilerParams(
            collective_id=2, has_side_effects=True, vmem_limit_bytes=24 << 20
        ),
        name="back",
    )(me, routes, packed, ids, others)


FACES = 5


FACE_LANES = (
    (0, (UP_Y, DOWN_Y, SAME_X)),
    (1, (UP_Y, DOWN_Y, SAME_X)),
    (0, (BELOW_X, ABOVE_X)),
    (1, (BELOW_X, ABOVE_X)),
)


def faces_kernel(
    table_ref,
    faces_ref,
    corners_ref,
    out_ref,
    all_ref,
    shifted,
    corner_send,
    corner_recv,
    shift_send,
    shift_recv,
    own_sem,
    *scratch,
):
    me = lax.axis_index("gy")
    peers = [shifted_id(0, k) for k in range(1, GROUPS)]
    bands = [shifted_id(1, 0), shifted_id(-1, 0)]
    greet(peers + bands)
    shifts = []
    for n, target in enumerate(bands):
        copy = pltpu.make_async_remote_copy(
            src_ref=faces_ref.at[:, 3 + n],
            dst_ref=shifted.at[n],
            send_sem=shift_send.at[n],
            recv_sem=shift_recv.at[n],
            device_id=target,
            device_id_type=MESH,
        )
        copy.start()
        shifts.append(copy)
    lanes = []
    for n, (order, perms) in enumerate(FACE_LANES):
        rows = slice(order * 3, order * 3 + 3)

        def first(k, slot, perms=perms, rows=rows):
            if perms[k] < BELOW_X:
                return faces_ref[slot, perms[k], rows]
            return shifted[perms[k] - BELOW_X, slot, rows]

        def final(here, perms=perms, order=order):
            return out_ref.at[here, pl.ds(perms[0], len(perms)), pl.ds(order * 3, 3)]

        lanes.append(Lane(order, perms, table_ref, first, scratch[16 * n : 16 * n + 16], final))
    spread_out, forward = [], []
    own = pltpu.make_async_copy(corners_ref, all_ref.at[0, me], own_sem)
    for stage in range(4):
        for n, lane in enumerate(lanes):
            if stage == 0 and n == 2:
                for k, target in enumerate(peers):
                    copy = pltpu.make_async_remote_copy(
                        src_ref=corners_ref,
                        dst_ref=all_ref.at[0, me],
                        send_sem=corner_send.at[k],
                        recv_sem=corner_recv.at[k],
                        device_id=target,
                        device_id_type=MESH,
                    )
                    copy.start()
                    spread_out.append(copy)
                own.start()
                for copy in shifts:
                    copy.wait_recv()
            lane.advance(stage)
        if stage == 1:
            own.wait()
            for copy in spread_out:
                copy.wait_recv()
            for n, target in enumerate(bands):
                copy = pltpu.make_async_remote_copy(
                    src_ref=all_ref.at[0],
                    dst_ref=all_ref.at[1 + n],
                    send_sem=corner_send.at[GROUPS - 1 + n],
                    recv_sem=corner_recv.at[GROUPS - 1 + n],
                    device_id=target,
                    device_id_type=MESH,
                )
                copy.start()
                forward.append(copy)
    for lane in lanes:
        lane.arrived()
    for copy in forward:
        copy.wait_recv()
    for copy in shifts + spread_out + forward:
        copy.wait_send()
    for lane in lanes:
        lane.close()


def send_faces(routes, faces, corners):
    vmem = pl.BlockSpec(memory_space=pltpu.VMEM)
    f32 = jnp.float32
    dma = pltpu.SemaphoreType.DMA
    scratch = []
    for _, perms in FACE_LANES:
        scratch += lane_scratch(len(perms), (3, EDGE, DEPTH))
    return pl.pallas_call(
        faces_kernel,
        out_shape=(
            jax.ShapeDtypeStruct((TILES, FACES, 6, EDGE, DEPTH), f32),
            jax.ShapeDtypeStruct((3, GROUPS, 2, 8, DEPTH), f32),
        ),
        in_specs=[pl.BlockSpec(memory_space=pltpu.SMEM), vmem, vmem],
        out_specs=(vmem, vmem),
        scratch_shapes=[
            pltpu.VMEM((2, TILES, 6, EDGE, DEPTH), f32),
            dma((GROUPS + 1,)),
            dma((GROUPS + 1,)),
            dma((2,)),
            dma((2,)),
            dma,
        ]
        + scratch,
        compiler_params=pltpu.CompilerParams(
            collective_id=3, has_side_effects=True, vmem_limit_bytes=24 << 20
        ),
        name="faces",
    )(routes, faces, corners)


def collide_rows(pops, charge, field):
    force = [charge * component for component in field]
    sums = {}
    diffs = {}
    for a, b in PAIRS:
        sums[a] = pops[a] + pops[b]
        diffs[a] = pops[a] - pops[b]
    density = pops[0]
    for a, _ in PAIRS:
        density = density + sums[a]
    momentum = [
        diffs[1] + diffs[7] + diffs[9] + diffs[11] + diffs[13],
        diffs[3] + diffs[7] - diffs[9] + diffs[15] + diffs[17],
        diffs[5] + diffs[11] - diffs[13] + diffs[15] - diffs[17],
    ]
    inverse = 1.0 / density
    velocity = [(momentum[d] + 0.5 * force[d]) * inverse for d in range(3)]
    scale = 1.0 - 0.5 / relax_time
    rate = 1.0 / relax_time
    speed = velocity[0] * velocity[0] + velocity[1] * velocity[1] + velocity[2] * velocity[2]
    work = velocity[0] * force[0] + velocity[1] * force[1] + velocity[2] * force[2]
    weighted = rate * density
    base = weighted - (1.5 * weighted) * speed - (3.0 * scale) * work
    odd = [3.0 * weighted * velocity[d] + (3.0 * scale) * force[d] for d in range(3)]
    inner = [4.5 * weighted * velocity[d] + (9.0 * scale) * force[d] for d in range(3)]
    keep = 1.0 - rate
    result = [None] * 19
    result[0] = keep * pops[0] + WEIGHTS[0] * base
    for a, b in PAIRS:
        step = LATTICE[a]
        axes = [d for d in range(3) if step[d] != 0]
        if len(axes) == 1:
            (d,) = axes
            cu, co, ci = velocity[d], odd[d], inner[d]
            weight = WEIGHTS[1]
        else:
            d, e = axes
            weight = WEIGHTS[2]
            if step[d] * step[e] > 0:
                cu, co, ci = velocity[d] + velocity[e], odd[d] + odd[e], inner[d] + inner[e]
            else:
                cu, co, ci = velocity[d] - velocity[e], odd[d] - odd[e], inner[d] - inner[e]
        even = weight * (base + cu * ci)
        lean = weight * co
        result[a] = keep * pops[a] + (even + lean)
        result[b] = keep * pops[b] + (even - lean)
    return result, velocity


def collide_kernel(
    table_ref, routes_ref, pops_ref, charge_ref, mask_ref, pot_ref, out_ref, vel_ref, face_ref, corner_ref, grown
):
    tile = pl.program_id(0)

    def place(i, carry):
        grown[i + 1, pl.ds(8, EDGE)] = pot_ref[0, 0, i]
        grown[i + 1, pl.ds(7, 1)] = pot_ref[0, 0, EDGE + 2, pl.ds(i, 1)]
        grown[i + 1, pl.ds(8 + EDGE, 1)] = pot_ref[0, 0, EDGE + 3, pl.ds(i, 1)]
        return carry

    lax.fori_loop(0, EDGE, place, 0)
    grown[0, pl.ds(8, EDGE)] = pot_ref[0, 0, EDGE]
    grown[EDGE + 1, pl.ds(8, EDGE)] = pot_ref[0, 0, EDGE + 1]
    y_low, y_high = crossing(1, -1), crossing(1, 1)

    def rows(i, carry):
        here = grown[i + 1, pl.ds(8, EDGE)]
        field = [
            0.5 * (grown[i, pl.ds(8, EDGE)] - grown[i + 2, pl.ds(8, EDGE)]),
            0.5 * (grown[i + 1, pl.ds(7, EDGE)] - grown[i + 1, pl.ds(9, EDGE)]),
            0.5 * (pltpu.roll(here, 1, 1) - pltpu.roll(here, DEPTH - 1, 1)),
        ]
        pops = [pops_ref[q, 0, i] for q in range(19)]
        relaxed, velocity = collide_rows(pops, charge_ref[0, i], field)
        fluid = mask_ref[0, i + 1, pl.ds(1, EDGE), :] == 1
        for q in range(19):
            value = jnp.where(fluid, relaxed[q], pops[q])
            out_ref[q, 0, i] = value
            if q in y_low:
                face_ref[0, 1, y_low.index(q), pl.ds(i, 1)] = value[0:1]
            if q in y_high:
                face_ref[0, 0, y_high.index(q), pl.ds(i, 1)] = value[EDGE - 1 :]
        for d in range(3):
            vel_ref[d, 0, i] = velocity[d]
        face_ref[0, 1, 5, pl.ds(i, 1)] = velocity[1][0:1]
        face_ref[0, 0, 5, pl.ds(i, 1)] = velocity[1][EDGE - 1 :]
        return carry

    lax.fori_loop(0, EDGE, rows, 0)

    def x_face(face, sign, layer):
        for k, q in enumerate(crossing(0, sign)):
            face_ref[0, face, k] = out_ref[q, 0, layer]
        face_ref[0, face, 5] = vel_ref[0, 0, layer]

    x_face(3, 1, EDGE - 1)
    x_face(4, -1, 0)

    @pl.when(table_ref[R_ROW, tile] == 0)
    def _():
        x_face(2, 1, EDGE - 1)

    @pl.when(table_ref[R_ROW, tile] == 1)
    def _():
        x_face(2, -1, 0)

    for n, (q, i, j) in enumerate(
        ((7, EDGE - 1, EDGE - 1), (9, EDGE - 1, 0), (10, 0, EDGE - 1), (8, 0, 0))
    ):
        corner_ref[tile // 2, pl.ds(lax.rem(tile, 2) * 4 + n, 1)] = out_ref[q, 0, i, pl.ds(j, 1)]


def collide(table, routes, populations, charge, fluid_mask, returned):
    f32 = jnp.float32
    pot_spec = pl.BlockSpec(
        (1, 1, PACK, EDGE, DEPTH), lambda s, tab, rts: (rts[TO_HOLDER * 8 + K_LAST, s], 0, 0, 0, 0)
    )
    return pl.pallas_call(
        collide_kernel,
        out_shape=(
            jax.ShapeDtypeStruct((19, TILES, EDGE, EDGE, DEPTH), f32),
            jax.ShapeDtypeStruct((3, TILES, EDGE, EDGE, DEPTH), f32),
            jax.ShapeDtypeStruct((TILES, FACES, 6, EDGE, DEPTH), f32),
            jax.ShapeDtypeStruct((2, 8, DEPTH), f32),
        ),
        grid_spec=pltpu.PrefetchScalarGridSpec(
            num_scalar_prefetch=2,
            grid=(TILES,),
            in_specs=[
                pl.BlockSpec((19, 1, EDGE, EDGE, DEPTH), lambda s, tab, rts: (0, s, 0, 0, 0)),
                pl.BlockSpec((1, EDGE, EDGE, DEPTH), lambda s, tab, rts: (s, 0, 0, 0)),
                pl.BlockSpec((1, EDGE + 2, EDGE + 2, DEPTH), lambda s, tab, rts: (s, 0, 0, 0)),
                pot_spec,
            ],
            out_specs=[
                pl.BlockSpec((19, 1, EDGE, EDGE, DEPTH), lambda s, tab, rts: (0, s, 0, 0, 0)),
                pl.BlockSpec((3, 1, EDGE, EDGE, DEPTH), lambda s, tab, rts: (0, s, 0, 0, 0)),
                pl.BlockSpec((1, FACES, 6, EDGE, DEPTH), lambda s, tab, rts: (s, 0, 0, 0, 0)),
                pl.BlockSpec((2, 8, DEPTH), lambda s, tab, rts: (0, 0, 0)),
            ],
            scratch_shapes=[pltpu.VMEM((EDGE + 2, 32, DEPTH), f32)],
        ),
        compiler_params=pltpu.CompilerParams(vmem_limit_bytes=32 << 20),
        name="collide",
    )(table, routes, populations, charge, fluid_mask, returned)


CHARGE, SPEED = 19, 20
SOLID = 3.0e38
FIRST = 8 + EDGE
STRIP = 8 + (EDGE + 2) * EDGE + 8


def stream_kernel(
    table_ref,
    routes_ref,
    relaxed_ref,
    vel_ref,
    charge_ref,
    mask_ref,
    rim_ref,
    *rest,
):
    faces, (corner_ref, pops_out, charge_out, grown, side, sems) = rest[:FACES], rest[FACES:]
    tile = pl.program_id(0)
    here = lax.rem(tile, 2)

    def fetch(t, slot):
        rows = pl.ds(FIRST, EDGE * EDGE)
        return [
            pltpu.make_async_copy(
                relaxed_ref.at[:, t], grown.at[slot, pl.ds(0, 19), rows], sems.at[slot, 0]
            ),
            pltpu.make_async_copy(
                charge_ref.at[t], grown.at[slot, CHARGE, rows], sems.at[slot, 1]
            ),
            pltpu.make_async_copy(
                vel_ref.at[:, t], grown.at[slot, pl.ds(SPEED, 3), rows], sems.at[slot, 2]
            ),
        ]

    @pl.when(tile == 0)
    def _():
        for copy in fetch(0, 0):
            copy.start()

    @pl.when(tile + 1 < TILES)
    def _():
        for copy in fetch(tile + 1, 1 - here):
            copy.start()

    for copy in fetch(tile, here):
        copy.wait()

    cells = grown.at[here]
    before, after = pl.ds(8, EDGE), pl.ds(FIRST + EDGE * EDGE, EDGE)

    def x_rim(face, sign, rows):
        for k, q in enumerate(crossing(0, sign) + [SPEED]):
            cells[q, rows] = faces[face][0, 0, k]

    row = table_ref[R_ROW, tile]

    @pl.when(row == 0)
    def _():
        x_rim(BELOW_X, 1, before)
        x_rim(SAME_X, -1, after)

    @pl.when(row == 1)
    def _():
        x_rim(SAME_X, 1, before)
        x_rim(ABOVE_X, -1, after)

    cells[CHARGE, before] = rim_ref[0, 0, 0]
    cells[CHARGE, after] = rim_ref[0, 0, 1]
    for face, sign, end in ((UP_Y, 1, 0), (DOWN_Y, -1, 1)):
        for k, q in enumerate(crossing(1, sign)):
            side[end, k, pl.ds(1, EDGE)] = faces[face][0, 0, k]
        side[end, 5, pl.ds(1, EDGE)] = faces[face][0, 0, 5]
        side[end, 6, pl.ds(1, EDGE)] = rim_ref[0, 0, 2 + end]
    for n, (q, sign, layer) in enumerate(((7, 1, 0), (9, -1, 0), (10, 1, 17), (8, -1, 17))):
        found = table_ref[R_CORNER + n, tile]
        inside = lax.rem(found, TILES)
        side[n % 2, crossing(1, sign).index(q), pl.ds(layer, 1)] = corner_ref[
            found // TILES, inside // 2, pl.ds(lax.rem(inside, 2) * 4 + n, 1)
        ]
    spot = lax.broadcasted_iota(jnp.int32, (EDGE, DEPTH), 0)
    ends = {-1: spot == 0, 1: spot == EDGE - 1}

    def rows(i, carry):
        def cell(q, di=0, dj=0):
            value = cells[q, pl.ds(i * EDGE + (FIRST + di * EDGE + dj), EDGE)]
            if dj == 0:
                return value
            if q < 19:
                k = crossing(1, -dj).index(q)
            else:
                k = 6 if q == CHARGE else 5
            return jnp.where(ends[dj], side[(dj + 1) // 2, k, pl.ds(i + 1 + di, 1)], value)

        def flag(di=0, dj=0):
            return mask_ref[0, i + 1 + di, pl.ds(1 + dj, EDGE), :]

        own = flag()
        own_fluid = own == 1
        for q in range(19):
            step_x, step_y, step_z = LATTICE[q]
            value = cell(q)
            if q == 0:
                pops_out[q, 0, i] = value
                continue
            moved = cell(q, -step_x, -step_y)
            from_fluid = flag(-step_x, -step_y) == 1
            if step_z != 0:
                moved = pltpu.roll(jnp.where(from_fluid, moved, SOLID), step_z % DEPTH, 1)
                from_fluid = moved < SOLID
            read = jnp.where(from_fluid, moved, cell(opposite(q)))
            pops_out[q, 0, i] = jnp.where(own_fluid, read, value)

        charge = cell(CHARGE)
        weight = own.astype(jnp.float32)

        def flux(speed_a, speed_b, value_a, value_b, flags):
            speed = 0.5 * (speed_a + speed_b)
            return speed * jnp.where(speed > 0, value_a, value_b) * flags

        change = None
        for d, (di, dj) in enumerate(((1, 0), (0, 1))):
            speed = cell(SPEED + d)
            for sign in (1, -1):
                other = cell(CHARGE, sign * di, sign * dj)
                other_speed = cell(SPEED + d, sign * di, sign * dj)
                flags = weight * flag(sign * di, sign * dj).astype(jnp.float32)
                if sign > 0:
                    part = flux(speed, other_speed, charge, other, flags)
                    change = part if change is None else change + part
                else:
                    change = change - flux(other_speed, speed, other, charge, flags)
        speed = cell(SPEED + 2)
        next_charge = pltpu.roll(jnp.where(own_fluid, charge, SOLID), DEPTH - 1, 1)
        middle = 0.5 * (speed + pltpu.roll(speed, DEPTH - 1, 1))
        over = middle * jnp.where(middle > 0, charge, next_charge)
        over = jnp.where(own_fluid & (next_charge < SOLID), over, 0.0)
        change = change + over - pltpu.roll(over, 1, 1)
        charge_out[0, i] = jnp.where(own_fluid, charge - change, charge)
        return carry

    lax.fori_loop(0, EDGE, rows, 0, unroll=2)


def stream(table, routes, relaxed, velocity, charge, fluid_mask, returned, faces, corners):
    f32 = jnp.float32
    face_specs = [
        pl.BlockSpec(
            (1, 1, 6, EDGE, DEPTH),
            lambda s, tab, rts, face=face: (tab[face * 8 + K_LAST, s], face, 0, 0, 0),
        )
        for face in range(FACES)
    ]
    anywhere = pl.BlockSpec(memory_space=pl.ANY)
    return pl.pallas_call(
        stream_kernel,
        out_shape=(
            jax.ShapeDtypeStruct((19, TILES, EDGE, EDGE, DEPTH), f32),
            jax.ShapeDtypeStruct((TILES, EDGE, EDGE, DEPTH), f32),
        ),
        grid_spec=pltpu.PrefetchScalarGridSpec(
            num_scalar_prefetch=2,
            grid=(TILES,),
            in_specs=[
                anywhere,
                anywhere,
                anywhere,
                pl.BlockSpec((1, EDGE + 2, EDGE + 2, DEPTH), lambda s, tab, rts: (s, 0, 0, 0)),
                pl.BlockSpec(
                    (1, 1, 4, EDGE, DEPTH),
                    lambda s, tab, rts: (rts[TO_HOLDER * 8 + K_LAST, s], 0, 0, 0, 0),
                ),
            ]
            + face_specs
            + [pl.BlockSpec((3 * GROUPS, 2, 8, DEPTH), lambda s, tab, rts: (0, 0, 0, 0))],
            out_specs=[
                pl.BlockSpec((19, 1, EDGE, EDGE, DEPTH), lambda s, tab, rts: (0, s, 0, 0, 0)),
                pl.BlockSpec((1, EDGE, EDGE, DEPTH), lambda s, tab, rts: (s, 0, 0, 0)),
            ],
            scratch_shapes=[
                pltpu.VMEM((2, 23, STRIP, DEPTH), f32),
                pltpu.VMEM((2, 7, 24, DEPTH), f32),
                pltpu.SemaphoreType.DMA((2, 3)),
            ],
        ),
        compiler_params=pltpu.CompilerParams(vmem_limit_bytes=32 << 20),
        name="stream",
    )(
        table,
        routes,
        relaxed.reshape(19, TILES, EDGE * EDGE, DEPTH),
        velocity.reshape(3, TILES, EDGE * EDGE, DEPTH),
        charge.reshape(TILES, EDGE * EDGE, DEPTH),
        fluid_mask,
        returned,
        *([faces] * FACES),
        corners.reshape(3 * GROUPS, 2, 8, DEPTH),
    )


def per_device(populations, charge, fluid_mask, tile_ids, phase_label, permittivity):
    me = lax.axis_index("gy").astype(jnp.int32).reshape(1)
    place = jnp.arange(8 * DEPTH, dtype=jnp.int32).reshape(8, DEPTH)
    ids_row = jnp.where(place // TILES == me, jnp.tile(tile_ids, 2 * DEPTH).reshape(8, DEPTH), 0)
    ids = exchange_start(ids_row)
    routes = make_routes(owner_routes_kernel, 16, me, ids)
    potential, packed, others, charge_rims = find_potential(
        permittivity, routes, charge, fluid_mask, ids, phase_label
    )
    returned, table = send_back(me, routes, packed, ids, others)
    relaxed, velocity, faces, corners = collide(
        table, routes, populations, charge, fluid_mask, returned
    )
    rims, all_corners = send_faces(table, faces, corners)
    populations_next, charge_next = stream(
        table, routes, relaxed, velocity, charge, fluid_mask, charge_rims, rims, all_corners
    )
    return (populations_next, charge_next, potential)


def solution(mesh):
    placed = (
        P(None, ("gx", "gy"), None, None, None),
        P(("gx", "gy"), None, None, None),
        P(("gx", "gy"), None, None, None),
        P(("gx", "gy")),
        P("gx", "gy", None),
        P(),
    )
    return jax.shard_map(
        per_device,
        mesh=mesh,
        in_specs=placed,
        out_specs=(
            P(None, ("gx", "gy"), None, None, None),
            P(("gx", "gy"), None, None, None),
            P("gx", "gy", None),
        ),
        check_vma=False,
    )
```

```python
import functools

import jax
import jax.numpy as jnp
from jax import lax
from jax.experimental import pallas as pl
from jax.experimental.pallas import tpu as pltpu
from jax.sharding import PartitionSpec as P

EDGE = 16
DEPTH = 128
BLOCK = 32
PHASES = 4
SWEEPS = 4
UNROLL = 2
TILES = 4
GROUPS = 16
BANDS = 8
COLS = 32
SIDE = 8
MESH = pl.DeviceIdType.MESH

LATTICE = (
    (0, 0, 0),
    (1, 0, 0),
    (-1, 0, 0),
    (0, 1, 0),
    (0, -1, 0),
    (0, 0, 1),
    (0, 0, -1),
    (1, 1, 0),
    (-1, -1, 0),
    (1, -1, 0),
    (-1, 1, 0),
    (1, 0, 1),
    (-1, 0, -1),
    (1, 0, -1),
    (-1, 0, 1),
    (0, 1, 1),
    (0, -1, -1),
    (0, 1, -1),
    (0, -1, 1),
)
WEIGHTS = (1.0 / 3.0, 1.0 / 18.0, 1.0 / 36.0)
PAIRS = ((1, 2), (3, 4), (5, 6), (7, 8), (9, 10), (11, 12), (13, 14), (15, 16), (17, 18))
relax_time = 0.8
screening = 0.001
spectrum_low = 0.1
spectrum_high = 2.0

AROUND = tuple((dx, dy) for dx in (-1, 0, 1) for dy in (-1, 0, 1) if (dx, dy) != (0, 0))

TO_OWNER, TO_HOLDER = 0, 1
UP_Y, DOWN_Y, SAME_X, BELOW_X, ABOVE_X = range(5)
R_ROW, R_CORNER = 40, 41


def opposite(direction):
    return LATTICE.index(tuple(-entry for entry in LATTICE[direction]))


def crossing(axis_index, face_sign):
    return [d for d in range(19) if LATTICE[d][axis_index] == face_sign]


def shifted_id(dx, dy):
    gx = lax.rem(lax.axis_index("gx") + dx + BANDS, BANDS)
    gy = lax.rem(lax.axis_index("gy") + dy + GROUPS, GROUPS)
    return {"gx": gx, "gy": gy}


def span(step, width, pad):
    if step == 0:
        return pl.ds(0, BLOCK), pl.ds(pad, BLOCK)
    if step > 0:
        return pl.ds(BLOCK - width, width), pl.ds(pad - width, width)
    return pl.ds(0, width), pl.ds(pad + BLOCK, width)


def halo_copies(block_ref, ext_ref, width, send_sem, recv_sem):
    copies = []
    for n, (dx, dy) in enumerate(AROUND):
        src_i, dst_i = span(dx, width, width)
        src_j, dst_j = span(dy, SIDE, SIDE)
        copies.append(
            pltpu.make_async_remote_copy(
                src_ref=block_ref.at[src_i, src_j],
                dst_ref=ext_ref.at[dst_i, dst_j],
                send_sem=send_sem.at[n],
                recv_sem=recv_sem.at[n],
                device_id=shifted_id(dx, dy),
                device_id_type=MESH,
            )
        )
    return copies


def greet(targets):
    barrier = pltpu.get_barrier_semaphore()
    for target in targets:
        pl.semaphore_signal(barrier, inc=1, device_id=target, device_id_type=MESH)
    pl.semaphore_wait(barrier, len(targets))


def start_kernel(ids_ref, all_ref, ids_send, ids_recv, own_sem):
    me = lax.axis_index("gy")
    peers = [shifted_id(0, k) for k in range(1, GROUPS)]
    greet(peers)
    started = []
    for k, target in enumerate(peers):
        copy = pltpu.make_async_remote_copy(
            src_ref=ids_ref,
            dst_ref=all_ref.at[me],
            send_sem=ids_send.at[k],
            recv_sem=ids_recv.at[k],
            device_id=target,
            device_id_type=MESH,
        )
        copy.start()
        started.append(copy)
    own = pltpu.make_async_copy(ids_ref, all_ref.at[me], own_sem)
    own.start()
    own.wait()
    for copy in started:
        copy.wait()


def exchange_start(ids):
    vmem = pl.BlockSpec(memory_space=pltpu.VMEM)
    dma = pltpu.SemaphoreType.DMA
    return pl.pallas_call(
        start_kernel,
        out_shape=jax.ShapeDtypeStruct((GROUPS, 8, DEPTH), jnp.int32),
        in_specs=[vmem],
        out_specs=vmem,
        scratch_shapes=[dma((GROUPS - 1,)), dma((GROUPS - 1,)), dma],
        compiler_params=pltpu.CompilerParams(
            collective_id=0, has_side_effects=True, vmem_limit_bytes=8 << 20
        ),
        name="start",
    )(ids)


WIDE = BLOCK + 2 * SIDE
TALL = BLOCK + 8
ROOM = WIDE + 16
INNER = pl.ds(8, WIDE)
BEFORE = pl.ds(7, WIDE)
AFTER = pl.ds(9, WIDE)
PACK = 20
FACES = 5


def harmonic(left, right):
    return 2.0 * left * right / (left + right)


def look_up_rows(permit_ref, phase_ref, permit):
    def look_up(i, carry):
        label = phase_ref[i]
        value = jnp.where(label == 0, permit_ref[0], 0.0)
        for k in range(1, PHASES):
            value = jnp.where(label == k, permit_ref[k], value)
        permit[i] = value
        return carry

    lax.fori_loop(0, TALL + 2, look_up, 0)


def weigh_rows(begin, end, permit, coef, scale_ref):
    def weigh(i, below):
        here = permit[i + 1]
        above = harmonic(here, permit[i + 2])
        right = harmonic(here, pltpu.roll(here, WIDE - 1, 0))
        left = pltpu.roll(right, 1, 0)
        up = harmonic(here, pltpu.roll(here, DEPTH - 1, 1))
        down = pltpu.roll(up, 1, 1)
        scale = 1.0 / (above + below + right + left + up + down + screening)
        for k, weight in enumerate((above, below, right, left, up, down)):
            coef[k, i] = weight * scale
        scale_ref[i] = scale
        return above

    lax.fori_loop(begin, end, weigh, harmonic(permit[begin], permit[begin + 1]), unroll=2)


def tile_corner(t):
    return 4 + (t // 2) * EDGE, SIDE + (t % 2) * EDGE


def pack_rims(out, place, ref):
    for t in range(TILES):
        i0, j0 = tile_corner(t)

        def rows(i, carry, t=t, i0=i0, j0=j0):
            out[t, place + 2, pl.ds(i, 1)] = ref[i0 + i, pl.ds(j0 - 1, 1)]
            out[t, place + 3, pl.ds(i, 1)] = ref[i0 + i, pl.ds(j0 + EDGE, 1)]
            return carry

        lax.fori_loop(0, EDGE, rows, 0, unroll=4)
        out[t, place] = ref[i0 - 1, pl.ds(j0, EDGE)]
        out[t, place + 1] = ref[i0 + EDGE, pl.ds(j0, EDGE)]


def sweep_rows(coef, scale_ref, source_ref, pot_ref, pack, resid, upd_a, upd_b, total, between):
    center = 0.5 * (spectrum_high + spectrum_low)
    half = 0.5 * (spectrum_high - spectrum_low)
    ratio = center / half

    def begin(i, carry):
        value = source_ref[i] * scale_ref[i]
        resid[i] = value
        value = value * (1.0 / center)
        upd_a[i, INNER] = value
        total[i] = value
        return carry

    lax.fori_loop(0, TALL, begin, 0, unroll=2)
    rho = 1.0 / ratio
    old, new = upd_a, upd_b
    for sweep in range(SWEEPS - 1):
        between(sweep + 1)
        rho_new = 1.0 / (2.0 * ratio - rho)
        keep, gain = rho_new * rho, 2.0 * rho_new / half

        def relax(i, carry, old=old, new=new, keep=keep, gain=gain):
            here = old[i, INNER]
            near = coef[0, i] * old[i + 1, INNER] + coef[1, i] * old[i - 1, INNER]
            near += coef[2, i] * old[i, AFTER] + coef[3, i] * old[i, BEFORE]
            near += coef[4, i] * pltpu.roll(here, DEPTH - 1, 1)
            near += coef[5, i] * pltpu.roll(here, 1, 1)
            left = resid[i] - here + near
            resid[i] = left
            here = keep * here + gain * left
            new[i, INNER] = here
            total[i] = total[i] + here
            return carry

        lax.fori_loop(sweep + 1, TALL - 1 - sweep, relax, 0, unroll=UNROLL)
        old, new = new, old
        rho = rho_new

    def emit(i, carry):
        pot_ref[i] = total[i + 4, pl.ds(SIDE, BLOCK)]
        return carry

    lax.fori_loop(0, BLOCK, emit, 0, unroll=4)
    for t in range(TILES):
        i0, j0 = tile_corner(t)

        def rows(i, carry, t=t, i0=i0, j0=j0):
            pack[t, i] = total[i0 + i, pl.ds(j0, EDGE)]
            return carry

        lax.fori_loop(0, EDGE, rows, 0, unroll=4)
    pack_rims(pack, EDGE, total)


K_FIRST, K_X2, K_X3, K_X4, K_Y2, K_Y3, K_Y4, K_LAST = range(8)
PORTS = 64


def to_column(row, eye):
    return jnp.sum(jnp.where(eye, row, 0), axis=1, keepdims=True)


def split_edges(left, right, sub, lane, doublings):
    def partners(ends):
        same = ends[0] == ends[1]
        before = jnp.where(same & (lane < sub), 1, 0)
        after = jnp.where(same & (sub < lane), 1, 0)
        rank_c = jnp.sum(before, axis=1, keepdims=True)
        rank_r = jnp.sum(after, axis=0, keepdims=True)
        pair = same & ((rank_c >> 1) == (rank_r >> 1)) & (sub != lane)
        return jnp.where(pair, 1.0, 0.0).astype(jnp.bfloat16)

    def times(a, b):
        return jnp.dot(a, b, preferred_element_type=jnp.float32)

    by_left, by_right = partners(left), partners(right)
    reach = times(by_left, by_right) + times(by_right, by_left)
    reach = jnp.where((sub == lane) | (reach > 0.0), 1.0, 0.0).astype(jnp.bfloat16)
    for _ in range(doublings):
        reach = jnp.where(times(reach, reach) > 0.0, 1.0, 0.0).astype(jnp.bfloat16)
    mate = times(by_left, reach) > 0.0
    own = reach.astype(jnp.float32) > 0.0
    size = sub.shape[0]
    col = jnp.where(
        jnp.min(jnp.where(own, lane, size), axis=1, keepdims=True)
        > jnp.min(jnp.where(mate, lane, size), axis=1, keepdims=True),
        1,
        0,
    )
    row = jnp.where(
        jnp.min(jnp.where(own, sub, size), axis=0, keepdims=True)
        > jnp.min(jnp.where(mate, sub, size), axis=0, keepdims=True),
        1,
        0,
    )
    return col, row


def join(first, second, base):
    return tuple(a * base + b for a, b in zip(first, second))


def colour(left, right, sub, lane, doublings):
    high = split_edges(left, right, sub, lane, doublings)
    low = split_edges(join(left, high, 2), join(right, high, 2), sub, lane, doublings - 1)
    return join(high, low, 2)


class Ports:
    def __init__(self, size):
        self.size = size
        self.sub = lax.broadcasted_iota(jnp.int32, (size, size), 0)
        self.lane = lax.broadcasted_iota(jnp.int32, (size, size), 1)
        self.eye = self.sub == self.lane
        edge = (
            lax.broadcasted_iota(jnp.int32, (size, 1), 0),
            lax.broadcasted_iota(jnp.int32, (1, size), 1),
        )
        self.port = tuple(e & (PORTS - 1) for e in edge)
        self.half = tuple(e >> 6 for e in edge)
        self.device = tuple(e >> 2 for e in self.port)
        self.entry = lax.broadcasted_iota(jnp.int32, (size, DEPTH), 1)


def store_routes(me, ports, places, goal_ids, target, store):
    half, port, device = ports.half, ports.port, ports.device
    sub, lane = ports.sub, ports.lane
    my_row, my_col = me >> 2, me & 3
    at = to_column(goal_ids, ports.eye) + half[0] * PORTS
    target = target + half[1] * PORTS
    drop = jnp.sum(jnp.where(at == target, sub & (PORTS - 1), 0), axis=0, keepdims=True)
    drop = (to_column(drop, ports.eye), drop)
    goal = tuple(d >> 2 for d in drop)
    begin = tuple(h * GROUPS + d for h, d in zip(half, device))
    end = tuple(h * GROUPS + d for h, d in zip(half, goal))
    j = colour(begin, end, sub, lane, 4)
    group = tuple(h * 4 + c for h, c in zip(half, j))
    rows = (tuple(d >> 2 for d in device), tuple(d >> 2 for d in goal))
    cols = (tuple(d & 3 for d in device), tuple(d & 3 for d in goal))
    b = colour(join(group, rows[0], 4), join(group, rows[1], 4), sub, lane, 2)[0]
    g = colour(join(group, cols[0], 4), join(group, cols[1], 4), sub, lane, 2)[0]
    j = j[0]
    slots = (port[0] & 3, drop[0] & 3)
    ends = (device[0], goal[0])
    rows, cols = tuple(r[0] for r in rows), tuple(c[0] for c in cols)
    for perm, h, back in places:
        mine = half[0] == h
        src, dst = (1, 0) if back else (0, 1)
        for kind, given, key, value in (
            (K_FIRST, ends[src] == me, j, slots[src]),
            (K_X2, (rows[src] == my_row) & (j == my_col), b, cols[src]),
            (K_X3, (j == my_col) & (b == my_row), rows[dst], rows[src]),
            (K_X4, (j == my_col) & (rows[dst] == my_row), cols[dst], b),
            (K_Y2, (cols[src] == my_col) & (j == my_row), g, rows[src]),
            (K_Y3, (j == my_row) & (g == my_col), cols[dst], cols[src]),
            (K_Y4, (j == my_row) & (cols[dst] == my_col), rows[dst], g),
            (K_LAST, ends[dst] == me, slots[dst], j),
        ):
            kept = jnp.where(mine & given, value, 0)
            found = jnp.where(key == ports.entry, kept, 0)
            store(perm * 8 + kind, jnp.sum(found, axis=0, keepdims=True))


def owner_tables(me, own, store):
    ports = Ports(PORTS)
    owner = (ports.port[1] & 3) // 2 * COLS + ports.device[1] * 2 + (ports.port[1] & 1)
    places = ((TO_OWNER, 0, True), (TO_HOLDER, 0, False))
    store_routes(me, ports, places, own[:, :PORTS], owner, store)


def face_tables(me, own, below, above, store):
    ports = Ports(2 * PORTS)
    half = ports.half

    def turn(pos, step):
        return (pos & COLS) + ((pos + step) & (COLS - 1))

    def both(first, second):
        return jnp.where(half[1] == 0, first, pltpu.roll(second, PORTS, 1))

    twice = both(own, own)
    places = ((UP_Y, 0, False), (DOWN_Y, 0, True), (SAME_X, 1, False))
    store_routes(me, ports, places, twice, both(turn(own, 1), own ^ COLS), store)
    yield
    places = ((BELOW_X, 0, False), (ABOVE_X, 1, False))
    store_routes(me, ports, places, twice, both(below ^ COLS, above ^ COLS), store)
    yield
    mine = jnp.sum(
        jnp.where((ports.sub == me * TILES + ports.lane) & (ports.lane < TILES), to_column(own, ports.eye), 0),
        axis=0,
        keepdims=True,
    )
    store(R_ROW, mine >> 5)
    found = []
    for band in (own, below, above):
        at = to_column(band, ports.eye)
        for step in (-1, 1):
            there = (at == turn(mine ^ COLS, step)) & (ports.sub < PORTS)
            found.append(jnp.sum(jnp.where(there, ports.sub, 0), axis=0, keepdims=True))
    upper = (mine >> 5) == 1
    for n in range(2):
        store(R_CORNER + n, jnp.where(upper, found[n], found[2 + n] + PORTS))
        store(R_CORNER + 2 + n, jnp.where(upper, found[4 + n] + 2 * PORTS, found[n]))


def gathered_ids(ids):
    return jnp.sum(ids, axis=0)[0:1]


def owner_routes_kernel(me_ref, ids_ref, out_ref):
    def store(place, row):
        out_ref[pl.ds(place, 1)] = row

    owner_tables(me_ref[0], gathered_ids(ids_ref[...]), store)


def make_routes(kernel, rows, me, *ids):
    vmem = pl.BlockSpec(memory_space=pltpu.VMEM)
    return pl.pallas_call(
        kernel,
        out_shape=jax.ShapeDtypeStruct((rows, DEPTH), jnp.int32),
        in_specs=[pl.BlockSpec(memory_space=pltpu.SMEM)] + [vmem] * len(ids),
        out_specs=vmem,
        compiler_params=pltpu.CompilerParams(vmem_limit_bytes=8 << 20),
        name=kernel.__name__,
    )(me, *ids)


def ring(axis, step):
    gy = lax.axis_index("gy")
    row, col = gy // 4, lax.rem(gy, 4)
    if axis == 0:
        place = lax.rem(col + step, 4)
        return col, place, {"gx": lax.axis_index("gx"), "gy": row * 4 + place}
    place = lax.rem(row + step, 4)
    return row, place, {"gx": lax.axis_index("gx"), "gy": place * 4 + col}


RING_AXES = ((0, 1, 1, 0), (1, 0, 0, 1))
RING_KINDS = ((K_FIRST, K_X2, K_X3, K_X4), (K_FIRST, K_Y2, K_Y3, K_Y4))


class Lane:
    def __init__(self, order, perms, table_ref, first, scratch, final=None):
        self.order, self.perms, self.table_ref = order, perms, table_ref
        self.first, self.final = first, final
        self.stages = [scratch[4 * n : 4 * n + 4] for n in range(4)]
        self.waiting, self.sent = [], []

    def arrived(self):
        for copy in self.waiting:
            copy.wait_recv()
        self.waiting = []

    def target(self, stage, here):
        if stage == 3 and self.final is not None:
            return self.final(here)
        return self.stages[stage][1].at[here]

    def advance(self, stage):
        self.arrived()
        send, _, send_sem, recv_sem = self.stages[stage]
        for step in (2, 1, 3, 0):
            here, place, target = ring(RING_AXES[self.order][stage], step)
            landing = self.target(stage, here)
            for n, perm in enumerate(self.perms):
                slot = self.table_ref[perm * 8 + RING_KINDS[self.order][stage], place]
                if stage:
                    value = self.stages[stage - 1][1][slot, n]
                else:
                    value = self.first(n, slot)
                if step:
                    send[step - 1, n] = value
                else:
                    landing[n] = value
            if step:
                copy = pltpu.make_async_remote_copy(
                    src_ref=send.at[step - 1],
                    dst_ref=landing,
                    send_sem=send_sem.at[step - 1],
                    recv_sem=recv_sem.at[step - 1],
                    device_id=target,
                    device_id_type=MESH,
                )
                copy.start()
                self.waiting.append(copy)
                self.sent.append(copy)

    def close(self):
        for copy in self.sent:
            copy.wait_send()


def lane_scratch(items, shape):
    scratch = []
    for stage in range(4):
        scratch += [
            pltpu.VMEM((3, items) + shape, jnp.float32),
            pltpu.VMEM((4, items) + shape, jnp.float32),
            pltpu.SemaphoreType.DMA((3,)),
            pltpu.SemaphoreType.DMA((3,)),
        ]
    return scratch


RING_PEERS = tuple((axis, step) for axis in range(2) for step in (1, 2, 3))
LANES = 4


def source_kernel(
    permit_ref,
    table_ref,
    charge_hbm,
    mask_hbm,
    ids_ref,
    phase_ref,
    pot_ref,
    pack_ref,
    others,
    rims_ref,
    charge_ref,
    mask_ref,
    fetch_sem,
    rims,
    ext_ref,
    coef_ref,
    scale_ref,
    resid,
    upd_a,
    upd_b,
    total,
    phase_ext,
    permit,
    send_sem,
    recv_sem,
    phase_send,
    phase_recv,
    ids_send,
    ids_recv,
    own_sem,
    *scratch,
):
    bands = [shifted_id(1, 0), shifted_id(-1, 0)]
    fetches = [
        pltpu.make_async_copy(charge_hbm, charge_ref, fetch_sem.at[0]),
        pltpu.make_async_copy(mask_hbm, mask_ref, fetch_sem.at[1]),
        pltpu.make_async_copy(
            phase_ref, phase_ext.at[pl.ds(5, BLOCK), pl.ds(SIDE, BLOCK)], own_sem
        ),
    ]
    for copy in fetches:
        copy.start()
    greet([ring(*peer)[2] for peer in RING_PEERS] + [shifted_id(dx, dy) for dx, dy in AROUND])
    for copy in fetches:
        copy.wait()
    part = EDGE // LANES
    lanes = []
    for n in range(LANES):

        def first(_, slot, n=n):
            flags = mask_ref[slot, 1 + n * part : 1 + (n + 1) * part, 1 : EDGE + 1]
            return charge_ref[slot, n * part : (n + 1) * part] * flags.astype(jnp.float32)

        lanes.append(
            Lane(n % 2, (TO_OWNER,), table_ref, first, scratch[16 * n : 16 * n + 16])
        )
    passed = []
    phases = halo_copies(phase_ref, phase_ext, 5, phase_send, phase_recv)

    def weights(begin, end):
        weigh_rows(begin, end, permit, coef_ref, scale_ref)

    for stage in range(4):
        for lane in lanes:
            lane.advance(stage)
        if stage == 0:
            for copy in phases:
                copy.start()
            for n, target in enumerate(bands):
                copy = pltpu.make_async_remote_copy(
                    src_ref=ids_ref,
                    dst_ref=others.at[n],
                    send_sem=ids_send.at[n],
                    recv_sem=ids_recv.at[n],
                    device_id=target,
                    device_id_type=MESH,
                )
                copy.start()
                passed.append(copy)
        elif stage == 1:
            for copy in phases:
                copy.wait_recv()
            look_up_rows(permit_ref, phase_ext, permit)
            weights(0, 8)
        elif stage == 2:
            weights(8, 18)
        else:
            weights(18, 30)
    for n, lane in enumerate(lanes):
        lane.arrived()
        final = lane.stages[3][1]
        for t in range(TILES):
            i0, j0 = 4 + (t // 2) * EDGE + n * part, SIDE + (t % 2) * EDGE
            ext_ref[i0 : i0 + part, j0 : j0 + EDGE] = final[
                table_ref[TO_OWNER * 8 + K_LAST, t], 0
            ]
    block = ext_ref.at[pl.ds(4, BLOCK), pl.ds(SIDE, BLOCK)]
    copies = halo_copies(block, ext_ref, 4, send_sem, recv_sem)
    for copy in copies:
        copy.start()
    weights(30, TALL)
    for copy in copies + passed:
        copy.wait()
    for copy in phases:
        copy.wait_send()
    pack_rims(rims, 0, ext_ref)
    returning = []
    for n in range(2):

        def first(_, slot, n=n):
            return rims[slot, 2 * n : 2 * n + 2]

        def final(here, n=n):
            return rims_ref.at[here, :, pl.ds(2 * n, 2)]

        refs = scratch[16 * (LANES + n) : 16 * (LANES + n) + 16]
        returning.append(Lane(n, (TO_HOLDER,), table_ref, first, refs, final))

    def between(stage):
        for lane in returning:
            lane.advance(stage)

    between(0)
    sweep_rows(
        coef_ref, scale_ref, ext_ref, pot_ref, pack_ref, resid, upd_a, upd_b, total, between
    )
    for lane in returning:
        lane.arrived()
    for lane in lanes + returning:
        lane.close()


def find_potential(permittivity, routes, charge, fluid_mask, ids, phase):
    vmem = pl.BlockSpec(memory_space=pltpu.VMEM)
    smem = pl.BlockSpec(memory_space=pltpu.SMEM)
    anywhere = pl.BlockSpec(memory_space=pltpu.HBM)
    dma = pltpu.SemaphoreType.DMA
    f32 = jnp.float32
    return pl.pallas_call(
        source_kernel,
        out_shape=(
            jax.ShapeDtypeStruct((BLOCK, BLOCK, DEPTH), f32),
            jax.ShapeDtypeStruct((TILES, PACK, EDGE, DEPTH), f32),
            jax.ShapeDtypeStruct((2, GROUPS, 8, DEPTH), jnp.int32),
            jax.ShapeDtypeStruct((TILES, 1, 4, EDGE, DEPTH), f32),
            jax.ShapeDtypeStruct((TILES, EDGE, EDGE, DEPTH), f32),
            jax.ShapeDtypeStruct((TILES, EDGE + 2, EDGE + 2, DEPTH), jnp.int32),
        ),
        in_specs=[smem] * 2 + [anywhere, anywhere, vmem, anywhere],
        out_specs=(vmem,) * 6,
        scratch_shapes=[
            dma((2,)),
            pltpu.VMEM((TILES, 4, EDGE, DEPTH), f32),
            pltpu.VMEM((TALL, WIDE, DEPTH), f32),
            pltpu.VMEM((6, TALL, WIDE, DEPTH), f32),
            pltpu.VMEM((TALL, WIDE, DEPTH), f32),
            pltpu.VMEM((TALL, WIDE, DEPTH), f32),
            pltpu.VMEM((TALL, ROOM, DEPTH), f32),
            pltpu.VMEM((TALL, ROOM, DEPTH), f32),
            pltpu.VMEM((TALL, WIDE, DEPTH), f32),
            pltpu.VMEM((TALL + 2, WIDE, DEPTH), jnp.int32),
            pltpu.VMEM((TALL + 2, WIDE, DEPTH), f32),
            dma((8,)),
            dma((8,)),
            dma((8,)),
            dma((8,)),
            dma((2,)),
            dma((2,)),
            dma,
        ]
        + lane_scratch(1, (EDGE // LANES, EDGE, DEPTH)) * LANES
        + lane_scratch(1, (2, EDGE, DEPTH)) * 2,
        compiler_params=pltpu.CompilerParams(
            collective_id=1, has_side_effects=True, vmem_limit_bytes=28 << 20
        ),
        name="source",
    )(permittivity, routes, charge, fluid_mask, ids, phase)


def back_kernel(
    me_ref,
    table_ref,
    items_ref,
    ids_ref,
    others_ref,
    pops_hbm,
    out_ref,
    face_ref,
    pops_ref,
    pops_sem,
    *scratch,
):
    fetches = [
        pltpu.make_async_copy(pops_hbm.at[:, t], pops_ref.at[:, t], pops_sem.at[t])
        for t in range(TILES)
    ]
    for copy in fetches:
        copy.start()

    def store(place, row):
        face_ref[pl.ds(place, 1)] = row

    greet([ring(*peer)[2] for peer in RING_PEERS])
    part = PACK // LANES
    lanes = []
    for n in range(LANES):
        rows = slice(n * part, (n + 1) * part)

        def first(_, slot, rows=rows):
            return items_ref[slot, rows]

        def final(here, n=n):
            return out_ref.at[here, :, pl.ds(n * part, part)]

        lanes.append(
            Lane(n % 2, (TO_HOLDER,), table_ref, first, scratch[16 * n : 16 * n + 16], final)
        )
    tables = None
    for stage in range(4):
        for lane in lanes:
            lane.advance(stage)
        if stage == 0:
            tables = face_tables(
                me_ref[0],
                gathered_ids(ids_ref[...]),
                gathered_ids(others_ref[0]),
                gathered_ids(others_ref[1]),
                store,
            )
        next(tables, None)
    for lane in lanes:
        lane.arrived()
    for lane in lanes:
        lane.close()
    for copy in fetches:
        copy.wait()


def send_back(me, routes, packed, ids, others, populations):
    vmem = pl.BlockSpec(memory_space=pltpu.VMEM)
    smem = pl.BlockSpec(memory_space=pltpu.SMEM)
    return pl.pallas_call(
        back_kernel,
        out_shape=(
            jax.ShapeDtypeStruct((TILES, 1, PACK, EDGE, DEPTH), jnp.float32),
            jax.ShapeDtypeStruct((48, DEPTH), jnp.int32),
            jax.ShapeDtypeStruct((19, TILES, EDGE, EDGE, DEPTH), jnp.float32),
        ),
        in_specs=[smem, smem, vmem, vmem, vmem, pl.BlockSpec(memory_space=pltpu.HBM)],
        out_specs=(vmem, vmem, vmem),
        scratch_shapes=[pltpu.SemaphoreType.DMA((TILES,))]
        + lane_scratch(1, (PACK // LANES, EDGE, DEPTH)) * LANES,
        compiler_params=pltpu.CompilerParams(
            collective_id=2, has_side_effects=True, vmem_limit_bytes=40 << 20
        ),
        name="back",
    )(me, routes, packed, ids, others, populations)


def collide_rows(pops, charge, field):
    force = [charge * component for component in field]
    sums = {}
    diffs = {}
    for a, b in PAIRS:
        sums[a] = pops[a] + pops[b]
        diffs[a] = pops[a] - pops[b]
    density = pops[0]
    for a, _ in PAIRS:
        density = density + sums[a]
    momentum = [
        diffs[1] + diffs[7] + diffs[9] + diffs[11] + diffs[13],
        diffs[3] + diffs[7] - diffs[9] + diffs[15] + diffs[17],
        diffs[5] + diffs[11] - diffs[13] + diffs[15] - diffs[17],
    ]
    inverse = 1.0 / density
    velocity = [(momentum[d] + 0.5 * force[d]) * inverse for d in range(3)]
    scale = 1.0 - 0.5 / relax_time
    rate = 1.0 / relax_time
    speed = velocity[0] * velocity[0] + velocity[1] * velocity[1] + velocity[2] * velocity[2]
    work = velocity[0] * force[0] + velocity[1] * force[1] + velocity[2] * force[2]
    weighted = rate * density
    base = weighted - (1.5 * weighted) * speed - (3.0 * scale) * work
    odd = [3.0 * weighted * velocity[d] + (3.0 * scale) * force[d] for d in range(3)]
    inner = [4.5 * weighted * velocity[d] + (9.0 * scale) * force[d] for d in range(3)]
    keep = 1.0 - rate
    result = [None] * 19
    result[0] = keep * pops[0] + WEIGHTS[0] * base
    for a, b in PAIRS:
        step = LATTICE[a]
        axes = [d for d in range(3) if step[d] != 0]
        if len(axes) == 1:
            (d,) = axes
            cu, co, ci = velocity[d], odd[d], inner[d]
            weight = WEIGHTS[1]
        else:
            d, e = axes
            weight = WEIGHTS[2]
            if step[d] * step[e] > 0:
                cu, co, ci = velocity[d] + velocity[e], odd[d] + odd[e], inner[d] + inner[e]
            else:
                cu, co, ci = velocity[d] - velocity[e], odd[d] - odd[e], inner[d] - inner[e]
        even = weight * (base + cu * ci)
        lean = weight * co
        result[a] = keep * pops[a] + (even + lean)
        result[b] = keep * pops[b] + (even - lean)
    return result, velocity


PITCH = 32


def place_potential(grown, pot_ref, slot):
    def place(i, carry):
        start = (i + 1) * PITCH
        grown[pl.ds(start + 8, EDGE)] = pot_ref[slot, 0, i]
        grown[pl.ds(start + 7, 1)] = pot_ref[slot, 0, EDGE + 2, pl.ds(i, 1)]
        grown[pl.ds(start + 8 + EDGE, 1)] = pot_ref[slot, 0, EDGE + 3, pl.ds(i, 1)]
        return carry

    lax.fori_loop(0, EDGE, place, 0, unroll=4)
    grown[pl.ds(8, EDGE)] = pot_ref[slot, 0, EDGE]
    grown[pl.ds((EDGE + 1) * PITCH + 8, EDGE)] = pot_ref[slot, 0, EDGE + 1]


def field_at(here, x_low, x_high, y_low, y_high):
    return [
        0.5 * (x_low - x_high),
        0.5 * (y_low - y_high),
        0.5 * (pltpu.roll(here, 1, 1) - pltpu.roll(here, DEPTH - 1, 1)),
    ]


def row_field(grown, i):
    start = i * PITCH + 8
    return field_at(
        *[grown[pl.ds(start + step, EDGE)] for step in (PITCH, 0, 2 * PITCH, PITCH - 1, PITCH + 1)]
    )


def column_field(grown, j):
    return field_at(
        *[
            grown[pl.ds(8 + j + step, EDGE, stride=PITCH)]
            for step in (PITCH, 0, 2 * PITCH, PITCH - 1, PITCH + 1)
        ]
    )


def edges_kernel(
    table_ref, routes_ref, pops_ref, charge_ref, mask_ref, pot_ref, block_ref, face_ref, corner_ref, block_out, grown
):
    tile = pl.program_id(0)
    block_out[...] = block_ref[...]
    place_potential(grown, pot_ref, 0)

    def finish(face, axis, sign, pops, charge, flags, field):
        relaxed, velocity = collide_rows(pops, charge, field)
        fluid = flags == 1

        def value(q):
            return jnp.where(fluid, relaxed[q], pops[q])

        for k, q in enumerate(crossing(axis, sign)):
            face_ref[0, face, k] = value(q)
        face_ref[0, face, 5] = velocity[axis]
        return value

    for face, sign, j in ((UP_Y, 1, EDGE - 1), (DOWN_Y, -1, 0)):
        finish(
            face,
            1,
            sign,
            [pops_ref[q, 0, pl.ds(j, EDGE, stride=EDGE)] for q in range(19)],
            charge_ref[0, pl.ds(j, EDGE, stride=EDGE)],
            mask_ref[0, pl.ds(1, EDGE), 1 + j, :],
            column_field(grown, j),
        )
    for face, sign, i, corners in (
        (BELOW_X, 1, EDGE - 1, ((0, 7, EDGE - 1), (1, 9, 0))),
        (ABOVE_X, -1, 0, ((2, 10, EDGE - 1), (3, 8, 0))),
    ):
        value = finish(
            face,
            0,
            sign,
            [pops_ref[q, 0, pl.ds(i * EDGE, EDGE)] for q in range(19)],
            charge_ref[0, pl.ds(i * EDGE, EDGE)],
            mask_ref[0, i + 1, pl.ds(1, EDGE), :],
            row_field(grown, i),
        )
        for n, q, j in corners:
            corner_ref[tile // 2, pl.ds(lax.rem(tile, 2) * 4 + n, 1)] = value(q)[j : j + 1]
    same = lax.rem(table_ref[R_ROW, tile], 2)
    for k in range(6):
        face_ref[0, SAME_X, k] = jnp.where(
            same == 0, face_ref[0, BELOW_X, k], face_ref[0, ABOVE_X, k]
        )


def edges(table, routes, populations, charge, fluid_mask, returned, potential):
    f32 = jnp.float32
    return pl.pallas_call(
        edges_kernel,
        out_shape=(
            jax.ShapeDtypeStruct((TILES, FACES, 6, EDGE, DEPTH), f32),
            jax.ShapeDtypeStruct((2, 8, DEPTH), f32),
            jax.ShapeDtypeStruct((BLOCK, BLOCK, DEPTH), f32),
        ),
        grid_spec=pltpu.PrefetchScalarGridSpec(
            num_scalar_prefetch=2,
            grid=(TILES,),
            in_specs=[
                pl.BlockSpec((19, 1, EDGE * EDGE, DEPTH), lambda s, tab, rts: (0, s, 0, 0)),
                pl.BlockSpec((1, EDGE * EDGE, DEPTH), lambda s, tab, rts: (s, 0, 0)),
                pl.BlockSpec((1, EDGE + 2, EDGE + 2, DEPTH), lambda s, tab, rts: (s, 0, 0, 0)),
                pl.BlockSpec(
                    (1, 1, PACK, EDGE, DEPTH),
                    lambda s, tab, rts: (rts[TO_HOLDER * 8 + K_LAST, s], 0, 0, 0, 0),
                ),
                pl.BlockSpec((BLOCK // TILES, BLOCK, DEPTH), lambda s, tab, rts: (s, 0, 0)),
            ],
            out_specs=[
                pl.BlockSpec((1, FACES, 6, EDGE, DEPTH), lambda s, tab, rts: (s, 0, 0, 0, 0)),
                pl.BlockSpec((2, 8, DEPTH), lambda s, tab, rts: (0, 0, 0)),
                pl.BlockSpec((BLOCK // TILES, BLOCK, DEPTH), lambda s, tab, rts: (s, 0, 0)),
            ],
            scratch_shapes=[pltpu.VMEM(((EDGE + 2) * PITCH, DEPTH), f32)],
        ),
        compiler_params=pltpu.CompilerParams(vmem_limit_bytes=16 << 20),
        name="edges",
    )(
        table,
        routes,
        populations.reshape(19, TILES, EDGE * EDGE, DEPTH),
        charge.reshape(TILES, EDGE * EDGE, DEPTH),
        fluid_mask,
        returned,
        potential,
    )


FACE_LANES = (
    (0, (UP_Y, DOWN_Y, SAME_X)),
    (1, (UP_Y, DOWN_Y, SAME_X)),
    (0, (BELOW_X, ABOVE_X)),
    (1, (BELOW_X, ABOVE_X)),
)


def faces_kernel(
    table_ref,
    routes_ref,
    faces_ref,
    corners_ref,
    charge_ref,
    mask_ref,
    pot_ref,
    pops_ref,
    out_ref,
    all_ref,
    cells_ref,
    vel_ref,
    shifted,
    grown,
    pops_sem,
    corner_send,
    corner_recv,
    shift_send,
    shift_recv,
    own_sem,
    *scratch,
):
    me = lax.axis_index("gy")
    peers = [shifted_id(0, k) for k in range(1, GROUPS)]
    bands = [shifted_id(1, 0), shifted_id(-1, 0)]
    fetches = [
        pltpu.make_async_copy(pops_ref.at[:, t], cells_ref.at[:, t], pops_sem.at[t])
        for t in range(TILES)
    ]
    for copy in fetches:
        copy.start()

    def collide(t, begin):
        def rows(i, carry):
            pops = [cells_ref[q, t, i] for q in range(19)]
            relaxed, velocity = collide_rows(pops, charge_ref[t, i], row_field(grown, i))
            fluid = mask_ref[t, i + 1, pl.ds(1, EDGE), :] == 1
            for q in range(19):
                cells_ref[q, t, i] = jnp.where(fluid, relaxed[q], pops[q])
            for d in range(3):
                vel_ref[d, t, i] = velocity[d]
            return carry

        lax.fori_loop(begin, begin + EDGE // len(FACE_LANES), rows, 0)

    greet(peers + bands)
    shifts = []
    for n, target in enumerate(bands):
        copy = pltpu.make_async_remote_copy(
            src_ref=faces_ref.at[:, 3 + n],
            dst_ref=shifted.at[n],
            send_sem=shift_send.at[n],
            recv_sem=shift_recv.at[n],
            device_id=target,
            device_id_type=MESH,
        )
        copy.start()
        shifts.append(copy)
    lanes = []
    for n, (order, perms) in enumerate(FACE_LANES):
        rows = slice(order * 3, order * 3 + 3)

        def first(k, slot, perms=perms, rows=rows):
            if perms[k] < BELOW_X:
                return faces_ref[slot, perms[k], rows]
            return shifted[perms[k] - BELOW_X, slot, rows]

        def final(here, perms=perms, order=order):
            return out_ref.at[here, pl.ds(perms[0], len(perms)), pl.ds(order * 3, 3)]

        lanes.append(Lane(order, perms, table_ref, first, scratch[16 * n : 16 * n + 16], final))
    spread_out, forward = [], []
    own = pltpu.make_async_copy(corners_ref, all_ref.at[0, me], own_sem)
    for stage in range(4):
        for n, lane in enumerate(lanes):
            if stage == 0 and n == 2:
                for k, target in enumerate(peers):
                    copy = pltpu.make_async_remote_copy(
                        src_ref=corners_ref,
                        dst_ref=all_ref.at[0, me],
                        send_sem=corner_send.at[k],
                        recv_sem=corner_recv.at[k],
                        device_id=target,
                        device_id_type=MESH,
                    )
                    copy.start()
                    spread_out.append(copy)
                own.start()
                for copy in shifts:
                    copy.wait_recv()
            lane.advance(stage)
            if n == 0:
                fetches[stage].wait()
                place_potential(grown, pot_ref, routes_ref[TO_HOLDER * 8 + K_LAST, stage])
            collide(stage, n * (EDGE // len(FACE_LANES)))
        if stage == 1:
            own.wait()
            for copy in spread_out:
                copy.wait_recv()
            for n, target in enumerate(bands):
                copy = pltpu.make_async_remote_copy(
                    src_ref=all_ref.at[0],
                    dst_ref=all_ref.at[1 + n],
                    send_sem=corner_send.at[GROUPS - 1 + n],
                    recv_sem=corner_recv.at[GROUPS - 1 + n],
                    device_id=target,
                    device_id_type=MESH,
                )
                copy.start()
                forward.append(copy)
    for lane in lanes:
        lane.arrived()
    for copy in forward:
        copy.wait_recv()
    for copy in shifts + spread_out + forward:
        copy.wait_send()
    for lane in lanes:
        lane.close()


def collide_and_send(table, routes, faces, corners, charge, fluid_mask, returned, populations):
    vmem = pl.BlockSpec(memory_space=pltpu.VMEM)
    smem = pl.BlockSpec(memory_space=pltpu.SMEM)
    anywhere = pl.BlockSpec(memory_space=pltpu.HBM)
    f32 = jnp.float32
    dma = pltpu.SemaphoreType.DMA
    scratch = []
    for _, perms in FACE_LANES:
        scratch += lane_scratch(len(perms), (3, EDGE, DEPTH))
    return pl.pallas_call(
        faces_kernel,
        out_shape=(
            jax.ShapeDtypeStruct((TILES, FACES, 6, EDGE, DEPTH), f32),
            jax.ShapeDtypeStruct((3, GROUPS, 2, 8, DEPTH), f32),
            jax.ShapeDtypeStruct((19, TILES, EDGE, EDGE, DEPTH), f32),
            jax.ShapeDtypeStruct((3, TILES, EDGE, EDGE, DEPTH), f32),
        ),
        in_specs=[smem, smem] + [vmem] * 5 + [pl.BlockSpec(memory_space=pl.ANY)],
        out_specs=(vmem,) * 4,
        scratch_shapes=[
            pltpu.VMEM((2, TILES, 6, EDGE, DEPTH), f32),
            pltpu.VMEM(((EDGE + 2) * PITCH, DEPTH), f32),
            dma((TILES,)),
            dma((GROUPS + 1,)),
            dma((GROUPS + 1,)),
            dma((2,)),
            dma((2,)),
            dma,
        ]
        + scratch,
        compiler_params=pltpu.CompilerParams(
            collective_id=3, has_side_effects=True, vmem_limit_bytes=20 << 20
        ),
        name="faces",
    )(table, routes, faces, corners, charge, fluid_mask, returned, populations)


CHARGE, SPEED = 19, 20
SOLID = 3.0e38
FIRST = 8 + EDGE
STRIP = 8 + (EDGE + 2) * EDGE + 8


def stream_kernel(
    table_ref,
    routes_ref,
    relaxed_ref,
    vel_ref,
    charge_ref,
    mask_ref,
    rim_ref,
    *rest,
):
    faces, (corner_ref, pops_out, charge_out, grown, side, sems) = rest[:FACES], rest[FACES:]
    tile = pl.program_id(0)
    here = lax.rem(tile, 2)

    def fetch(t, slot):
        rows = pl.ds(FIRST, EDGE * EDGE)
        return [
            pltpu.make_async_copy(
                relaxed_ref.at[:, t], grown.at[slot, pl.ds(0, 19), rows], sems.at[slot, 0]
            ),
            pltpu.make_async_copy(
                charge_ref.at[t], grown.at[slot, CHARGE, rows], sems.at[slot, 1]
            ),
            pltpu.make_async_copy(
                vel_ref.at[:, t], grown.at[slot, pl.ds(SPEED, 3), rows], sems.at[slot, 2]
            ),
        ]

    @pl.when(tile == 0)
    def _():
        for copy in fetch(0, 0):
            copy.start()

    @pl.when(tile + 1 < TILES)
    def _():
        for copy in fetch(tile + 1, 1 - here):
            copy.start()

    for copy in fetch(tile, here):
        copy.wait()

    cells = grown.at[here]
    before, after = pl.ds(8, EDGE), pl.ds(FIRST + EDGE * EDGE, EDGE)

    def x_rim(face, sign, rows):
        for k, q in enumerate(crossing(0, sign) + [SPEED]):
            cells[q, rows] = faces[face][0, 0, k]

    row = table_ref[R_ROW, tile]

    @pl.when(row == 0)
    def _():
        x_rim(BELOW_X, 1, before)
        x_rim(SAME_X, -1, after)

    @pl.when(row == 1)
    def _():
        x_rim(SAME_X, 1, before)
        x_rim(ABOVE_X, -1, after)

    cells[CHARGE, before] = rim_ref[0, 0, 0]
    cells[CHARGE, after] = rim_ref[0, 0, 1]
    for face, sign, end in ((UP_Y, 1, 0), (DOWN_Y, -1, 1)):
        for k, q in enumerate(crossing(1, sign)):
            side[end, k, pl.ds(1, EDGE)] = faces[face][0, 0, k]
        side[end, 5, pl.ds(1, EDGE)] = faces[face][0, 0, 5]
        side[end, 6, pl.ds(1, EDGE)] = rim_ref[0, 0, 2 + end]
    for n, (q, sign, layer) in enumerate(((7, 1, 0), (9, -1, 0), (10, 1, 17), (8, -1, 17))):
        found = table_ref[R_CORNER + n, tile]
        inside = lax.rem(found, TILES)
        side[n % 2, crossing(1, sign).index(q), pl.ds(layer, 1)] = corner_ref[
            found // TILES, inside // 2, pl.ds(lax.rem(inside, 2) * 4 + n, 1)
        ]
    spot = lax.broadcasted_iota(jnp.int32, (EDGE, DEPTH), 0)
    ends = {-1: spot == 0, 1: spot == EDGE - 1}

    def rows(i, carry):
        def cell(q, di=0, dj=0):
            value = cells[q, pl.ds(i * EDGE + (FIRST + di * EDGE + dj), EDGE)]
            if dj == 0:
                return value
            if q < 19:
                k = crossing(1, -dj).index(q)
            else:
                k = 6 if q == CHARGE else 5
            return jnp.where(ends[dj], side[(dj + 1) // 2, k, pl.ds(i + 1 + di, 1)], value)

        def flag(di=0, dj=0):
            return mask_ref[0, i + 1 + di, pl.ds(1 + dj, EDGE), :]

        own = flag()
        own_fluid = own == 1
        for q in range(19):
            step_x, step_y, step_z = LATTICE[q]
            value = cell(q)
            if q == 0:
                pops_out[q, 0, i] = value
                continue
            moved = cell(q, -step_x, -step_y)
            from_fluid = flag(-step_x, -step_y) == 1
            if step_z != 0:
                moved = pltpu.roll(jnp.where(from_fluid, moved, SOLID), step_z % DEPTH, 1)
                from_fluid = moved < SOLID
            read = jnp.where(from_fluid, moved, cell(opposite(q)))
            pops_out[q, 0, i] = jnp.where(own_fluid, read, value)

        charge = cell(CHARGE)
        weight = own.astype(jnp.float32)

        def flux(speed_a, speed_b, value_a, value_b, flags):
            speed = 0.5 * (speed_a + speed_b)
            return speed * jnp.where(speed > 0, value_a, value_b) * flags

        change = None
        for d, (di, dj) in enumerate(((1, 0), (0, 1))):
            speed = cell(SPEED + d)
            for sign in (1, -1):
                other = cell(CHARGE, sign * di, sign * dj)
                other_speed = cell(SPEED + d, sign * di, sign * dj)
                flags = weight * flag(sign * di, sign * dj).astype(jnp.float32)
                if sign > 0:
                    part = flux(speed, other_speed, charge, other, flags)
                    change = part if change is None else change + part
                else:
                    change = change - flux(other_speed, speed, other, charge, flags)
        speed = cell(SPEED + 2)
        next_charge = pltpu.roll(jnp.where(own_fluid, charge, SOLID), DEPTH - 1, 1)
        middle = 0.5 * (speed + pltpu.roll(speed, DEPTH - 1, 1))
        over = middle * jnp.where(middle > 0, charge, next_charge)
        over = jnp.where(own_fluid & (next_charge < SOLID), over, 0.0)
        change = change + over - pltpu.roll(over, 1, 1)
        charge_out[0, i] = jnp.where(own_fluid, charge - change, charge)
        return carry

    lax.fori_loop(0, EDGE, rows, 0, unroll=2)


def stream(table, routes, relaxed, velocity, charge, fluid_mask, returned, faces, corners):
    f32 = jnp.float32
    face_specs = [
        pl.BlockSpec(
            (1, 1, 6, EDGE, DEPTH),
            lambda s, tab, rts, face=face: (tab[face * 8 + K_LAST, s], face, 0, 0, 0),
        )
        for face in range(FACES)
    ]
    anywhere = pl.BlockSpec(memory_space=pl.ANY)
    return pl.pallas_call(
        stream_kernel,
        out_shape=(
            jax.ShapeDtypeStruct((19, TILES, EDGE, EDGE, DEPTH), f32),
            jax.ShapeDtypeStruct((TILES, EDGE, EDGE, DEPTH), f32),
        ),
        grid_spec=pltpu.PrefetchScalarGridSpec(
            num_scalar_prefetch=2,
            grid=(TILES,),
            in_specs=[
                anywhere,
                anywhere,
                anywhere,
                pl.BlockSpec((1, EDGE + 2, EDGE + 2, DEPTH), lambda s, tab, rts: (s, 0, 0, 0)),
                pl.BlockSpec(
                    (1, 1, 4, EDGE, DEPTH),
                    lambda s, tab, rts: (rts[TO_HOLDER * 8 + K_LAST, s], 0, 0, 0, 0),
                ),
            ]
            + face_specs
            + [pl.BlockSpec((3 * GROUPS, 2, 8, DEPTH), lambda s, tab, rts: (0, 0, 0, 0))],
            out_specs=[
                pl.BlockSpec((19, 1, EDGE, EDGE, DEPTH), lambda s, tab, rts: (0, s, 0, 0, 0)),
                pl.BlockSpec((1, EDGE, EDGE, DEPTH), lambda s, tab, rts: (s, 0, 0, 0)),
            ],
            scratch_shapes=[
                pltpu.VMEM((2, 23, STRIP, DEPTH), f32),
                pltpu.VMEM((2, 7, 24, DEPTH), f32),
                pltpu.SemaphoreType.DMA((2, 3)),
            ],
        ),
        compiler_params=pltpu.CompilerParams(vmem_limit_bytes=24 << 20),
        name="stream",
    )(
        table,
        routes,
        relaxed.reshape(19, TILES, EDGE * EDGE, DEPTH),
        velocity.reshape(3, TILES, EDGE * EDGE, DEPTH),
        charge.reshape(TILES, EDGE * EDGE, DEPTH),
        fluid_mask,
        returned,
        *([faces] * FACES),
        corners.reshape(3 * GROUPS, 2, 8, DEPTH),
    )


def per_device(populations, charge, fluid_mask, tile_ids, phase_label, permittivity):
    me = lax.axis_index("gy").astype(jnp.int32).reshape(1)
    place = jnp.arange(8 * DEPTH, dtype=jnp.int32).reshape(8, DEPTH)
    ids_row = jnp.where(place // TILES == me, jnp.tile(tile_ids, 2 * DEPTH).reshape(8, DEPTH), 0)
    ids = exchange_start(ids_row)
    routes = make_routes(owner_routes_kernel, 16, me, ids)
    potential, packed, others, charge_rims, charge, fluid_mask = find_potential(
        permittivity, routes, charge, fluid_mask, ids, phase_label
    )
    returned, table, populations = send_back(me, routes, packed, ids, others, populations)
    faces, corners, potential = edges(
        table, routes, populations, charge, fluid_mask, returned, potential
    )
    rims, all_corners, relaxed, velocity = collide_and_send(
        table, routes, faces, corners, charge, fluid_mask, returned, populations
    )
    populations_next, charge_next = stream(
        table, routes, relaxed, velocity, charge, fluid_mask, charge_rims, rims, all_corners
    )
    return (populations_next, charge_next, potential)


def solution(mesh):
    placed = (
        P(None, ("gx", "gy"), None, None, None),
        P(("gx", "gy"), None, None, None),
        P(("gx", "gy"), None, None, None),
        P(("gx", "gy")),
        P("gx", "gy", None),
        P(),
    )
    return jax.shard_map(
        per_device,
        mesh=mesh,
        in_specs=placed,
        out_specs=(
            P(None, ("gx", "gy"), None, None, None),
            P(("gx", "gy"), None, None, None),
            P("gx", "gy", None),
        ),
        check_vma=False,
    )
```

```python
import functools

import jax
import jax.numpy as jnp
from jax import lax
from jax.experimental import pallas as pl
from jax.experimental.pallas import tpu as pltpu
from jax.sharding import PartitionSpec as P

EDGE = 16
DEPTH = 128
BLOCK = 32
PHASES = 4
SWEEPS = 4
UNROLL = 2
TILES = 4
GROUPS = 16
BANDS = 8
COLS = 32
SIDE = 8
MESH = pl.DeviceIdType.MESH

LATTICE = (
    (0, 0, 0),
    (1, 0, 0),
    (-1, 0, 0),
    (0, 1, 0),
    (0, -1, 0),
    (0, 0, 1),
    (0, 0, -1),
    (1, 1, 0),
    (-1, -1, 0),
    (1, -1, 0),
    (-1, 1, 0),
    (1, 0, 1),
    (-1, 0, -1),
    (1, 0, -1),
    (-1, 0, 1),
    (0, 1, 1),
    (0, -1, -1),
    (0, 1, -1),
    (0, -1, 1),
)
WEIGHTS = (1.0 / 3.0, 1.0 / 18.0, 1.0 / 36.0)
PAIRS = ((1, 2), (3, 4), (5, 6), (7, 8), (9, 10), (11, 12), (13, 14), (15, 16), (17, 18))
relax_time = 0.8
screening = 0.001
spectrum_low = 0.1
spectrum_high = 2.0

AROUND = tuple((dx, dy) for dx in (-1, 0, 1) for dy in (-1, 0, 1) if (dx, dy) != (0, 0))

TO_OWNER, TO_HOLDER = 0, 1
UP_Y, DOWN_Y, SAME_X, BELOW_X, ABOVE_X = range(5)
R_ROW, R_CORNER = 40, 41


def opposite(direction):
    return LATTICE.index(tuple(-entry for entry in LATTICE[direction]))


def crossing(axis_index, face_sign):
    return [d for d in range(19) if LATTICE[d][axis_index] == face_sign]


def shifted_id(dx, dy):
    gx = lax.rem(lax.axis_index("gx") + dx + BANDS, BANDS)
    gy = lax.rem(lax.axis_index("gy") + dy + GROUPS, GROUPS)
    return {"gx": gx, "gy": gy}


def span(step, width, pad):
    if step == 0:
        return pl.ds(0, BLOCK), pl.ds(pad, BLOCK)
    if step > 0:
        return pl.ds(BLOCK - width, width), pl.ds(pad - width, width)
    return pl.ds(0, width), pl.ds(pad + BLOCK, width)


def halo_copies(block_ref, ext_ref, width, side, send_sem, recv_sem):
    copies = []
    for n, (dx, dy) in enumerate(AROUND):
        src_i, dst_i = span(dx, width, width)
        src_j, dst_j = span(dy, side, SIDE)
        copies.append(
            pltpu.make_async_remote_copy(
                src_ref=block_ref.at[src_i, src_j],
                dst_ref=ext_ref.at[dst_i, dst_j],
                send_sem=send_sem.at[n],
                recv_sem=recv_sem.at[n],
                device_id=shifted_id(dx, dy),
                device_id_type=MESH,
            )
        )
    return copies


def greet(targets):
    barrier = pltpu.get_barrier_semaphore()
    for target in targets:
        pl.semaphore_signal(barrier, inc=1, device_id=target, device_id_type=MESH)
    pl.semaphore_wait(barrier, len(targets))


def start_kernel(ids_ref, all_ref, ids_send, ids_recv, own_sem):
    me = lax.axis_index("gy")
    peers = [shifted_id(0, k) for k in range(1, GROUPS)]
    greet(peers)
    started = []
    for k, target in enumerate(peers):
        copy = pltpu.make_async_remote_copy(
            src_ref=ids_ref,
            dst_ref=all_ref.at[me],
            send_sem=ids_send.at[k],
            recv_sem=ids_recv.at[k],
            device_id=target,
            device_id_type=MESH,
        )
        copy.start()
        started.append(copy)
    own = pltpu.make_async_copy(ids_ref, all_ref.at[me], own_sem)
    own.start()
    own.wait()
    for copy in started:
        copy.wait()


def exchange_start(ids):
    vmem = pl.BlockSpec(memory_space=pltpu.VMEM)
    dma = pltpu.SemaphoreType.DMA
    return pl.pallas_call(
        start_kernel,
        out_shape=jax.ShapeDtypeStruct((GROUPS, 8, DEPTH), jnp.int32),
        in_specs=[vmem],
        out_specs=vmem,
        scratch_shapes=[dma((GROUPS - 1,)), dma((GROUPS - 1,)), dma],
        compiler_params=pltpu.CompilerParams(
            collective_id=0, has_side_effects=True, vmem_limit_bytes=8 << 20
        ),
        name="start",
    )(ids)


WIDE = BLOCK + 2 * SIDE
TALL = BLOCK + 8
ROOM = WIDE + 16
INNER = pl.ds(8, WIDE)
BEFORE = pl.ds(7, WIDE)
AFTER = pl.ds(9, WIDE)
PACK = 20
FACES = 5


def harmonic(left, right):
    return 2.0 * left * right / (left + right)


def look_up_rows(permit_ref, phase_ref, permit):
    def look_up(i, carry):
        label = phase_ref[i]
        value = jnp.where(label == 0, permit_ref[0], 0.0)
        for k in range(1, PHASES):
            value = jnp.where(label == k, permit_ref[k], value)
        permit[i] = value
        return carry

    lax.fori_loop(0, TALL + 2, look_up, 0)


def weigh_rows(begin, end, permit, coef, scale_ref):
    def weigh(i, below):
        here = permit[i + 1]
        above = harmonic(here, permit[i + 2])
        right = harmonic(here, pltpu.roll(here, WIDE - 1, 0))
        left = pltpu.roll(right, 1, 0)
        up = harmonic(here, pltpu.roll(here, DEPTH - 1, 1))
        down = pltpu.roll(up, 1, 1)
        scale = 1.0 / (above + below + right + left + up + down + screening)
        for k, weight in enumerate((above, below, right, left, up, down)):
            coef[k, i] = weight * scale
        scale_ref[i] = scale
        return above

    lax.fori_loop(begin, end, weigh, harmonic(permit[begin], permit[begin + 1]), unroll=2)


def tile_corner(t):
    return 4 + (t // 2) * EDGE, SIDE + (t % 2) * EDGE


def pack_rims(out, place, ref):
    for t in range(TILES):
        i0, j0 = tile_corner(t)

        def rows(i, carry, t=t, i0=i0, j0=j0):
            out[t, place + 2, pl.ds(i, 1)] = ref[i0 + i, pl.ds(j0 - 1, 1)]
            out[t, place + 3, pl.ds(i, 1)] = ref[i0 + i, pl.ds(j0 + EDGE, 1)]
            return carry

        lax.fori_loop(0, EDGE, rows, 0, unroll=4)
        out[t, place] = ref[i0 - 1, pl.ds(j0, EDGE)]
        out[t, place + 1] = ref[i0 + EDGE, pl.ds(j0, EDGE)]


def sweep_rows(coef, scale_ref, source_ref, pot_ref, pack, resid, upd_a, upd_b, total, between):
    center = 0.5 * (spectrum_high + spectrum_low)
    half = 0.5 * (spectrum_high - spectrum_low)
    ratio = center / half

    def begin(i, carry):
        value = source_ref[i] * scale_ref[i]
        resid[i] = value
        value = value * (1.0 / center)
        upd_a[i, INNER] = value
        total[i] = value
        return carry

    lax.fori_loop(0, TALL, begin, 0, unroll=2)
    rho = 1.0 / ratio
    old, new = upd_a, upd_b
    for sweep in range(SWEEPS - 1):
        between(sweep + 1)
        rho_new = 1.0 / (2.0 * ratio - rho)
        keep, gain = rho_new * rho, 2.0 * rho_new / half

        def relax(i, carry, old=old, new=new, keep=keep, gain=gain):
            here = old[i, INNER]
            near = coef[0, i] * old[i + 1, INNER] + coef[1, i] * old[i - 1, INNER]
            near += coef[2, i] * old[i, AFTER] + coef[3, i] * old[i, BEFORE]
            near += coef[4, i] * pltpu.roll(here, DEPTH - 1, 1)
            near += coef[5, i] * pltpu.roll(here, 1, 1)
            left = resid[i] - here + near
            resid[i] = left
            here = keep * here + gain * left
            new[i, INNER] = here
            total[i] = total[i] + here
            return carry

        lax.fori_loop(sweep + 1, TALL - 1 - sweep, relax, 0, unroll=UNROLL)
        old, new = new, old
        rho = rho_new

    def emit(i, carry):
        pot_ref[i] = total[i + 4, pl.ds(SIDE, BLOCK)]
        return carry

    lax.fori_loop(0, BLOCK, emit, 0, unroll=4)
    for t in range(TILES):
        i0, j0 = tile_corner(t)

        def rows(i, carry, t=t, i0=i0, j0=j0):
            pack[t, i] = total[i0 + i, pl.ds(j0, EDGE)]
            return carry

        lax.fori_loop(0, EDGE, rows, 0, unroll=4)
    pack_rims(pack, EDGE, total)


K_FIRST, K_X2, K_X3, K_X4, K_Y2, K_Y3, K_Y4, K_LAST = range(8)
PORTS = 64


def to_column(row, eye):
    return jnp.sum(jnp.where(eye, row, 0), axis=1, keepdims=True)


def split_edges(left, right, sub, lane, doublings):
    def partners(ends):
        same = ends[0] == ends[1]
        before = jnp.where(same & (lane < sub), 1, 0)
        after = jnp.where(same & (sub < lane), 1, 0)
        rank_c = jnp.sum(before, axis=1, keepdims=True)
        rank_r = jnp.sum(after, axis=0, keepdims=True)
        pair = same & ((rank_c >> 1) == (rank_r >> 1)) & (sub != lane)
        return jnp.where(pair, 1.0, 0.0).astype(jnp.bfloat16)

    def times(a, b):
        return jnp.dot(a, b, preferred_element_type=jnp.float32)

    by_left, by_right = partners(left), partners(right)
    reach = times(by_left, by_right) + times(by_right, by_left)
    reach = jnp.where((sub == lane) | (reach > 0.0), 1.0, 0.0).astype(jnp.bfloat16)
    for _ in range(doublings):
        reach = jnp.where(times(reach, reach) > 0.0, 1.0, 0.0).astype(jnp.bfloat16)
    mate = times(by_left, reach) > 0.0
    own = reach.astype(jnp.float32) > 0.0
    size = sub.shape[0]
    col = jnp.where(
        jnp.min(jnp.where(own, lane, size), axis=1, keepdims=True)
        > jnp.min(jnp.where(mate, lane, size), axis=1, keepdims=True),
        1,
        0,
    )
    row = jnp.where(
        jnp.min(jnp.where(own, sub, size), axis=0, keepdims=True)
        > jnp.min(jnp.where(mate, sub, size), axis=0, keepdims=True),
        1,
        0,
    )
    return col, row


def join(first, second, base):
    return tuple(a * base + b for a, b in zip(first, second))


def colour(left, right, sub, lane, doublings):
    high = split_edges(left, right, sub, lane, doublings)
    low = split_edges(join(left, high, 2), join(right, high, 2), sub, lane, doublings - 1)
    return join(high, low, 2)


class Ports:
    def __init__(self, size):
        self.size = size
        self.sub = lax.broadcasted_iota(jnp.int32, (size, size), 0)
        self.lane = lax.broadcasted_iota(jnp.int32, (size, size), 1)
        self.eye = self.sub == self.lane
        edge = (
            lax.broadcasted_iota(jnp.int32, (size, 1), 0),
            lax.broadcasted_iota(jnp.int32, (1, size), 1),
        )
        self.port = tuple(e & (PORTS - 1) for e in edge)
        self.half = tuple(e >> 6 for e in edge)
        self.device = tuple(e >> 2 for e in self.port)
        self.entry = lax.broadcasted_iota(jnp.int32, (size, DEPTH), 1)


def store_routes(me, ports, places, goal_ids, target, store):
    half, port, device = ports.half, ports.port, ports.device
    sub, lane = ports.sub, ports.lane
    my_row, my_col = me >> 2, me & 3
    at = to_column(goal_ids, ports.eye) + half[0] * PORTS
    target = target + half[1] * PORTS
    drop = jnp.sum(jnp.where(at == target, sub & (PORTS - 1), 0), axis=0, keepdims=True)
    drop = (to_column(drop, ports.eye), drop)
    goal = tuple(d >> 2 for d in drop)
    begin = tuple(h * GROUPS + d for h, d in zip(half, device))
    end = tuple(h * GROUPS + d for h, d in zip(half, goal))
    j = colour(begin, end, sub, lane, 4)
    group = tuple(h * 4 + c for h, c in zip(half, j))
    rows = (tuple(d >> 2 for d in device), tuple(d >> 2 for d in goal))
    cols = (tuple(d & 3 for d in device), tuple(d & 3 for d in goal))
    b = colour(join(group, rows[0], 4), join(group, rows[1], 4), sub, lane, 2)[0]
    g = colour(join(group, cols[0], 4), join(group, cols[1], 4), sub, lane, 2)[0]
    j = j[0]
    slots = (port[0] & 3, drop[0] & 3)
    ends = (device[0], goal[0])
    rows, cols = tuple(r[0] for r in rows), tuple(c[0] for c in cols)
    for perm, h, back in places:
        mine = half[0] == h
        src, dst = (1, 0) if back else (0, 1)
        for kind, given, key, value in (
            (K_FIRST, ends[src] == me, j, slots[src]),
            (K_X2, (rows[src] == my_row) & (j == my_col), b, cols[src]),
            (K_X3, (j == my_col) & (b == my_row), rows[dst], rows[src]),
            (K_X4, (j == my_col) & (rows[dst] == my_row), cols[dst], b),
            (K_Y2, (cols[src] == my_col) & (j == my_row), g, rows[src]),
            (K_Y3, (j == my_row) & (g == my_col), cols[dst], cols[src]),
            (K_Y4, (j == my_row) & (cols[dst] == my_col), rows[dst], g),
            (K_LAST, ends[dst] == me, slots[dst], j),
        ):
            kept = jnp.where(mine & given, value, 0)
            found = jnp.where(key == ports.entry, kept, 0)
            store(perm * 8 + kind, jnp.sum(found, axis=0, keepdims=True))


def owner_tables(me, own, store):
    ports = Ports(PORTS)
    owner = (ports.port[1] & 3) // 2 * COLS + ports.device[1] * 2 + (ports.port[1] & 1)
    places = ((TO_OWNER, 0, True), (TO_HOLDER, 0, False))
    store_routes(me, ports, places, own[:, :PORTS], owner, store)


def face_tables(me, own, below, above, store):
    ports = Ports(2 * PORTS)
    half = ports.half

    def turn(pos, step):
        return (pos & COLS) + ((pos + step) & (COLS - 1))

    def both(first, second):
        return jnp.where(half[1] == 0, first, pltpu.roll(second, PORTS, 1))

    twice = both(own, own)
    places = ((UP_Y, 0, False), (DOWN_Y, 0, True), (SAME_X, 1, False))
    store_routes(me, ports, places, twice, both(turn(own, 1), own ^ COLS), store)
    yield
    places = ((BELOW_X, 0, False), (ABOVE_X, 1, False))
    store_routes(me, ports, places, twice, both(below ^ COLS, above ^ COLS), store)
    yield
    mine = jnp.sum(
        jnp.where((ports.sub == me * TILES + ports.lane) & (ports.lane < TILES), to_column(own, ports.eye), 0),
        axis=0,
        keepdims=True,
    )
    store(R_ROW, mine >> 5)
    found = []
    for band in (own, below, above):
        at = to_column(band, ports.eye)
        for step in (-1, 1):
            there = (at == turn(mine ^ COLS, step)) & (ports.sub < PORTS)
            found.append(jnp.sum(jnp.where(there, ports.sub, 0), axis=0, keepdims=True))
    upper = (mine >> 5) == 1
    for n in range(2):
        store(R_CORNER + n, jnp.where(upper, found[n], found[2 + n] + PORTS))
        store(R_CORNER + 2 + n, jnp.where(upper, found[4 + n] + 2 * PORTS, found[n]))


def gathered_ids(ids):
    return jnp.sum(ids, axis=0)[0:1]


def owner_routes_kernel(me_ref, ids_ref, out_ref):
    def store(place, row):
        out_ref[pl.ds(place, 1)] = row

    owner_tables(me_ref[0], gathered_ids(ids_ref[...]), store)


def make_routes(kernel, rows, me, *ids):
    vmem = pl.BlockSpec(memory_space=pltpu.VMEM)
    return pl.pallas_call(
        kernel,
        out_shape=jax.ShapeDtypeStruct((rows, DEPTH), jnp.int32),
        in_specs=[pl.BlockSpec(memory_space=pltpu.SMEM)] + [vmem] * len(ids),
        out_specs=vmem,
        compiler_params=pltpu.CompilerParams(vmem_limit_bytes=8 << 20),
        name=kernel.__name__,
    )(me, *ids)


def ring(axis, step):
    gy = lax.axis_index("gy")
    row, col = gy // 4, lax.rem(gy, 4)
    if axis == 0:
        place = lax.rem(col + step, 4)
        return col, place, {"gx": lax.axis_index("gx"), "gy": row * 4 + place}
    place = lax.rem(row + step, 4)
    return row, place, {"gx": lax.axis_index("gx"), "gy": place * 4 + col}


RING_AXES = ((0, 1, 1, 0), (1, 0, 0, 1))
RING_KINDS = ((K_FIRST, K_X2, K_X3, K_X4), (K_FIRST, K_Y2, K_Y3, K_Y4))


class Lane:
    def __init__(self, order, perms, table_ref, first, scratch, final=None):
        self.order, self.perms, self.table_ref = order, perms, table_ref
        self.first, self.final = first, final
        self.stages = [scratch[4 * n : 4 * n + 4] for n in range(4)]
        self.waiting, self.sent = [], []

    def arrived(self):
        for copy in self.waiting:
            copy.wait_recv()
        self.waiting = []

    def target(self, stage, here):
        if stage == 3 and self.final is not None:
            return self.final(here)
        return self.stages[stage][1].at[here]

    def advance(self, stage):
        self.arrived()
        send, _, send_sem, recv_sem = self.stages[stage]
        for step in (2, 1, 3, 0):
            here, place, target = ring(RING_AXES[self.order][stage], step)
            landing = self.target(stage, here)
            for n, perm in enumerate(self.perms):
                slot = self.table_ref[perm * 8 + RING_KINDS[self.order][stage], place]
                if stage:
                    value = self.stages[stage - 1][1][slot, n]
                else:
                    value = self.first(n, slot)
                if step:
                    send[step - 1, n] = value
                else:
                    landing[n] = value
            if step:
                copy = pltpu.make_async_remote_copy(
                    src_ref=send.at[step - 1],
                    dst_ref=landing,
                    send_sem=send_sem.at[step - 1],
                    recv_sem=recv_sem.at[step - 1],
                    device_id=target,
                    device_id_type=MESH,
                )
                copy.start()
                self.waiting.append(copy)
                self.sent.append(copy)

    def close(self):
        for copy in self.sent:
            copy.wait_send()


def lane_scratch(items, shape):
    scratch = []
    for stage in range(4):
        scratch += [
            pltpu.VMEM((3, items) + shape, jnp.float32),
            pltpu.VMEM((4, items) + shape, jnp.float32),
            pltpu.SemaphoreType.DMA((3,)),
            pltpu.SemaphoreType.DMA((3,)),
        ]
    return scratch


RING_PEERS = tuple((axis, step) for axis in range(2) for step in (1, 2, 3))
LANES = 4


def source_kernel(
    permit_ref,
    table_ref,
    charge_hbm,
    mask_hbm,
    ids_ref,
    phase_ref,
    pot_ref,
    pack_ref,
    others,
    rims_ref,
    charge_ref,
    mask_ref,
    fetch_sem,
    rims,
    ext_ref,
    coef_ref,
    scale_ref,
    resid,
    upd_a,
    upd_b,
    total,
    phase_ext,
    permit,
    send_sem,
    recv_sem,
    phase_send,
    phase_recv,
    ids_send,
    ids_recv,
    own_sem,
    *scratch,
):
    bands = [shifted_id(1, 0), shifted_id(-1, 0)]
    fetches = [
        pltpu.make_async_copy(charge_hbm, charge_ref, fetch_sem.at[0]),
        pltpu.make_async_copy(mask_hbm, mask_ref, fetch_sem.at[1]),
        pltpu.make_async_copy(
            phase_ref, phase_ext.at[pl.ds(5, BLOCK), pl.ds(SIDE, BLOCK)], own_sem
        ),
    ]
    for copy in fetches:
        copy.start()
    greet([ring(*peer)[2] for peer in RING_PEERS] + [shifted_id(dx, dy) for dx, dy in AROUND])
    for copy in fetches:
        copy.wait()
    part = EDGE // LANES
    lanes = []
    for n in range(LANES):

        def first(_, slot, n=n):
            flags = mask_ref[slot, 1 + n * part : 1 + (n + 1) * part, 1 : EDGE + 1]
            return charge_ref[slot, n * part : (n + 1) * part] * flags.astype(jnp.float32)

        lanes.append(
            Lane(n % 2, (TO_OWNER,), table_ref, first, scratch[16 * n : 16 * n + 16])
        )
    passed = []
    phases = halo_copies(phase_ref, phase_ext, 5, SIDE, phase_send, phase_recv)

    def weights(begin, end):
        weigh_rows(begin, end, permit, coef_ref, scale_ref)

    for stage in range(4):
        for lane in lanes:
            lane.advance(stage)
        if stage == 0:
            for copy in phases:
                copy.start()
            for n, target in enumerate(bands):
                copy = pltpu.make_async_remote_copy(
                    src_ref=ids_ref,
                    dst_ref=others.at[n],
                    send_sem=ids_send.at[n],
                    recv_sem=ids_recv.at[n],
                    device_id=target,
                    device_id_type=MESH,
                )
                copy.start()
                passed.append(copy)
        elif stage == 1:
            for copy in phases:
                copy.wait_recv()
            look_up_rows(permit_ref, phase_ext, permit)
            weights(0, 8)
        elif stage == 2:
            weights(8, 18)
        else:
            weights(18, 30)
    for n, lane in enumerate(lanes):
        lane.arrived()
        final = lane.stages[3][1]
        for t in range(TILES):
            i0, j0 = 4 + (t // 2) * EDGE + n * part, SIDE + (t % 2) * EDGE
            ext_ref[i0 : i0 + part, j0 : j0 + EDGE] = final[
                table_ref[TO_OWNER * 8 + K_LAST, t], 0
            ]
    block = ext_ref.at[pl.ds(4, BLOCK), pl.ds(SIDE, BLOCK)]
    copies = halo_copies(block, ext_ref, 4, 4, send_sem, recv_sem)
    for copy in copies:
        copy.start()
    weights(30, TALL)
    for copy in copies + passed:
        copy.wait()
    for copy in phases:
        copy.wait_send()
    pack_rims(rims, 0, ext_ref)
    returning = []
    for n in range(2):

        def first(_, slot, n=n):
            return rims[slot, 2 * n : 2 * n + 2]

        def final(here, n=n):
            return rims_ref.at[here, :, pl.ds(2 * n, 2)]

        refs = scratch[16 * (LANES + n) : 16 * (LANES + n) + 16]
        returning.append(Lane(n, (TO_HOLDER,), table_ref, first, refs, final))

    def between(stage):
        for lane in returning:
            lane.advance(stage)

    between(0)
    sweep_rows(
        coef_ref, scale_ref, ext_ref, pot_ref, pack_ref, resid, upd_a, upd_b, total, between
    )
    for lane in returning:
        lane.arrived()
    for lane in lanes + returning:
        lane.close()


def find_potential(permittivity, routes, charge, fluid_mask, ids, phase):
    vmem = pl.BlockSpec(memory_space=pltpu.VMEM)
    smem = pl.BlockSpec(memory_space=pltpu.SMEM)
    anywhere = pl.BlockSpec(memory_space=pltpu.HBM)
    dma = pltpu.SemaphoreType.DMA
    f32 = jnp.float32
    return pl.pallas_call(
        source_kernel,
        out_shape=(
            jax.ShapeDtypeStruct((BLOCK, BLOCK, DEPTH), f32),
            jax.ShapeDtypeStruct((TILES, PACK, EDGE, DEPTH), f32),
            jax.ShapeDtypeStruct((2, GROUPS, 8, DEPTH), jnp.int32),
            jax.ShapeDtypeStruct((TILES, 1, 4, EDGE, DEPTH), f32),
            jax.ShapeDtypeStruct((TILES, EDGE, EDGE, DEPTH), f32),
            jax.ShapeDtypeStruct((TILES, EDGE + 2, EDGE + 2, DEPTH), jnp.int32),
        ),
        in_specs=[smem] * 2 + [anywhere, anywhere, vmem, anywhere],
        out_specs=(vmem,) * 6,
        scratch_shapes=[
            dma((2,)),
            pltpu.VMEM((TILES, 4, EDGE, DEPTH), f32),
            pltpu.VMEM((TALL, WIDE, DEPTH), f32),
            pltpu.VMEM((6, TALL, WIDE, DEPTH), f32),
            pltpu.VMEM((TALL, WIDE, DEPTH), f32),
            pltpu.VMEM((TALL, WIDE, DEPTH), f32),
            pltpu.VMEM((TALL, ROOM, DEPTH), f32),
            pltpu.VMEM((TALL, ROOM, DEPTH), f32),
            pltpu.VMEM((TALL, WIDE, DEPTH), f32),
            pltpu.VMEM((TALL + 2, WIDE, DEPTH), jnp.int32),
            pltpu.VMEM((TALL + 2, WIDE, DEPTH), f32),
            dma((8,)),
            dma((8,)),
            dma((8,)),
            dma((8,)),
            dma((2,)),
            dma((2,)),
            dma,
        ]
        + lane_scratch(1, (EDGE // LANES, EDGE, DEPTH)) * LANES
        + lane_scratch(1, (2, EDGE, DEPTH)) * 2,
        compiler_params=pltpu.CompilerParams(
            collective_id=1, has_side_effects=True, vmem_limit_bytes=28 << 20
        ),
        name="source",
    )(permittivity, routes, charge, fluid_mask, ids, phase)


def back_kernel(
    me_ref,
    table_ref,
    items_ref,
    ids_ref,
    others_ref,
    pops_hbm,
    out_ref,
    face_ref,
    pops_ref,
    pops_sem,
    *scratch,
):
    fetches = [
        pltpu.make_async_copy(pops_hbm.at[:, t], pops_ref.at[:, t], pops_sem.at[t])
        for t in range(TILES)
    ]
    for copy in fetches:
        copy.start()

    def store(place, row):
        face_ref[pl.ds(place, 1)] = row

    greet([ring(*peer)[2] for peer in RING_PEERS])
    part = PACK // LANES
    lanes = []
    for n in range(LANES):
        rows = slice(n * part, (n + 1) * part)

        def first(_, slot, rows=rows):
            return items_ref[slot, rows]

        def final(here, n=n):
            return out_ref.at[here, :, pl.ds(n * part, part)]

        lanes.append(
            Lane(n % 2, (TO_HOLDER,), table_ref, first, scratch[16 * n : 16 * n + 16], final)
        )
    tables = None
    for stage in range(4):
        for lane in lanes:
            lane.advance(stage)
        if stage == 0:
            tables = face_tables(
                me_ref[0],
                gathered_ids(ids_ref[...]),
                gathered_ids(others_ref[0]),
                gathered_ids(others_ref[1]),
                store,
            )
        next(tables, None)
    for lane in lanes:
        lane.arrived()
    for lane in lanes:
        lane.close()
    for copy in fetches:
        copy.wait()


def send_back(me, routes, packed, ids, others, populations):
    vmem = pl.BlockSpec(memory_space=pltpu.VMEM)
    smem = pl.BlockSpec(memory_space=pltpu.SMEM)
    return pl.pallas_call(
        back_kernel,
        out_shape=(
            jax.ShapeDtypeStruct((TILES, 1, PACK, EDGE, DEPTH), jnp.float32),
            jax.ShapeDtypeStruct((48, DEPTH), jnp.int32),
            jax.ShapeDtypeStruct((19, TILES, EDGE, EDGE, DEPTH), jnp.float32),
        ),
        in_specs=[smem, smem, vmem, vmem, vmem, pl.BlockSpec(memory_space=pltpu.HBM)],
        out_specs=(vmem, vmem, vmem),
        scratch_shapes=[pltpu.SemaphoreType.DMA((TILES,))]
        + lane_scratch(1, (PACK // LANES, EDGE, DEPTH)) * LANES,
        compiler_params=pltpu.CompilerParams(
            collective_id=2, has_side_effects=True, vmem_limit_bytes=40 << 20
        ),
        name="back",
    )(me, routes, packed, ids, others, populations)


def collide_rows(pops, charge, field):
    force = [charge * component for component in field]
    sums = {}
    diffs = {}
    for a, b in PAIRS:
        sums[a] = pops[a] + pops[b]
        diffs[a] = pops[a] - pops[b]
    density = pops[0]
    for a, _ in PAIRS:
        density = density + sums[a]
    momentum = [
        diffs[1] + diffs[7] + diffs[9] + diffs[11] + diffs[13],
        diffs[3] + diffs[7] - diffs[9] + diffs[15] + diffs[17],
        diffs[5] + diffs[11] - diffs[13] + diffs[15] - diffs[17],
    ]
    inverse = 1.0 / density
    velocity = [(momentum[d] + 0.5 * force[d]) * inverse for d in range(3)]
    scale = 1.0 - 0.5 / relax_time
    rate = 1.0 / relax_time
    speed = velocity[0] * velocity[0] + velocity[1] * velocity[1] + velocity[2] * velocity[2]
    work = velocity[0] * force[0] + velocity[1] * force[1] + velocity[2] * force[2]
    weighted = rate * density
    base = weighted - (1.5 * weighted) * speed - (3.0 * scale) * work
    odd = [3.0 * weighted * velocity[d] + (3.0 * scale) * force[d] for d in range(3)]
    inner = [4.5 * weighted * velocity[d] + (9.0 * scale) * force[d] for d in range(3)]
    keep = 1.0 - rate
    result = [None] * 19
    result[0] = keep * pops[0] + WEIGHTS[0] * base
    for a, b in PAIRS:
        step = LATTICE[a]
        axes = [d for d in range(3) if step[d] != 0]
        if len(axes) == 1:
            (d,) = axes
            cu, co, ci = velocity[d], odd[d], inner[d]
            weight = WEIGHTS[1]
        else:
            d, e = axes
            weight = WEIGHTS[2]
            if step[d] * step[e] > 0:
                cu, co, ci = velocity[d] + velocity[e], odd[d] + odd[e], inner[d] + inner[e]
            else:
                cu, co, ci = velocity[d] - velocity[e], odd[d] - odd[e], inner[d] - inner[e]
        even = weight * (base + cu * ci)
        lean = weight * co
        result[a] = keep * pops[a] + (even + lean)
        result[b] = keep * pops[b] + (even - lean)
    return result, velocity


PITCH = 32


def place_potential(grown, pot_ref, slot):
    def place(i, carry):
        start = (i + 1) * PITCH
        grown[pl.ds(start + 8, EDGE)] = pot_ref[slot, 0, i]
        grown[pl.ds(start + 7, 1)] = pot_ref[slot, 0, EDGE + 2, pl.ds(i, 1)]
        grown[pl.ds(start + 8 + EDGE, 1)] = pot_ref[slot, 0, EDGE + 3, pl.ds(i, 1)]
        return carry

    lax.fori_loop(0, EDGE, place, 0, unroll=4)
    grown[pl.ds(8, EDGE)] = pot_ref[slot, 0, EDGE]
    grown[pl.ds((EDGE + 1) * PITCH + 8, EDGE)] = pot_ref[slot, 0, EDGE + 1]


def field_at(here, x_low, x_high, y_low, y_high):
    return [
        0.5 * (x_low - x_high),
        0.5 * (y_low - y_high),
        0.5 * (pltpu.roll(here, 1, 1) - pltpu.roll(here, DEPTH - 1, 1)),
    ]


def row_field(grown, i):
    start = i * PITCH + 8
    return field_at(
        *[grown[pl.ds(start + step, EDGE)] for step in (PITCH, 0, 2 * PITCH, PITCH - 1, PITCH + 1)]
    )


def column_field(grown, j):
    return field_at(
        *[
            grown[pl.ds(8 + j + step, EDGE, stride=PITCH)]
            for step in (PITCH, 0, 2 * PITCH, PITCH - 1, PITCH + 1)
        ]
    )


def edges_kernel(
    table_ref, routes_ref, pops_ref, charge_ref, mask_ref, pot_ref, block_ref, face_ref, corner_ref, block_out, grown
):
    tile = pl.program_id(0)
    block_out[...] = block_ref[...]
    place_potential(grown, pot_ref, 0)

    def finish(face, axis, sign, pops, charge, flags, field):
        relaxed, velocity = collide_rows(pops, charge, field)
        fluid = flags == 1

        def value(q):
            return jnp.where(fluid, relaxed[q], pops[q])

        for k, q in enumerate(crossing(axis, sign)):
            face_ref[0, face, k] = value(q)
        face_ref[0, face, 5] = velocity[axis]
        return value

    for face, sign, j in ((UP_Y, 1, EDGE - 1), (DOWN_Y, -1, 0)):
        finish(
            face,
            1,
            sign,
            [pops_ref[q, 0, pl.ds(j, EDGE, stride=EDGE)] for q in range(19)],
            charge_ref[0, pl.ds(j, EDGE, stride=EDGE)],
            mask_ref[0, pl.ds(1, EDGE), 1 + j, :],
            column_field(grown, j),
        )
    for face, sign, i, corners in (
        (BELOW_X, 1, EDGE - 1, ((0, 7, EDGE - 1), (1, 9, 0))),
        (ABOVE_X, -1, 0, ((2, 10, EDGE - 1), (3, 8, 0))),
    ):
        value = finish(
            face,
            0,
            sign,
            [pops_ref[q, 0, pl.ds(i * EDGE, EDGE)] for q in range(19)],
            charge_ref[0, pl.ds(i * EDGE, EDGE)],
            mask_ref[0, i + 1, pl.ds(1, EDGE), :],
            row_field(grown, i),
        )
        for n, q, j in corners:
            corner_ref[tile // 2, pl.ds(lax.rem(tile, 2) * 4 + n, 1)] = value(q)[j : j + 1]
    same = lax.rem(table_ref[R_ROW, tile], 2)
    for k in range(6):
        face_ref[0, SAME_X, k] = jnp.where(
            same == 0, face_ref[0, BELOW_X, k], face_ref[0, ABOVE_X, k]
        )


def edges(table, routes, populations, charge, fluid_mask, returned, potential):
    f32 = jnp.float32
    return pl.pallas_call(
        edges_kernel,
        out_shape=(
            jax.ShapeDtypeStruct((TILES, FACES, 6, EDGE, DEPTH), f32),
            jax.ShapeDtypeStruct((2, 8, DEPTH), f32),
            jax.ShapeDtypeStruct((BLOCK, BLOCK, DEPTH), f32),
        ),
        grid_spec=pltpu.PrefetchScalarGridSpec(
            num_scalar_prefetch=2,
            grid=(TILES,),
            in_specs=[
                pl.BlockSpec((19, 1, EDGE * EDGE, DEPTH), lambda s, tab, rts: (0, s, 0, 0)),
                pl.BlockSpec((1, EDGE * EDGE, DEPTH), lambda s, tab, rts: (s, 0, 0)),
                pl.BlockSpec((1, EDGE + 2, EDGE + 2, DEPTH), lambda s, tab, rts: (s, 0, 0, 0)),
                pl.BlockSpec(
                    (1, 1, PACK, EDGE, DEPTH),
                    lambda s, tab, rts: (rts[TO_HOLDER * 8 + K_LAST, s], 0, 0, 0, 0),
                ),
                pl.BlockSpec((BLOCK // TILES, BLOCK, DEPTH), lambda s, tab, rts: (s, 0, 0)),
            ],
            out_specs=[
                pl.BlockSpec((1, FACES, 6, EDGE, DEPTH), lambda s, tab, rts: (s, 0, 0, 0, 0)),
                pl.BlockSpec((2, 8, DEPTH), lambda s, tab, rts: (0, 0, 0)),
                pl.BlockSpec((BLOCK // TILES, BLOCK, DEPTH), lambda s, tab, rts: (s, 0, 0)),
            ],
            scratch_shapes=[pltpu.VMEM(((EDGE + 2) * PITCH, DEPTH), f32)],
        ),
        compiler_params=pltpu.CompilerParams(vmem_limit_bytes=16 << 20),
        name="edges",
    )(
        table,
        routes,
        populations.reshape(19, TILES, EDGE * EDGE, DEPTH),
        charge.reshape(TILES, EDGE * EDGE, DEPTH),
        fluid_mask,
        returned,
        potential,
    )


FACE_LANES = (
    (0, (UP_Y, DOWN_Y, SAME_X)),
    (1, (UP_Y, DOWN_Y, SAME_X)),
    (0, (BELOW_X, ABOVE_X)),
    (1, (BELOW_X, ABOVE_X)),
)


def faces_kernel(
    table_ref,
    routes_ref,
    faces_ref,
    corners_ref,
    charge_ref,
    mask_ref,
    pot_ref,
    pops_ref,
    out_ref,
    all_ref,
    cells_ref,
    vel_ref,
    shifted,
    grown,
    pops_sem,
    corner_send,
    corner_recv,
    shift_send,
    shift_recv,
    own_sem,
    *scratch,
):
    me = lax.axis_index("gy")
    peers = [shifted_id(0, k) for k in range(1, GROUPS)]
    bands = [shifted_id(1, 0), shifted_id(-1, 0)]
    fetches = [
        pltpu.make_async_copy(pops_ref.at[:, t], cells_ref.at[:, t], pops_sem.at[t])
        for t in range(TILES)
    ]
    for copy in fetches:
        copy.start()

    def collide(t, begin):
        def rows(i, carry):
            pops = [cells_ref[q, t, i] for q in range(19)]
            relaxed, velocity = collide_rows(pops, charge_ref[t, i], row_field(grown, i))
            fluid = mask_ref[t, i + 1, pl.ds(1, EDGE), :] == 1
            for q in range(19):
                cells_ref[q, t, i] = jnp.where(fluid, relaxed[q], pops[q])
            for d in range(3):
                vel_ref[d, t, i] = velocity[d]
            return carry

        lax.fori_loop(begin, begin + EDGE // len(FACE_LANES), rows, 0)

    greet(peers + bands)
    shifts = []
    for n, target in enumerate(bands):
        copy = pltpu.make_async_remote_copy(
            src_ref=faces_ref.at[:, 3 + n],
            dst_ref=shifted.at[n],
            send_sem=shift_send.at[n],
            recv_sem=shift_recv.at[n],
            device_id=target,
            device_id_type=MESH,
        )
        copy.start()
        shifts.append(copy)
    lanes = []
    for n, (order, perms) in enumerate(FACE_LANES):
        rows = slice(order * 3, order * 3 + 3)

        def first(k, slot, perms=perms, rows=rows):
            if perms[k] < BELOW_X:
                return faces_ref[slot, perms[k], rows]
            return shifted[perms[k] - BELOW_X, slot, rows]

        def final(here, perms=perms, order=order):
            return out_ref.at[here, pl.ds(perms[0], len(perms)), pl.ds(order * 3, 3)]

        lanes.append(Lane(order, perms, table_ref, first, scratch[16 * n : 16 * n + 16], final))
    spread_out, forward = [], []
    own = pltpu.make_async_copy(corners_ref, all_ref.at[0, me], own_sem)
    for stage in range(4):
        for n, lane in enumerate(lanes):
            if stage == 0 and n == 2:
                for k, target in enumerate(peers):
                    copy = pltpu.make_async_remote_copy(
                        src_ref=corners_ref,
                        dst_ref=all_ref.at[0, me],
                        send_sem=corner_send.at[k],
                        recv_sem=corner_recv.at[k],
                        device_id=target,
                        device_id_type=MESH,
                    )
                    copy.start()
                    spread_out.append(copy)
                own.start()
                for copy in shifts:
                    copy.wait_recv()
            lane.advance(stage)
            if n == 0:
                fetches[stage].wait()
                place_potential(grown, pot_ref, routes_ref[TO_HOLDER * 8 + K_LAST, stage])
            collide(stage, n * (EDGE // len(FACE_LANES)))
        if stage == 1:
            own.wait()
            for copy in spread_out:
                copy.wait_recv()
            for n, target in enumerate(bands):
                copy = pltpu.make_async_remote_copy(
                    src_ref=all_ref.at[0],
                    dst_ref=all_ref.at[1 + n],
                    send_sem=corner_send.at[GROUPS - 1 + n],
                    recv_sem=corner_recv.at[GROUPS - 1 + n],
                    device_id=target,
                    device_id_type=MESH,
                )
                copy.start()
                forward.append(copy)
    for lane in lanes:
        lane.arrived()
    for copy in forward:
        copy.wait_recv()
    for copy in shifts + spread_out + forward:
        copy.wait_send()
    for lane in lanes:
        lane.close()


def collide_and_send(table, routes, faces, corners, charge, fluid_mask, returned, populations):
    vmem = pl.BlockSpec(memory_space=pltpu.VMEM)
    smem = pl.BlockSpec(memory_space=pltpu.SMEM)
    anywhere = pl.BlockSpec(memory_space=pltpu.HBM)
    f32 = jnp.float32
    dma = pltpu.SemaphoreType.DMA
    scratch = []
    for _, perms in FACE_LANES:
        scratch += lane_scratch(len(perms), (3, EDGE, DEPTH))
    return pl.pallas_call(
        faces_kernel,
        out_shape=(
            jax.ShapeDtypeStruct((TILES, FACES, 6, EDGE, DEPTH), f32),
            jax.ShapeDtypeStruct((3, GROUPS, 2, 8, DEPTH), f32),
            jax.ShapeDtypeStruct((19, TILES, EDGE, EDGE, DEPTH), f32),
            jax.ShapeDtypeStruct((3, TILES, EDGE, EDGE, DEPTH), f32),
        ),
        in_specs=[smem, smem] + [vmem] * 5 + [pl.BlockSpec(memory_space=pl.ANY)],
        out_specs=(vmem,) * 4,
        scratch_shapes=[
            pltpu.VMEM((2, TILES, 6, EDGE, DEPTH), f32),
            pltpu.VMEM(((EDGE + 2) * PITCH, DEPTH), f32),
            dma((TILES,)),
            dma((GROUPS + 1,)),
            dma((GROUPS + 1,)),
            dma((2,)),
            dma((2,)),
            dma,
        ]
        + scratch,
        compiler_params=pltpu.CompilerParams(
            collective_id=3, has_side_effects=True, vmem_limit_bytes=20 << 20
        ),
        name="faces",
    )(table, routes, faces, corners, charge, fluid_mask, returned, populations)


CHARGE, SPEED = 19, 20
SOLID = 3.0e38
FIRST = 8 + EDGE
STRIP = 8 + (EDGE + 2) * EDGE + 8


def stream_kernel(
    table_ref,
    routes_ref,
    relaxed_ref,
    vel_ref,
    charge_ref,
    mask_ref,
    rim_ref,
    *rest,
):
    faces, (corner_ref, pops_out, charge_out, grown, side, sems) = rest[:FACES], rest[FACES:]
    tile = pl.program_id(0)
    here = lax.rem(tile, 2)

    def fetch(t, slot):
        rows = pl.ds(FIRST, EDGE * EDGE)
        return [
            pltpu.make_async_copy(
                relaxed_ref.at[:, t], grown.at[slot, pl.ds(0, 19), rows], sems.at[slot, 0]
            ),
            pltpu.make_async_copy(
                charge_ref.at[t], grown.at[slot, CHARGE, rows], sems.at[slot, 1]
            ),
            pltpu.make_async_copy(
                vel_ref.at[:, t], grown.at[slot, pl.ds(SPEED, 3), rows], sems.at[slot, 2]
            ),
        ]

    @pl.when(tile == 0)
    def _():
        for copy in fetch(0, 0):
            copy.start()

    @pl.when(tile + 1 < TILES)
    def _():
        for copy in fetch(tile + 1, 1 - here):
            copy.start()

    for copy in fetch(tile, here):
        copy.wait()

    cells = grown.at[here]
    before, after = pl.ds(8, EDGE), pl.ds(FIRST + EDGE * EDGE, EDGE)

    def x_rim(face, sign, rows):
        for k, q in enumerate(crossing(0, sign) + [SPEED]):
            cells[q, rows] = faces[face][0, 0, k]

    row = table_ref[R_ROW, tile]

    @pl.when(row == 0)
    def _():
        x_rim(BELOW_X, 1, before)
        x_rim(SAME_X, -1, after)

    @pl.when(row == 1)
    def _():
        x_rim(SAME_X, 1, before)
        x_rim(ABOVE_X, -1, after)

    cells[CHARGE, before] = rim_ref[0, 0, 0]
    cells[CHARGE, after] = rim_ref[0, 0, 1]
    for face, sign, end in ((UP_Y, 1, 0), (DOWN_Y, -1, 1)):
        for k, q in enumerate(crossing(1, sign)):
            side[end, k, pl.ds(1, EDGE)] = faces[face][0, 0, k]
        side[end, 5, pl.ds(1, EDGE)] = faces[face][0, 0, 5]
        side[end, 6, pl.ds(1, EDGE)] = rim_ref[0, 0, 2 + end]
    for n, (q, sign, layer) in enumerate(((7, 1, 0), (9, -1, 0), (10, 1, 17), (8, -1, 17))):
        found = table_ref[R_CORNER + n, tile]
        inside = lax.rem(found, TILES)
        side[n % 2, crossing(1, sign).index(q), pl.ds(layer, 1)] = corner_ref[
            found // TILES, inside // 2, pl.ds(lax.rem(inside, 2) * 4 + n, 1)
        ]
    spot = lax.broadcasted_iota(jnp.int32, (EDGE, DEPTH), 0)
    ends = {-1: spot == 0, 1: spot == EDGE - 1}

    def rows(i, carry):
        def cell(q, di=0, dj=0):
            value = cells[q, pl.ds(i * EDGE + (FIRST + di * EDGE + dj), EDGE)]
            if dj == 0:
                return value
            if q < 19:
                k = crossing(1, -dj).index(q)
            else:
                k = 6 if q == CHARGE else 5
            return jnp.where(ends[dj], side[(dj + 1) // 2, k, pl.ds(i + 1 + di, 1)], value)

        def flag(di=0, dj=0):
            return mask_ref[0, i + 1 + di, pl.ds(1 + dj, EDGE), :]

        own = flag()
        own_fluid = own == 1
        for q in range(19):
            step_x, step_y, step_z = LATTICE[q]
            value = cell(q)
            if q == 0:
                pops_out[q, 0, i] = value
                continue
            moved = cell(q, -step_x, -step_y)
            from_fluid = flag(-step_x, -step_y) == 1
            if step_z != 0:
                moved = pltpu.roll(jnp.where(from_fluid, moved, SOLID), step_z % DEPTH, 1)
                from_fluid = moved < SOLID
            read = jnp.where(from_fluid, moved, cell(opposite(q)))
            pops_out[q, 0, i] = jnp.where(own_fluid, read, value)

        charge = cell(CHARGE)
        weight = own.astype(jnp.float32)

        def flux(speed_a, speed_b, value_a, value_b, flags):
            speed = 0.5 * (speed_a + speed_b)
            return speed * jnp.where(speed > 0, value_a, value_b) * flags

        change = None
        for d, (di, dj) in enumerate(((1, 0), (0, 1))):
            speed = cell(SPEED + d)
            for sign in (1, -1):
                other = cell(CHARGE, sign * di, sign * dj)
                other_speed = cell(SPEED + d, sign * di, sign * dj)
                flags = weight * flag(sign * di, sign * dj).astype(jnp.float32)
                if sign > 0:
                    part = flux(speed, other_speed, charge, other, flags)
                    change = part if change is None else change + part
                else:
                    change = change - flux(other_speed, speed, other, charge, flags)
        speed = cell(SPEED + 2)
        next_charge = pltpu.roll(jnp.where(own_fluid, charge, SOLID), DEPTH - 1, 1)
        middle = 0.5 * (speed + pltpu.roll(speed, DEPTH - 1, 1))
        over = middle * jnp.where(middle > 0, charge, next_charge)
        over = jnp.where(own_fluid & (next_charge < SOLID), over, 0.0)
        change = change + over - pltpu.roll(over, 1, 1)
        charge_out[0, i] = jnp.where(own_fluid, charge - change, charge)
        return carry

    lax.fori_loop(0, EDGE, rows, 0, unroll=2)


def stream(table, routes, relaxed, velocity, charge, fluid_mask, returned, faces, corners):
    f32 = jnp.float32
    face_specs = [
        pl.BlockSpec(
            (1, 1, 6, EDGE, DEPTH),
            lambda s, tab, rts, face=face: (tab[face * 8 + K_LAST, s], face, 0, 0, 0),
        )
        for face in range(FACES)
    ]
    anywhere = pl.BlockSpec(memory_space=pl.ANY)
    return pl.pallas_call(
        stream_kernel,
        out_shape=(
            jax.ShapeDtypeStruct((19, TILES, EDGE, EDGE, DEPTH), f32),
            jax.ShapeDtypeStruct((TILES, EDGE, EDGE, DEPTH), f32),
        ),
        grid_spec=pltpu.PrefetchScalarGridSpec(
            num_scalar_prefetch=2,
            grid=(TILES,),
            in_specs=[
                anywhere,
                anywhere,
                anywhere,
                pl.BlockSpec((1, EDGE + 2, EDGE + 2, DEPTH), lambda s, tab, rts: (s, 0, 0, 0)),
                pl.BlockSpec(
                    (1, 1, 4, EDGE, DEPTH),
                    lambda s, tab, rts: (rts[TO_HOLDER * 8 + K_LAST, s], 0, 0, 0, 0),
                ),
            ]
            + face_specs
            + [pl.BlockSpec((3 * GROUPS, 2, 8, DEPTH), lambda s, tab, rts: (0, 0, 0, 0))],
            out_specs=[
                pl.BlockSpec((19, 1, EDGE, EDGE, DEPTH), lambda s, tab, rts: (0, s, 0, 0, 0)),
                pl.BlockSpec((1, EDGE, EDGE, DEPTH), lambda s, tab, rts: (s, 0, 0, 0)),
            ],
            scratch_shapes=[
                pltpu.VMEM((2, 23, STRIP, DEPTH), f32),
                pltpu.VMEM((2, 7, 24, DEPTH), f32),
                pltpu.SemaphoreType.DMA((2, 3)),
            ],
        ),
        compiler_params=pltpu.CompilerParams(vmem_limit_bytes=24 << 20),
        name="stream",
    )(
        table,
        routes,
        relaxed.reshape(19, TILES, EDGE * EDGE, DEPTH),
        velocity.reshape(3, TILES, EDGE * EDGE, DEPTH),
        charge.reshape(TILES, EDGE * EDGE, DEPTH),
        fluid_mask,
        returned,
        *([faces] * FACES),
        corners.reshape(3 * GROUPS, 2, 8, DEPTH),
    )


def per_device(populations, charge, fluid_mask, tile_ids, phase_label, permittivity):
    me = lax.axis_index("gy").astype(jnp.int32).reshape(1)
    place = jnp.arange(8 * DEPTH, dtype=jnp.int32).reshape(8, DEPTH)
    ids_row = jnp.where(place // TILES == me, jnp.tile(tile_ids, 2 * DEPTH).reshape(8, DEPTH), 0)
    ids = exchange_start(ids_row)
    routes = make_routes(owner_routes_kernel, 16, me, ids)
    potential, packed, others, charge_rims, charge, fluid_mask = find_potential(
        permittivity, routes, charge, fluid_mask, ids, phase_label
    )
    returned, table, populations = send_back(me, routes, packed, ids, others, populations)
    faces, corners, potential = edges(
        table, routes, populations, charge, fluid_mask, returned, potential
    )
    rims, all_corners, relaxed, velocity = collide_and_send(
        table, routes, faces, corners, charge, fluid_mask, returned, populations
    )
    populations_next, charge_next = stream(
        table, routes, relaxed, velocity, charge, fluid_mask, charge_rims, rims, all_corners
    )
    return (populations_next, charge_next, potential)


def solution(mesh):
    placed = (
        P(None, ("gx", "gy"), None, None, None),
        P(("gx", "gy"), None, None, None),
        P(("gx", "gy"), None, None, None),
        P(("gx", "gy")),
        P("gx", "gy", None),
        P(),
    )
    return jax.shard_map(
        per_device,
        mesh=mesh,
        in_specs=placed,
        out_specs=(
            P(None, ("gx", "gy"), None, None, None),
            P(("gx", "gy"), None, None, None),
            P("gx", "gy", None),
        ),
        check_vma=False,
    )
```

```python
import functools

import jax
import jax.numpy as jnp
from jax import lax
from jax.experimental import pallas as pl
from jax.experimental.pallas import tpu as pltpu
from jax.sharding import PartitionSpec as P

EDGE = 16
DEPTH = 128
BLOCK = 32
PHASES = 4
SWEEPS = 4
UNROLL = 2
TILES = 4
GROUPS = 16
BANDS = 8
COLS = 32
SIDE = 8
MESH = pl.DeviceIdType.MESH

LATTICE = (
    (0, 0, 0),
    (1, 0, 0),
    (-1, 0, 0),
    (0, 1, 0),
    (0, -1, 0),
    (0, 0, 1),
    (0, 0, -1),
    (1, 1, 0),
    (-1, -1, 0),
    (1, -1, 0),
    (-1, 1, 0),
    (1, 0, 1),
    (-1, 0, -1),
    (1, 0, -1),
    (-1, 0, 1),
    (0, 1, 1),
    (0, -1, -1),
    (0, 1, -1),
    (0, -1, 1),
)
WEIGHTS = (1.0 / 3.0, 1.0 / 18.0, 1.0 / 36.0)
PAIRS = ((1, 2), (3, 4), (5, 6), (7, 8), (9, 10), (11, 12), (13, 14), (15, 16), (17, 18))
relax_time = 0.8
screening = 0.001
spectrum_low = 0.1
spectrum_high = 2.0

AROUND = tuple((dx, dy) for dx in (-1, 0, 1) for dy in (-1, 0, 1) if (dx, dy) != (0, 0))

TO_OWNER, TO_HOLDER = 0, 1
UP_Y, DOWN_Y, SAME_X, BELOW_X, ABOVE_X = range(5)
R_ROW, R_CORNER = 40, 41


def opposite(direction):
    return LATTICE.index(tuple(-entry for entry in LATTICE[direction]))


def crossing(axis_index, face_sign):
    return [d for d in range(19) if LATTICE[d][axis_index] == face_sign]


def shifted_id(dx, dy):
    gx = lax.rem(lax.axis_index("gx") + dx + BANDS, BANDS)
    gy = lax.rem(lax.axis_index("gy") + dy + GROUPS, GROUPS)
    return {"gx": gx, "gy": gy}


def span(step, width, pad):
    if step == 0:
        return pl.ds(0, BLOCK), pl.ds(pad, BLOCK)
    if step > 0:
        return pl.ds(BLOCK - width, width), pl.ds(pad - width, width)
    return pl.ds(0, width), pl.ds(pad + BLOCK, width)


def halo_copies(block_ref, ext_ref, width, side, send_sem, recv_sem):
    copies = []
    for n, (dx, dy) in enumerate(AROUND):
        src_i, dst_i = span(dx, width, width)
        src_j, dst_j = span(dy, side, SIDE)
        copies.append(
            pltpu.make_async_remote_copy(
                src_ref=block_ref.at[src_i, src_j],
                dst_ref=ext_ref.at[dst_i, dst_j],
                send_sem=send_sem.at[n],
                recv_sem=recv_sem.at[n],
                device_id=shifted_id(dx, dy),
                device_id_type=MESH,
            )
        )
    return copies


def greet(targets):
    barrier = pltpu.get_barrier_semaphore()
    for target in targets:
        pl.semaphore_signal(barrier, inc=1, device_id=target, device_id_type=MESH)
    pl.semaphore_wait(barrier, len(targets))


def start_kernel(ids_ref, all_ref, ids_send, ids_recv, own_sem):
    me = lax.axis_index("gy")
    peers = [shifted_id(0, k) for k in range(1, GROUPS)]
    greet(peers)
    started = []
    for k, target in enumerate(peers):
        copy = pltpu.make_async_remote_copy(
            src_ref=ids_ref,
            dst_ref=all_ref.at[me],
            send_sem=ids_send.at[k],
            recv_sem=ids_recv.at[k],
            device_id=target,
            device_id_type=MESH,
        )
        copy.start()
        started.append(copy)
    own = pltpu.make_async_copy(ids_ref, all_ref.at[me], own_sem)
    own.start()
    own.wait()
    for copy in started:
        copy.wait()


def exchange_start(ids):
    vmem = pl.BlockSpec(memory_space=pltpu.VMEM)
    dma = pltpu.SemaphoreType.DMA
    return pl.pallas_call(
        start_kernel,
        out_shape=jax.ShapeDtypeStruct((GROUPS, 8, DEPTH), jnp.int32),
        in_specs=[vmem],
        out_specs=vmem,
        scratch_shapes=[dma((GROUPS - 1,)), dma((GROUPS - 1,)), dma],
        compiler_params=pltpu.CompilerParams(
            collective_id=0, has_side_effects=True, vmem_limit_bytes=8 << 20
        ),
        name="start",
    )(ids)


WIDE = BLOCK + 2 * SIDE
TALL = BLOCK + 8
ROOM = WIDE + 16
INNER = pl.ds(8, WIDE)
BEFORE = pl.ds(7, WIDE)
AFTER = pl.ds(9, WIDE)
PACK = 20
FACES = 5


def harmonic(left, right):
    return 2.0 * left * right / (left + right)


def look_up_rows(permit_ref, phase_ref, permit):
    def look_up(i, carry):
        label = phase_ref[i]
        value = jnp.where(label == 0, permit_ref[0], 0.0)
        for k in range(1, PHASES):
            value = jnp.where(label == k, permit_ref[k], value)
        permit[i] = value
        return carry

    lax.fori_loop(0, TALL + 2, look_up, 0)


def weigh_rows(begin, end, permit, coef, scale_ref):
    def weigh(i, below):
        here = permit[i + 1]
        above = harmonic(here, permit[i + 2])
        right = harmonic(here, pltpu.roll(here, WIDE - 1, 0))
        left = pltpu.roll(right, 1, 0)
        up = harmonic(here, pltpu.roll(here, DEPTH - 1, 1))
        down = pltpu.roll(up, 1, 1)
        scale = 1.0 / (above + below + right + left + up + down + screening)
        for k, weight in enumerate((above, below, right, left, up, down)):
            coef[k, i] = weight * scale
        scale_ref[i] = scale
        return above

    lax.fori_loop(begin, end, weigh, harmonic(permit[begin], permit[begin + 1]), unroll=2)


def tile_corner(t):
    return 4 + (t // 2) * EDGE, SIDE + (t % 2) * EDGE


def pack_rims(out, place, ref):
    for t in range(TILES):
        i0, j0 = tile_corner(t)

        def rows(i, carry, t=t, i0=i0, j0=j0):
            out[t, place + 2, pl.ds(i, 1)] = ref[i0 + i, pl.ds(j0 - 1, 1)]
            out[t, place + 3, pl.ds(i, 1)] = ref[i0 + i, pl.ds(j0 + EDGE, 1)]
            return carry

        lax.fori_loop(0, EDGE, rows, 0, unroll=4)
        out[t, place] = ref[i0 - 1, pl.ds(j0, EDGE)]
        out[t, place + 1] = ref[i0 + EDGE, pl.ds(j0, EDGE)]


def sweep_rows(coef, scale_ref, source_ref, pot_ref, pack, resid, upd_a, upd_b, total, between):
    center = 0.5 * (spectrum_high + spectrum_low)
    half = 0.5 * (spectrum_high - spectrum_low)
    ratio = center / half

    def begin(i, carry):
        value = source_ref[i] * scale_ref[i]
        resid[i] = value
        value = value * (1.0 / center)
        upd_a[i, INNER] = value
        total[i] = value
        return carry

    lax.fori_loop(0, TALL, begin, 0, unroll=2)
    rho = 1.0 / ratio
    old, new = upd_a, upd_b
    for sweep in range(SWEEPS - 1):
        between(sweep + 1)
        rho_new = 1.0 / (2.0 * ratio - rho)
        keep, gain = rho_new * rho, 2.0 * rho_new / half

        def relax(i, carry, old=old, new=new, keep=keep, gain=gain):
            here = old[i, INNER]
            near = coef[0, i] * old[i + 1, INNER] + coef[1, i] * old[i - 1, INNER]
            near += coef[2, i] * old[i, AFTER] + coef[3, i] * old[i, BEFORE]
            near += coef[4, i] * pltpu.roll(here, DEPTH - 1, 1)
            near += coef[5, i] * pltpu.roll(here, 1, 1)
            left = resid[i] - here + near
            resid[i] = left
            here = keep * here + gain * left
            new[i, INNER] = here
            total[i] = total[i] + here
            return carry

        lax.fori_loop(sweep + 1, TALL - 1 - sweep, relax, 0, unroll=UNROLL)
        old, new = new, old
        rho = rho_new

    def emit(i, carry):
        pot_ref[i] = total[i + 4, pl.ds(SIDE, BLOCK)]
        return carry

    lax.fori_loop(0, BLOCK, emit, 0, unroll=4)
    for t in range(TILES):
        i0, j0 = tile_corner(t)

        def rows(i, carry, t=t, i0=i0, j0=j0):
            pack[t, i] = total[i0 + i, pl.ds(j0, EDGE)]
            return carry

        lax.fori_loop(0, EDGE, rows, 0, unroll=4)
    pack_rims(pack, EDGE, total)


K_FIRST, K_X2, K_X3, K_X4, K_Y2, K_Y3, K_Y4, K_LAST = range(8)
PORTS = 64


def to_column(row, eye):
    return jnp.sum(jnp.where(eye, row, 0), axis=1, keepdims=True)


def split_edges(left, right, sub, lane, doublings):
    def partners(ends):
        same = ends[0] == ends[1]
        before = jnp.where(same & (lane < sub), 1, 0)
        after = jnp.where(same & (sub < lane), 1, 0)
        rank_c = jnp.sum(before, axis=1, keepdims=True)
        rank_r = jnp.sum(after, axis=0, keepdims=True)
        pair = same & ((rank_c >> 1) == (rank_r >> 1)) & (sub != lane)
        return jnp.where(pair, 1.0, 0.0).astype(jnp.bfloat16)

    def times(a, b):
        return jnp.dot(a, b, preferred_element_type=jnp.float32)

    by_left, by_right = partners(left), partners(right)
    reach = times(by_left, by_right) + times(by_right, by_left)
    reach = jnp.where((sub == lane) | (reach > 0.0), 1.0, 0.0).astype(jnp.bfloat16)
    for _ in range(doublings):
        reach = jnp.where(times(reach, reach) > 0.0, 1.0, 0.0).astype(jnp.bfloat16)
    mate = times(by_left, reach) > 0.0
    own = reach.astype(jnp.float32) > 0.0
    size = sub.shape[0]
    col = jnp.where(
        jnp.min(jnp.where(own, lane, size), axis=1, keepdims=True)
        > jnp.min(jnp.where(mate, lane, size), axis=1, keepdims=True),
        1,
        0,
    )
    row = jnp.where(
        jnp.min(jnp.where(own, sub, size), axis=0, keepdims=True)
        > jnp.min(jnp.where(mate, sub, size), axis=0, keepdims=True),
        1,
        0,
    )
    return col, row


def join(first, second, base):
    return tuple(a * base + b for a, b in zip(first, second))


def colour(left, right, sub, lane, doublings):
    high = split_edges(left, right, sub, lane, doublings)
    low = split_edges(join(left, high, 2), join(right, high, 2), sub, lane, doublings - 1)
    return join(high, low, 2)


class Ports:
    def __init__(self, size):
        self.size = size
        self.sub = lax.broadcasted_iota(jnp.int32, (size, size), 0)
        self.lane = lax.broadcasted_iota(jnp.int32, (size, size), 1)
        self.eye = self.sub == self.lane
        edge = (
            lax.broadcasted_iota(jnp.int32, (size, 1), 0),
            lax.broadcasted_iota(jnp.int32, (1, size), 1),
        )
        self.port = tuple(e & (PORTS - 1) for e in edge)
        self.half = tuple(e >> 6 for e in edge)
        self.device = tuple(e >> 2 for e in self.port)
        self.entry = lax.broadcasted_iota(jnp.int32, (size, DEPTH), 1)


def store_routes(me, ports, places, goal_ids, target, store):
    half, port, device = ports.half, ports.port, ports.device
    sub, lane = ports.sub, ports.lane
    my_row, my_col = me >> 2, me & 3
    at = to_column(goal_ids, ports.eye) + half[0] * PORTS
    target = target + half[1] * PORTS
    drop = jnp.sum(jnp.where(at == target, sub & (PORTS - 1), 0), axis=0, keepdims=True)
    drop = (to_column(drop, ports.eye), drop)
    goal = tuple(d >> 2 for d in drop)
    begin = tuple(h * GROUPS + d for h, d in zip(half, device))
    end = tuple(h * GROUPS + d for h, d in zip(half, goal))
    j = colour(begin, end, sub, lane, 4)
    group = tuple(h * 4 + c for h, c in zip(half, j))
    rows = (tuple(d >> 2 for d in device), tuple(d >> 2 for d in goal))
    cols = (tuple(d & 3 for d in device), tuple(d & 3 for d in goal))
    b = colour(join(group, rows[0], 4), join(group, rows[1], 4), sub, lane, 2)[0]
    g = colour(join(group, cols[0], 4), join(group, cols[1], 4), sub, lane, 2)[0]
    j = j[0]
    slots = (port[0] & 3, drop[0] & 3)
    ends = (device[0], goal[0])
    rows, cols = tuple(r[0] for r in rows), tuple(c[0] for c in cols)
    for perm, h, back in places:
        mine = half[0] == h
        src, dst = (1, 0) if back else (0, 1)
        for kind, given, key, value in (
            (K_FIRST, ends[src] == me, j, slots[src]),
            (K_X2, (rows[src] == my_row) & (j == my_col), b, cols[src]),
            (K_X3, (j == my_col) & (b == my_row), rows[dst], rows[src]),
            (K_X4, (j == my_col) & (rows[dst] == my_row), cols[dst], b),
            (K_Y2, (cols[src] == my_col) & (j == my_row), g, rows[src]),
            (K_Y3, (j == my_row) & (g == my_col), cols[dst], cols[src]),
            (K_Y4, (j == my_row) & (cols[dst] == my_col), rows[dst], g),
            (K_LAST, ends[dst] == me, slots[dst], j),
        ):
            kept = jnp.where(mine & given, value, 0)
            found = jnp.where(key == ports.entry, kept, 0)
            store(perm * 8 + kind, jnp.sum(found, axis=0, keepdims=True))


def owner_tables(me, own, store):
    ports = Ports(PORTS)
    owner = (ports.port[1] & 3) // 2 * COLS + ports.device[1] * 2 + (ports.port[1] & 1)
    places = ((TO_OWNER, 0, True), (TO_HOLDER, 0, False))
    store_routes(me, ports, places, own[:, :PORTS], owner, store)


def face_tables(me, own, below, above, store):
    ports = Ports(2 * PORTS)
    half = ports.half

    def turn(pos, step):
        return (pos & COLS) + ((pos + step) & (COLS - 1))

    def both(first, second):
        return jnp.where(half[1] == 0, first, pltpu.roll(second, PORTS, 1))

    twice = both(own, own)
    places = ((UP_Y, 0, False), (DOWN_Y, 0, True), (SAME_X, 1, False))
    store_routes(me, ports, places, twice, both(turn(own, 1), own ^ COLS), store)
    yield
    places = ((BELOW_X, 0, False), (ABOVE_X, 1, False))
    store_routes(me, ports, places, twice, both(below ^ COLS, above ^ COLS), store)
    yield
    mine = jnp.sum(
        jnp.where((ports.sub == me * TILES + ports.lane) & (ports.lane < TILES), to_column(own, ports.eye), 0),
        axis=0,
        keepdims=True,
    )
    store(R_ROW, mine >> 5)
    found = []
    for band in (own, below, above):
        at = to_column(band, ports.eye)
        for step in (-1, 1):
            there = (at == turn(mine ^ COLS, step)) & (ports.sub < PORTS)
            found.append(jnp.sum(jnp.where(there, ports.sub, 0), axis=0, keepdims=True))
    upper = (mine >> 5) == 1
    for n in range(2):
        store(R_CORNER + n, jnp.where(upper, found[n], found[2 + n] + PORTS))
        store(R_CORNER + 2 + n, jnp.where(upper, found[4 + n] + 2 * PORTS, found[n]))


def gathered_ids(ids):
    return jnp.sum(ids, axis=0)[0:1]


def owner_routes_kernel(me_ref, ids_ref, out_ref):
    def store(place, row):
        out_ref[pl.ds(place, 1)] = row

    owner_tables(me_ref[0], gathered_ids(ids_ref[...]), store)


def make_routes(kernel, rows, me, *ids):
    vmem = pl.BlockSpec(memory_space=pltpu.VMEM)
    return pl.pallas_call(
        kernel,
        out_shape=jax.ShapeDtypeStruct((rows, DEPTH), jnp.int32),
        in_specs=[pl.BlockSpec(memory_space=pltpu.SMEM)] + [vmem] * len(ids),
        out_specs=vmem,
        compiler_params=pltpu.CompilerParams(vmem_limit_bytes=8 << 20),
        name=kernel.__name__,
    )(me, *ids)


def ring(axis, step):
    gy = lax.axis_index("gy")
    row, col = gy // 4, lax.rem(gy, 4)
    if axis == 0:
        place = lax.rem(col + step, 4)
        return col, place, {"gx": lax.axis_index("gx"), "gy": row * 4 + place}
    place = lax.rem(row + step, 4)
    return row, place, {"gx": lax.axis_index("gx"), "gy": place * 4 + col}


RING_AXES = ((0, 1, 1, 0), (1, 0, 0, 1))
RING_KINDS = ((K_FIRST, K_X2, K_X3, K_X4), (K_FIRST, K_Y2, K_Y3, K_Y4))


class Lane:
    def __init__(self, order, perms, table_ref, first, scratch, final=None):
        self.order, self.perms, self.table_ref = order, perms, table_ref
        self.first, self.final = first, final
        self.stages = [scratch[4 * n : 4 * n + 4] for n in range(4)]
        self.waiting, self.sent = [], []

    def arrived(self):
        for copy in self.waiting:
            copy.wait_recv()
        self.waiting = []

    def target(self, stage, here):
        if stage == 3 and self.final is not None:
            return self.final(here)
        return self.stages[stage][1].at[here]

    def advance(self, stage):
        self.arrived()
        send, _, send_sem, recv_sem = self.stages[stage]
        for step in (2, 1, 3, 0):
            here, place, target = ring(RING_AXES[self.order][stage], step)
            landing = self.target(stage, here)
            for n, perm in enumerate(self.perms):
                slot = self.table_ref[perm * 8 + RING_KINDS[self.order][stage], place]
                if stage:
                    value = self.stages[stage - 1][1][slot, n]
                else:
                    value = self.first(n, slot)
                if step:
                    send[step - 1, n] = value
                else:
                    landing[n] = value
            if step:
                copy = pltpu.make_async_remote_copy(
                    src_ref=send.at[step - 1],
                    dst_ref=landing,
                    send_sem=send_sem.at[step - 1],
                    recv_sem=recv_sem.at[step - 1],
                    device_id=target,
                    device_id_type=MESH,
                )
                copy.start()
                self.waiting.append(copy)
                self.sent.append(copy)

    def close(self):
        for copy in self.sent:
            copy.wait_send()


def lane_scratch(items, shape):
    scratch = []
    for stage in range(4):
        scratch += [
            pltpu.VMEM((3, items) + shape, jnp.float32),
            pltpu.VMEM((4, items) + shape, jnp.float32),
            pltpu.SemaphoreType.DMA((3,)),
            pltpu.SemaphoreType.DMA((3,)),
        ]
    return scratch


RING_PEERS = tuple((axis, step) for axis in range(2) for step in (1, 2, 3))
LANES = 4


def source_kernel(
    permit_ref,
    table_ref,
    charge_hbm,
    mask_hbm,
    ids_ref,
    phase_ref,
    pot_ref,
    pack_ref,
    others,
    rims_ref,
    charge_ref,
    mask_ref,
    fetch_sem,
    rims,
    ext_ref,
    coef_ref,
    scale_ref,
    resid,
    upd_a,
    upd_b,
    total,
    phase_ext,
    permit,
    send_sem,
    recv_sem,
    phase_send,
    phase_recv,
    ids_send,
    ids_recv,
    own_sem,
    *scratch,
):
    bands = [shifted_id(1, 0), shifted_id(-1, 0)]
    fetches = [
        pltpu.make_async_copy(charge_hbm, charge_ref, fetch_sem.at[0]),
        pltpu.make_async_copy(mask_hbm, mask_ref, fetch_sem.at[1]),
        pltpu.make_async_copy(
            phase_ref, phase_ext.at[pl.ds(5, BLOCK), pl.ds(SIDE, BLOCK)], own_sem
        ),
    ]
    for copy in fetches:
        copy.start()
    greet([ring(*peer)[2] for peer in RING_PEERS] + [shifted_id(dx, dy) for dx, dy in AROUND])
    for copy in fetches:
        copy.wait()
    part = EDGE // LANES
    lanes = []
    for n in range(LANES):

        def first(_, slot, n=n):
            flags = mask_ref[slot, 1 + n * part : 1 + (n + 1) * part, 1 : EDGE + 1]
            return charge_ref[slot, n * part : (n + 1) * part] * flags.astype(jnp.float32)

        lanes.append(
            Lane(n % 2, (TO_OWNER,), table_ref, first, scratch[16 * n : 16 * n + 16])
        )
    passed = []
    phases = halo_copies(phase_ref, phase_ext, 5, 5, phase_send, phase_recv)

    def weights(begin, end):
        weigh_rows(begin, end, permit, coef_ref, scale_ref)

    for stage in range(4):
        for lane in lanes:
            lane.advance(stage)
        if stage == 0:
            for copy in phases:
                copy.start()
            for n, target in enumerate(bands):
                copy = pltpu.make_async_remote_copy(
                    src_ref=ids_ref,
                    dst_ref=others.at[n],
                    send_sem=ids_send.at[n],
                    recv_sem=ids_recv.at[n],
                    device_id=target,
                    device_id_type=MESH,
                )
                copy.start()
                passed.append(copy)
        elif stage == 1:
            for copy in phases:
                copy.wait_recv()
            look_up_rows(permit_ref, phase_ext, permit)
            weights(0, 8)
        elif stage == 2:
            weights(8, 18)
        else:
            weights(18, 30)
    for n, lane in enumerate(lanes):
        lane.arrived()
        final = lane.stages[3][1]
        for t in range(TILES):
            i0, j0 = 4 + (t // 2) * EDGE + n * part, SIDE + (t % 2) * EDGE
            ext_ref[i0 : i0 + part, j0 : j0 + EDGE] = final[
                table_ref[TO_OWNER * 8 + K_LAST, t], 0
            ]
    block = ext_ref.at[pl.ds(4, BLOCK), pl.ds(SIDE, BLOCK)]
    copies = halo_copies(block, ext_ref, 4, 4, send_sem, recv_sem)
    for copy in copies:
        copy.start()
    weights(30, TALL)
    for copy in copies + passed:
        copy.wait()
    for copy in phases:
        copy.wait_send()
    pack_rims(rims, 0, ext_ref)
    returning = []
    for n in range(2):

        def first(_, slot, n=n):
            return rims[slot, 2 * n : 2 * n + 2]

        def final(here, n=n):
            return rims_ref.at[here, :, pl.ds(2 * n, 2)]

        refs = scratch[16 * (LANES + n) : 16 * (LANES + n) + 16]
        returning.append(Lane(n, (TO_HOLDER,), table_ref, first, refs, final))

    def between(stage):
        for lane in returning:
            lane.advance(stage)

    between(0)
    sweep_rows(
        coef_ref, scale_ref, ext_ref, pot_ref, pack_ref, resid, upd_a, upd_b, total, between
    )
    for lane in returning:
        lane.arrived()
    for lane in lanes + returning:
        lane.close()


def find_potential(permittivity, routes, charge, fluid_mask, ids, phase):
    vmem = pl.BlockSpec(memory_space=pltpu.VMEM)
    smem = pl.BlockSpec(memory_space=pltpu.SMEM)
    anywhere = pl.BlockSpec(memory_space=pltpu.HBM)
    dma = pltpu.SemaphoreType.DMA
    f32 = jnp.float32
    return pl.pallas_call(
        source_kernel,
        out_shape=(
            jax.ShapeDtypeStruct((BLOCK, BLOCK, DEPTH), f32),
            jax.ShapeDtypeStruct((TILES, PACK, EDGE, DEPTH), f32),
            jax.ShapeDtypeStruct((2, GROUPS, 8, DEPTH), jnp.int32),
            jax.ShapeDtypeStruct((TILES, 1, 4, EDGE, DEPTH), f32),
            jax.ShapeDtypeStruct((TILES, EDGE, EDGE, DEPTH), f32),
            jax.ShapeDtypeStruct((TILES, EDGE + 2, EDGE + 2, DEPTH), jnp.int32),
        ),
        in_specs=[smem] * 2 + [anywhere, anywhere, vmem, anywhere],
        out_specs=(vmem,) * 6,
        scratch_shapes=[
            dma((2,)),
            pltpu.VMEM((TILES, 4, EDGE, DEPTH), f32),
            pltpu.VMEM((TALL, WIDE, DEPTH), f32),
            pltpu.VMEM((6, TALL, WIDE, DEPTH), f32),
            pltpu.VMEM((TALL, WIDE, DEPTH), f32),
            pltpu.VMEM((TALL, WIDE, DEPTH), f32),
            pltpu.VMEM((TALL, ROOM, DEPTH), f32),
            pltpu.VMEM((TALL, ROOM, DEPTH), f32),
            pltpu.VMEM((TALL, WIDE, DEPTH), f32),
            pltpu.VMEM((TALL + 2, WIDE, DEPTH), jnp.int32),
            pltpu.VMEM((TALL + 2, WIDE, DEPTH), f32),
            dma((8,)),
            dma((8,)),
            dma((8,)),
            dma((8,)),
            dma((2,)),
            dma((2,)),
            dma,
        ]
        + lane_scratch(1, (EDGE // LANES, EDGE, DEPTH)) * LANES
        + lane_scratch(1, (2, EDGE, DEPTH)) * 2,
        compiler_params=pltpu.CompilerParams(
            collective_id=1, has_side_effects=True, vmem_limit_bytes=28 << 20
        ),
        name="source",
    )(permittivity, routes, charge, fluid_mask, ids, phase)


def back_kernel(
    me_ref,
    table_ref,
    items_ref,
    ids_ref,
    others_ref,
    pops_hbm,
    out_ref,
    face_ref,
    pops_ref,
    pops_sem,
    *scratch,
):
    fetches = [
        pltpu.make_async_copy(pops_hbm.at[:, t], pops_ref.at[:, t], pops_sem.at[t])
        for t in range(TILES)
    ]
    for copy in fetches:
        copy.start()

    def store(place, row):
        face_ref[pl.ds(place, 1)] = row

    greet([ring(*peer)[2] for peer in RING_PEERS])
    part = PACK // LANES
    lanes = []
    for n in range(LANES):
        rows = slice(n * part, (n + 1) * part)

        def first(_, slot, rows=rows):
            return items_ref[slot, rows]

        def final(here, n=n):
            return out_ref.at[here, :, pl.ds(n * part, part)]

        lanes.append(
            Lane(n % 2, (TO_HOLDER,), table_ref, first, scratch[16 * n : 16 * n + 16], final)
        )
    tables = None
    for stage in range(4):
        for lane in lanes:
            lane.advance(stage)
        if stage == 0:
            tables = face_tables(
                me_ref[0],
                gathered_ids(ids_ref[...]),
                gathered_ids(others_ref[0]),
                gathered_ids(others_ref[1]),
                store,
            )
        next(tables, None)
    for lane in lanes:
        lane.arrived()
    for lane in lanes:
        lane.close()
    for copy in fetches:
        copy.wait()


def send_back(me, routes, packed, ids, others, populations):
    vmem = pl.BlockSpec(memory_space=pltpu.VMEM)
    smem = pl.BlockSpec(memory_space=pltpu.SMEM)
    return pl.pallas_call(
        back_kernel,
        out_shape=(
            jax.ShapeDtypeStruct((TILES, 1, PACK, EDGE, DEPTH), jnp.float32),
            jax.ShapeDtypeStruct((48, DEPTH), jnp.int32),
            jax.ShapeDtypeStruct((19, TILES, EDGE, EDGE, DEPTH), jnp.float32),
        ),
        in_specs=[smem, smem, vmem, vmem, vmem, pl.BlockSpec(memory_space=pltpu.HBM)],
        out_specs=(vmem, vmem, vmem),
        scratch_shapes=[pltpu.SemaphoreType.DMA((TILES,))]
        + lane_scratch(1, (PACK // LANES, EDGE, DEPTH)) * LANES,
        compiler_params=pltpu.CompilerParams(
            collective_id=2, has_side_effects=True, vmem_limit_bytes=40 << 20
        ),
        name="back",
    )(me, routes, packed, ids, others, populations)


def collide_rows(pops, charge, field):
    force = [charge * component for component in field]
    sums = {}
    diffs = {}
    for a, b in PAIRS:
        sums[a] = pops[a] + pops[b]
        diffs[a] = pops[a] - pops[b]
    density = pops[0]
    for a, _ in PAIRS:
        density = density + sums[a]
    momentum = [
        diffs[1] + diffs[7] + diffs[9] + diffs[11] + diffs[13],
        diffs[3] + diffs[7] - diffs[9] + diffs[15] + diffs[17],
        diffs[5] + diffs[11] - diffs[13] + diffs[15] - diffs[17],
    ]
    inverse = 1.0 / density
    velocity = [(momentum[d] + 0.5 * force[d]) * inverse for d in range(3)]
    scale = 1.0 - 0.5 / relax_time
    rate = 1.0 / relax_time
    speed = velocity[0] * velocity[0] + velocity[1] * velocity[1] + velocity[2] * velocity[2]
    work = velocity[0] * force[0] + velocity[1] * force[1] + velocity[2] * force[2]
    weighted = rate * density
    base = weighted - (1.5 * weighted) * speed - (3.0 * scale) * work
    odd = [3.0 * weighted * velocity[d] + (3.0 * scale) * force[d] for d in range(3)]
    inner = [4.5 * weighted * velocity[d] + (9.0 * scale) * force[d] for d in range(3)]
    keep = 1.0 - rate
    result = [None] * 19
    result[0] = keep * pops[0] + WEIGHTS[0] * base
    for a, b in PAIRS:
        step = LATTICE[a]
        axes = [d for d in range(3) if step[d] != 0]
        if len(axes) == 1:
            (d,) = axes
            cu, co, ci = velocity[d], odd[d], inner[d]
            weight = WEIGHTS[1]
        else:
            d, e = axes
            weight = WEIGHTS[2]
            if step[d] * step[e] > 0:
                cu, co, ci = velocity[d] + velocity[e], odd[d] + odd[e], inner[d] + inner[e]
            else:
                cu, co, ci = velocity[d] - velocity[e], odd[d] - odd[e], inner[d] - inner[e]
        even = weight * (base + cu * ci)
        lean = weight * co
        result[a] = keep * pops[a] + (even + lean)
        result[b] = keep * pops[b] + (even - lean)
    return result, velocity


PITCH = 32


def place_potential(grown, pot_ref, slot):
    def place(i, carry):
        start = (i + 1) * PITCH
        grown[pl.ds(start + 8, EDGE)] = pot_ref[slot, 0, i]
        grown[pl.ds(start + 7, 1)] = pot_ref[slot, 0, EDGE + 2, pl.ds(i, 1)]
        grown[pl.ds(start + 8 + EDGE, 1)] = pot_ref[slot, 0, EDGE + 3, pl.ds(i, 1)]
        return carry

    lax.fori_loop(0, EDGE, place, 0, unroll=4)
    grown[pl.ds(8, EDGE)] = pot_ref[slot, 0, EDGE]
    grown[pl.ds((EDGE + 1) * PITCH + 8, EDGE)] = pot_ref[slot, 0, EDGE + 1]


def field_at(here, x_low, x_high, y_low, y_high):
    return [
        0.5 * (x_low - x_high),
        0.5 * (y_low - y_high),
        0.5 * (pltpu.roll(here, 1, 1) - pltpu.roll(here, DEPTH - 1, 1)),
    ]


def row_field(grown, i):
    start = i * PITCH + 8
    return field_at(
        *[grown[pl.ds(start + step, EDGE)] for step in (PITCH, 0, 2 * PITCH, PITCH - 1, PITCH + 1)]
    )


def column_field(grown, j):
    return field_at(
        *[
            grown[pl.ds(8 + j + step, EDGE, stride=PITCH)]
            for step in (PITCH, 0, 2 * PITCH, PITCH - 1, PITCH + 1)
        ]
    )


def edges_kernel(
    table_ref, routes_ref, pops_ref, charge_ref, mask_ref, pot_ref, block_ref, face_ref, corner_ref, block_out, grown
):
    tile = pl.program_id(0)
    block_out[...] = block_ref[...]
    place_potential(grown, pot_ref, 0)

    def finish(face, axis, sign, pops, charge, flags, field):
        relaxed, velocity = collide_rows(pops, charge, field)
        fluid = flags == 1

        def value(q):
            return jnp.where(fluid, relaxed[q], pops[q])

        for k, q in enumerate(crossing(axis, sign)):
            face_ref[0, face, k] = value(q)
        face_ref[0, face, 5] = velocity[axis]
        return value

    for face, sign, j in ((UP_Y, 1, EDGE - 1), (DOWN_Y, -1, 0)):
        finish(
            face,
            1,
            sign,
            [pops_ref[q, 0, pl.ds(j, EDGE, stride=EDGE)] for q in range(19)],
            charge_ref[0, pl.ds(j, EDGE, stride=EDGE)],
            mask_ref[0, pl.ds(1, EDGE), 1 + j, :],
            column_field(grown, j),
        )
    for face, sign, i, corners in (
        (BELOW_X, 1, EDGE - 1, ((0, 7, EDGE - 1), (1, 9, 0))),
        (ABOVE_X, -1, 0, ((2, 10, EDGE - 1), (3, 8, 0))),
    ):
        value = finish(
            face,
            0,
            sign,
            [pops_ref[q, 0, pl.ds(i * EDGE, EDGE)] for q in range(19)],
            charge_ref[0, pl.ds(i * EDGE, EDGE)],
            mask_ref[0, i + 1, pl.ds(1, EDGE), :],
            row_field(grown, i),
        )
        for n, q, j in corners:
            corner_ref[tile // 2, pl.ds(lax.rem(tile, 2) * 4 + n, 1)] = value(q)[j : j + 1]
    same = lax.rem(table_ref[R_ROW, tile], 2)
    for k in range(6):
        face_ref[0, SAME_X, k] = jnp.where(
            same == 0, face_ref[0, BELOW_X, k], face_ref[0, ABOVE_X, k]
        )


def edges(table, routes, populations, charge, fluid_mask, returned, potential):
    f32 = jnp.float32
    return pl.pallas_call(
        edges_kernel,
        out_shape=(
            jax.ShapeDtypeStruct((TILES, FACES, 6, EDGE, DEPTH), f32),
            jax.ShapeDtypeStruct((2, 8, DEPTH), f32),
            jax.ShapeDtypeStruct((BLOCK, BLOCK, DEPTH), f32),
        ),
        grid_spec=pltpu.PrefetchScalarGridSpec(
            num_scalar_prefetch=2,
            grid=(TILES,),
            in_specs=[
                pl.BlockSpec((19, 1, EDGE * EDGE, DEPTH), lambda s, tab, rts: (0, s, 0, 0)),
                pl.BlockSpec((1, EDGE * EDGE, DEPTH), lambda s, tab, rts: (s, 0, 0)),
                pl.BlockSpec((1, EDGE + 2, EDGE + 2, DEPTH), lambda s, tab, rts: (s, 0, 0, 0)),
                pl.BlockSpec(
                    (1, 1, PACK, EDGE, DEPTH),
                    lambda s, tab, rts: (rts[TO_HOLDER * 8 + K_LAST, s], 0, 0, 0, 0),
                ),
                pl.BlockSpec((BLOCK // TILES, BLOCK, DEPTH), lambda s, tab, rts: (s, 0, 0)),
            ],
            out_specs=[
                pl.BlockSpec((1, FACES, 6, EDGE, DEPTH), lambda s, tab, rts: (s, 0, 0, 0, 0)),
                pl.BlockSpec((2, 8, DEPTH), lambda s, tab, rts: (0, 0, 0)),
                pl.BlockSpec((BLOCK // TILES, BLOCK, DEPTH), lambda s, tab, rts: (s, 0, 0)),
            ],
            scratch_shapes=[pltpu.VMEM(((EDGE + 2) * PITCH, DEPTH), f32)],
        ),
        compiler_params=pltpu.CompilerParams(vmem_limit_bytes=16 << 20),
        name="edges",
    )(
        table,
        routes,
        populations.reshape(19, TILES, EDGE * EDGE, DEPTH),
        charge.reshape(TILES, EDGE * EDGE, DEPTH),
        fluid_mask,
        returned,
        potential,
    )


FACE_LANES = (
    (0, (UP_Y, DOWN_Y, SAME_X)),
    (1, (UP_Y, DOWN_Y, SAME_X)),
    (0, (BELOW_X, ABOVE_X)),
    (1, (BELOW_X, ABOVE_X)),
)


def faces_kernel(
    table_ref,
    routes_ref,
    faces_ref,
    corners_ref,
    charge_ref,
    mask_ref,
    pot_ref,
    pops_ref,
    out_ref,
    all_ref,
    cells_ref,
    vel_ref,
    shifted,
    grown,
    pops_sem,
    corner_send,
    corner_recv,
    shift_send,
    shift_recv,
    own_sem,
    *scratch,
):
    me = lax.axis_index("gy")
    peers = [shifted_id(0, k) for k in range(1, GROUPS)]
    bands = [shifted_id(1, 0), shifted_id(-1, 0)]
    fetches = [
        pltpu.make_async_copy(pops_ref.at[:, t], cells_ref.at[:, t], pops_sem.at[t])
        for t in range(TILES)
    ]
    for copy in fetches:
        copy.start()

    def collide(t, begin):
        def rows(i, carry):
            pops = [cells_ref[q, t, i] for q in range(19)]
            relaxed, velocity = collide_rows(pops, charge_ref[t, i], row_field(grown, i))
            fluid = mask_ref[t, i + 1, pl.ds(1, EDGE), :] == 1
            for q in range(19):
                cells_ref[q, t, i] = jnp.where(fluid, relaxed[q], pops[q])
            for d in range(3):
                vel_ref[d, t, i] = velocity[d]
            return carry

        lax.fori_loop(begin, begin + EDGE // len(FACE_LANES), rows, 0)

    greet(peers + bands)
    shifts = []
    for n, target in enumerate(bands):
        copy = pltpu.make_async_remote_copy(
            src_ref=faces_ref.at[:, 3 + n],
            dst_ref=shifted.at[n],
            send_sem=shift_send.at[n],
            recv_sem=shift_recv.at[n],
            device_id=target,
            device_id_type=MESH,
        )
        copy.start()
        shifts.append(copy)
    lanes = []
    for n, (order, perms) in enumerate(FACE_LANES):
        rows = slice(order * 3, order * 3 + 3)

        def first(k, slot, perms=perms, rows=rows):
            if perms[k] < BELOW_X:
                return faces_ref[slot, perms[k], rows]
            return shifted[perms[k] - BELOW_X, slot, rows]

        def final(here, perms=perms, order=order):
            return out_ref.at[here, pl.ds(perms[0], len(perms)), pl.ds(order * 3, 3)]

        lanes.append(Lane(order, perms, table_ref, first, scratch[16 * n : 16 * n + 16], final))
    spread_out, forward = [], []
    own = pltpu.make_async_copy(corners_ref, all_ref.at[0, me], own_sem)
    for stage in range(4):
        for n, lane in enumerate(lanes):
            if stage == 0 and n == 2:
                for k, target in enumerate(peers):
                    copy = pltpu.make_async_remote_copy(
                        src_ref=corners_ref,
                        dst_ref=all_ref.at[0, me],
                        send_sem=corner_send.at[k],
                        recv_sem=corner_recv.at[k],
                        device_id=target,
                        device_id_type=MESH,
                    )
                    copy.start()
                    spread_out.append(copy)
                own.start()
                for copy in shifts:
                    copy.wait_recv()
            lane.advance(stage)
            if n == 0:
                fetches[stage].wait()
                place_potential(grown, pot_ref, routes_ref[TO_HOLDER * 8 + K_LAST, stage])
            collide(stage, n * (EDGE // len(FACE_LANES)))
        if stage == 1:
            own.wait()
            for copy in spread_out:
                copy.wait_recv()
            for n, target in enumerate(bands):
                copy = pltpu.make_async_remote_copy(
                    src_ref=all_ref.at[0],
                    dst_ref=all_ref.at[1 + n],
                    send_sem=corner_send.at[GROUPS - 1 + n],
                    recv_sem=corner_recv.at[GROUPS - 1 + n],
                    device_id=target,
                    device_id_type=MESH,
                )
                copy.start()
                forward.append(copy)
    for lane in lanes:
        lane.arrived()
    for copy in forward:
        copy.wait_recv()
    for copy in shifts + spread_out + forward:
        copy.wait_send()
    for lane in lanes:
        lane.close()


def collide_and_send(table, routes, faces, corners, charge, fluid_mask, returned, populations):
    vmem = pl.BlockSpec(memory_space=pltpu.VMEM)
    smem = pl.BlockSpec(memory_space=pltpu.SMEM)
    anywhere = pl.BlockSpec(memory_space=pltpu.HBM)
    f32 = jnp.float32
    dma = pltpu.SemaphoreType.DMA
    scratch = []
    for _, perms in FACE_LANES:
        scratch += lane_scratch(len(perms), (3, EDGE, DEPTH))
    return pl.pallas_call(
        faces_kernel,
        out_shape=(
            jax.ShapeDtypeStruct((TILES, FACES, 6, EDGE, DEPTH), f32),
            jax.ShapeDtypeStruct((3, GROUPS, 2, 8, DEPTH), f32),
            jax.ShapeDtypeStruct((19, TILES, EDGE, EDGE, DEPTH), f32),
            jax.ShapeDtypeStruct((3, TILES, EDGE, EDGE, DEPTH), f32),
        ),
        in_specs=[smem, smem] + [vmem] * 5 + [pl.BlockSpec(memory_space=pl.ANY)],
        out_specs=(vmem,) * 4,
        scratch_shapes=[
            pltpu.VMEM((2, TILES, 6, EDGE, DEPTH), f32),
            pltpu.VMEM(((EDGE + 2) * PITCH, DEPTH), f32),
            dma((TILES,)),
            dma((GROUPS + 1,)),
            dma((GROUPS + 1,)),
            dma((2,)),
            dma((2,)),
            dma,
        ]
        + scratch,
        compiler_params=pltpu.CompilerParams(
            collective_id=3, has_side_effects=True, vmem_limit_bytes=20 << 20
        ),
        name="faces",
    )(table, routes, faces, corners, charge, fluid_mask, returned, populations)


CHARGE, SPEED = 19, 20
SOLID = 3.0e38
FIRST = 8 + EDGE
STRIP = 8 + (EDGE + 2) * EDGE + 8


def stream_kernel(
    table_ref,
    routes_ref,
    relaxed_ref,
    vel_ref,
    charge_ref,
    mask_ref,
    rim_ref,
    *rest,
):
    faces, (corner_ref, pops_out, charge_out, grown, side, sems) = rest[:FACES], rest[FACES:]
    tile = pl.program_id(0)
    here = lax.rem(tile, 2)

    def fetch(t, slot):
        rows = pl.ds(FIRST, EDGE * EDGE)
        return [
            pltpu.make_async_copy(
                relaxed_ref.at[:, t], grown.at[slot, pl.ds(0, 19), rows], sems.at[slot, 0]
            ),
            pltpu.make_async_copy(
                charge_ref.at[t], grown.at[slot, CHARGE, rows], sems.at[slot, 1]
            ),
            pltpu.make_async_copy(
                vel_ref.at[:, t], grown.at[slot, pl.ds(SPEED, 3), rows], sems.at[slot, 2]
            ),
        ]

    @pl.when(tile == 0)
    def _():
        for copy in fetch(0, 0):
            copy.start()

    @pl.when(tile + 1 < TILES)
    def _():
        for copy in fetch(tile + 1, 1 - here):
            copy.start()

    for copy in fetch(tile, here):
        copy.wait()

    cells = grown.at[here]
    before, after = pl.ds(8, EDGE), pl.ds(FIRST + EDGE * EDGE, EDGE)

    def x_rim(face, sign, rows):
        for k, q in enumerate(crossing(0, sign) + [SPEED]):
            cells[q, rows] = faces[face][0, 0, k]

    row = table_ref[R_ROW, tile]

    @pl.when(row == 0)
    def _():
        x_rim(BELOW_X, 1, before)
        x_rim(SAME_X, -1, after)

    @pl.when(row == 1)
    def _():
        x_rim(SAME_X, 1, before)
        x_rim(ABOVE_X, -1, after)

    cells[CHARGE, before] = rim_ref[0, 0, 0]
    cells[CHARGE, after] = rim_ref[0, 0, 1]
    for face, sign, end in ((UP_Y, 1, 0), (DOWN_Y, -1, 1)):
        for k, q in enumerate(crossing(1, sign)):
            side[end, k, pl.ds(1, EDGE)] = faces[face][0, 0, k]
        side[end, 5, pl.ds(1, EDGE)] = faces[face][0, 0, 5]
        side[end, 6, pl.ds(1, EDGE)] = rim_ref[0, 0, 2 + end]
    for n, (q, sign, layer) in enumerate(((7, 1, 0), (9, -1, 0), (10, 1, 17), (8, -1, 17))):
        found = table_ref[R_CORNER + n, tile]
        inside = lax.rem(found, TILES)
        side[n % 2, crossing(1, sign).index(q), pl.ds(layer, 1)] = corner_ref[
            found // TILES, inside // 2, pl.ds(lax.rem(inside, 2) * 4 + n, 1)
        ]
    spot = lax.broadcasted_iota(jnp.int32, (EDGE, DEPTH), 0)
    ends = {-1: spot == 0, 1: spot == EDGE - 1}

    def rows(i, carry):
        def cell(q, di=0, dj=0):
            value = cells[q, pl.ds(i * EDGE + (FIRST + di * EDGE + dj), EDGE)]
            if dj == 0:
                return value
            if q < 19:
                k = crossing(1, -dj).index(q)
            else:
                k = 6 if q == CHARGE else 5
            return jnp.where(ends[dj], side[(dj + 1) // 2, k, pl.ds(i + 1 + di, 1)], value)

        def flag(di=0, dj=0):
            return mask_ref[0, i + 1 + di, pl.ds(1 + dj, EDGE), :]

        own = flag()
        own_fluid = own == 1
        for q in range(19):
            step_x, step_y, step_z = LATTICE[q]
            value = cell(q)
            if q == 0:
                pops_out[q, 0, i] = value
                continue
            moved = cell(q, -step_x, -step_y)
            from_fluid = flag(-step_x, -step_y) == 1
            if step_z != 0:
                moved = pltpu.roll(jnp.where(from_fluid, moved, SOLID), step_z % DEPTH, 1)
                from_fluid = moved < SOLID
            read = jnp.where(from_fluid, moved, cell(opposite(q)))
            pops_out[q, 0, i] = jnp.where(own_fluid, read, value)

        charge = cell(CHARGE)
        weight = own.astype(jnp.float32)

        def flux(speed_a, speed_b, value_a, value_b, flags):
            speed = 0.5 * (speed_a + speed_b)
            return speed * jnp.where(speed > 0, value_a, value_b) * flags

        change = None
        for d, (di, dj) in enumerate(((1, 0), (0, 1))):
            speed = cell(SPEED + d)
            for sign in (1, -1):
                other = cell(CHARGE, sign * di, sign * dj)
                other_speed = cell(SPEED + d, sign * di, sign * dj)
                flags = weight * flag(sign * di, sign * dj).astype(jnp.float32)
                if sign > 0:
                    part = flux(speed, other_speed, charge, other, flags)
                    change = part if change is None else change + part
                else:
                    change = change - flux(other_speed, speed, other, charge, flags)
        speed = cell(SPEED + 2)
        next_charge = pltpu.roll(jnp.where(own_fluid, charge, SOLID), DEPTH - 1, 1)
        middle = 0.5 * (speed + pltpu.roll(speed, DEPTH - 1, 1))
        over = middle * jnp.where(middle > 0, charge, next_charge)
        over = jnp.where(own_fluid & (next_charge < SOLID), over, 0.0)
        change = change + over - pltpu.roll(over, 1, 1)
        charge_out[0, i] = jnp.where(own_fluid, charge - change, charge)
        return carry

    lax.fori_loop(0, EDGE, rows, 0, unroll=2)


def stream(table, routes, relaxed, velocity, charge, fluid_mask, returned, faces, corners):
    f32 = jnp.float32
    face_specs = [
        pl.BlockSpec(
            (1, 1, 6, EDGE, DEPTH),
            lambda s, tab, rts, face=face: (tab[face * 8 + K_LAST, s], face, 0, 0, 0),
        )
        for face in range(FACES)
    ]
    anywhere = pl.BlockSpec(memory_space=pl.ANY)
    return pl.pallas_call(
        stream_kernel,
        out_shape=(
            jax.ShapeDtypeStruct((19, TILES, EDGE, EDGE, DEPTH), f32),
            jax.ShapeDtypeStruct((TILES, EDGE, EDGE, DEPTH), f32),
        ),
        grid_spec=pltpu.PrefetchScalarGridSpec(
            num_scalar_prefetch=2,
            grid=(TILES,),
            in_specs=[
                anywhere,
                anywhere,
                anywhere,
                pl.BlockSpec((1, EDGE + 2, EDGE + 2, DEPTH), lambda s, tab, rts: (s, 0, 0, 0)),
                pl.BlockSpec(
                    (1, 1, 4, EDGE, DEPTH),
                    lambda s, tab, rts: (rts[TO_HOLDER * 8 + K_LAST, s], 0, 0, 0, 0),
                ),
            ]
            + face_specs
            + [pl.BlockSpec((3 * GROUPS, 2, 8, DEPTH), lambda s, tab, rts: (0, 0, 0, 0))],
            out_specs=[
                pl.BlockSpec((19, 1, EDGE, EDGE, DEPTH), lambda s, tab, rts: (0, s, 0, 0, 0)),
                pl.BlockSpec((1, EDGE, EDGE, DEPTH), lambda s, tab, rts: (s, 0, 0, 0)),
            ],
            scratch_shapes=[
                pltpu.VMEM((2, 23, STRIP, DEPTH), f32),
                pltpu.VMEM((2, 7, 24, DEPTH), f32),
                pltpu.SemaphoreType.DMA((2, 3)),
            ],
        ),
        compiler_params=pltpu.CompilerParams(vmem_limit_bytes=24 << 20),
        name="stream",
    )(
        table,
        routes,
        relaxed.reshape(19, TILES, EDGE * EDGE, DEPTH),
        velocity.reshape(3, TILES, EDGE * EDGE, DEPTH),
        charge.reshape(TILES, EDGE * EDGE, DEPTH),
        fluid_mask,
        returned,
        *([faces] * FACES),
        corners.reshape(3 * GROUPS, 2, 8, DEPTH),
    )


def per_device(populations, charge, fluid_mask, tile_ids, phase_label, permittivity):
    me = lax.axis_index("gy").astype(jnp.int32).reshape(1)
    place = jnp.arange(8 * DEPTH, dtype=jnp.int32).reshape(8, DEPTH)
    ids_row = jnp.where(place // TILES == me, jnp.tile(tile_ids, 2 * DEPTH).reshape(8, DEPTH), 0)
    ids = exchange_start(ids_row)
    routes = make_routes(owner_routes_kernel, 16, me, ids)
    potential, packed, others, charge_rims, charge, fluid_mask = find_potential(
        permittivity, routes, charge, fluid_mask, ids, phase_label
    )
    returned, table, populations = send_back(me, routes, packed, ids, others, populations)
    faces, corners, potential = edges(
        table, routes, populations, charge, fluid_mask, returned, potential
    )
    rims, all_corners, relaxed, velocity = collide_and_send(
        table, routes, faces, corners, charge, fluid_mask, returned, populations
    )
    populations_next, charge_next = stream(
        table, routes, relaxed, velocity, charge, fluid_mask, charge_rims, rims, all_corners
    )
    return (populations_next, charge_next, potential)


def solution(mesh):
    placed = (
        P(None, ("gx", "gy"), None, None, None),
        P(("gx", "gy"), None, None, None),
        P(("gx", "gy"), None, None, None),
        P(("gx", "gy")),
        P("gx", "gy", None),
        P(),
    )
    return jax.shard_map(
        per_device,
        mesh=mesh,
        in_specs=placed,
        out_specs=(
            P(None, ("gx", "gy"), None, None, None),
            P(("gx", "gy"), None, None, None),
            P("gx", "gy", None),
        ),
        check_vma=False,
    )
```
